256 devices in a mesh: paths: 256 (over x, y, z, core).
Axes of the slice: x: 4, y: 4, z: 8, core: 2. Of those that a mesh axis runs over, the one named last changes fastest.
Arguments:
- params: float32 [2048, 4], replicated, may hold values from -0.9 to 2, as said below
- increments: bfloat16 [2, 64, 32768], P(None, None, 'paths'), may hold values from -5 to 5
- w_in: bfloat16 [6, 1024], replicated, may hold values from -2.5 to 2.5
- b_in: float32 [1024], replicated, may hold values from -3 to 3
- w_mid: bfloat16 [1024, 1024], replicated, may hold values from -0.1875 to 0.1875
- b_mid: float32 [1024], replicated, may hold values from -3 to 3
- w_out: bfloat16 [1024], replicated, may hold values from -0.1875 to 0.1875
- b_out: float32 [1], replicated, may hold values from -3 to 3
Outputs:
- prices: float32 [2048, 88], P('paths')
- direction_w_in: float32 [6, 1024], replicated
- direction_b_in: float32 [1024], replicated
- direction_w_mid: float32 [1024, 1024], replicated
- direction_b_mid: float32 [1024], replicated
- direction_w_out: float32 [1024], replicated
- direction_b_out: float32 [1], replicated
The draws below stay inside these ranges and needn't reach their ends.
Inputs may be any that keep to these rules, and one draw needn't show every extreme that they name: `params`: each row holds a Hurst index in [0.05, 0.45], a vol-of-vol in [0.8, 2.0], a correlation in [-0.9, -0.3] and an initial forward variance in [0.01, 0.15].
All inputs are finite; a program needn't handle non-finite values.
Results may differ from the reference program's by a relative error of at most 0.0003.
The reference program's roundings to bfloat16 on the way count: a program that leaves them out, or rounds other values in their place, can miss the bound.
Values sent between devices are 32-bit elements; how exact they have to be, the bound alone decides.
A program may use at most 64 MiB of HBM per device.

```python
import jax
import jax.numpy as jnp
from jax import lax

STEPS = 64
MATS = 8
STRIKES = 11
INPUTS = 6
WIDTH = 1024
PAIRS = 88
SETS = 2048
PATHS = 32768


def draw_params(key, part):
    uniform_draw = jax.random.uniform(key, (SETS, 4), jnp.float32)
    hurst = 0.05 + 0.4 * uniform_draw[:, 0]
    vol_of_vol = 0.8 + 1.2 * uniform_draw[:, 1]
    correl = -0.9 + 0.6 * uniform_draw[:, 2]
    rising = 1.0 + 2.0 * jnp.arange(SETS, dtype=jnp.float32) / SETS
    forward_var = 0.01 * jnp.exp(jnp.log(5.0) * uniform_draw[:, 3]) * rising
    return jnp.stack([hurst, vol_of_vol, correl, forward_var], axis=1).astype(jnp.float32)


def level_of(stream_key, extent, shards, low, top_value):
    def one(dim, blocks):
        draws = jax.random.uniform(jax.random.fold_in(jax.random.fold_in(stream_key, 6), dim), (blocks,), jnp.float32, low / len(shards), top_value / len(shards))
        return jnp.repeat(jnp.exp(draws), extent[dim] // blocks).reshape((-1,) + (1,) * (len(extent) - dim - 1))

    gain = one(*shards[0])
    for cut in shards[1:]:
        gain = gain * one(*cut)
    return gain


def normal_values(stream_key, dims, spread, reach, split=(), kind=jnp.bfloat16):
    level = level_of(stream_key, dims, split, -0.22, 0.18) if split else 1.0
    values = jax.random.normal(stream_key, dims, jnp.float32) * spread * level
    return jnp.minimum(jnp.maximum(values, -reach), reach).astype(kind)


def setup_inputs(seed: int = 0) -> dict:
    arg_keys = jax.random.split(jax.random.key(seed), 9)
    params = draw_params(jax.random.fold_in(arg_keys[8], 71), 0)
    increments = normal_values(arg_keys[1], (2, STEPS, PATHS), 1.0, 5.0, ((2, 256),))
    w_in = normal_values(arg_keys[2], (INPUTS, WIDTH), INPUTS ** -0.5, 2.5)
    b_in = normal_values(arg_keys[3], (WIDTH,), 0.5, 3.0, (), jnp.float32)
    w_mid = normal_values(arg_keys[4], (WIDTH, WIDTH), WIDTH ** -0.5, 0.1875)
    b_mid = normal_values(arg_keys[5], (WIDTH,), 0.5, 3.0, (), jnp.float32)
    w_out = normal_values(arg_keys[6], (WIDTH,), WIDTH ** -0.5, 0.1875)
    b_out = normal_values(arg_keys[7], (1,), 0.5, 3.0, (), jnp.float32)
    return {"params": params, "increments": increments, "w_in": w_in, "b_in": b_in, "w_mid": w_mid, "b_mid": b_mid, "w_out": w_out, "b_out": b_out}


EPSILON = 1e-06

def strike_grid():
    tenors = (jnp.arange(MATS, dtype=jnp.float32) + 1.0) / MATS
    offsets = jnp.arange(STRIKES, dtype=jnp.float32) - (STRIKES - 1) / 2.0
    log_strike = 0.05 * offsets[None, :] * jnp.sqrt(tenors)[:, None]
    return (tenors, log_strike)

def payoff_sums(block_params, increments):
    count = block_params.shape[0]
    paths_here = increments.shape[2]
    hurst = block_params[:, 0]
    vol_of_vol = block_params[:, 1]
    correl = block_params[:, 2]
    forward_var = block_params[:, 3]
    delta_t = 1.0 / STEPS
    position = jnp.arange(STEPS, dtype=jnp.float32)
    lag = position[:, None] - position[None, :]
    lag_high = jnp.maximum(lag, 1.0)
    exponent = (hurst + 0.5)[:, None, None]
    powers = jnp.power(lag_high[None], exponent) - jnp.power(lag_high[None] - 1.0, exponent)
    front = jnp.sqrt(2.0 * hurst) * jnp.power(delta_t, hurst) / (hurst + 0.5)
    kernel = jnp.where((lag >= 1.0)[None], powers * front[:, None, None], 0.0).astype(jnp.bfloat16)
    drive = jnp.dot(kernel.reshape(count * STEPS, STEPS), increments[0], preferred_element_type=jnp.float32)
    drive = drive.reshape(count, STEPS, paths_here)
    times = position * delta_t
    compensator = 0.5 * vol_of_vol[:, None] * vol_of_vol[:, None] * jnp.power(times[None, :], 2.0 * hurst[:, None])
    variance = forward_var[:, None, None] * jnp.exp(vol_of_vol[:, None, None] * drive - compensator[:, :, None])
    first_noise = increments[0].astype(jnp.float32)
    second_noise = increments[1].astype(jnp.float32)
    shock = correl[:, None, None] * first_noise[None] + jnp.sqrt(1.0 - correl * correl)[:, None, None] * second_noise[None]
    moves = jnp.sqrt(variance * delta_t) * shock - 0.5 * delta_t * variance
    log_spot = jnp.cumsum(moves.reshape(count, MATS, STEPS // MATS, paths_here).sum(axis=2), axis=1)
    tenors, log_strike = strike_grid()
    spot = jnp.exp(log_spot)
    gains = jnp.maximum(spot[:, :, None, :] - jnp.exp(log_strike)[None, :, :, None], 0.0)
    return lax.optimization_barrier(jnp.sum(gains, axis=3)).reshape(count, PAIRS)

def features(set_rows):
    count = set_rows.shape[0]
    tenors, log_strike = strike_grid()
    scaled = set_rows * jnp.array([4.0, 1.0, 1.0, 20.0], dtype=jnp.float32)
    per_pair = jnp.stack([4.0 * log_strike.reshape(PAIRS), jnp.repeat(tenors, STRIKES)], axis=1)
    left = jnp.broadcast_to(scaled[:, None, :], (count, PAIRS, 4))
    right = jnp.broadcast_to(per_pair[None], (count, PAIRS, 2))
    return jnp.concatenate([left, right], axis=2).reshape(count * PAIRS, 6).astype(jnp.bfloat16)

def silu_slope(value):
    logistic = jax.nn.sigmoid(value)
    return logistic * (1.0 + value * (1.0 - logistic))

def contract_rows(left, right):
    return lax.dot_general(left, right, (((0,), (0,)), ((), ())), preferred_element_type=jnp.float32)

def local_terms(inputs, target, w_in, b_in, w_mid, b_mid, w_out, b_out, inv_sets):
    raw_in = jnp.dot(inputs, w_in, preferred_element_type=jnp.float32) + b_in
    hidden_in = jax.nn.silu(raw_in).astype(jnp.bfloat16)
    raw_mid = jnp.dot(hidden_in, w_mid, preferred_element_type=jnp.float32) + b_mid
    hidden_mid = jax.nn.silu(raw_mid).astype(jnp.bfloat16)
    predicted = jnp.dot(hidden_mid, w_out, preferred_element_type=jnp.float32) + b_out[0]
    slope = (predicted - target) * inv_sets
    grad_out = lax.optimization_barrier(jnp.sum(hidden_mid.astype(jnp.float32) * slope[:, None], axis=0))
    grad_bout = lax.optimization_barrier(jnp.sum(slope, keepdims=True))
    delta_mid = (slope[:, None] * w_out.astype(jnp.float32)[None, :] * silu_slope(raw_mid)).astype(jnp.bfloat16)
    grad_bmid = lax.optimization_barrier(jnp.sum(delta_mid.astype(jnp.float32), axis=0))
    backward = lax.dot_general(delta_mid, w_mid, (((1,), (1,)), ((), ())), preferred_element_type=jnp.float32)
    delta_in = (backward * silu_slope(raw_in)).astype(jnp.bfloat16)
    grad_in = contract_rows(inputs, delta_in)
    grad_bin = lax.optimization_barrier(jnp.sum(delta_in.astype(jnp.float32), axis=0))
    return ((grad_in, grad_bin, grad_bmid, grad_out, grad_bout), hidden_in, delta_mid)

def directions(grad_w, grad_b):
    entries = grad_w.size + grad_b.size
    mean_square = (jnp.sum(grad_w * grad_w) + jnp.sum(grad_b * grad_b)) / entries
    factor = lax.rsqrt(mean_square + EPSILON)
    return (grad_w * factor, grad_b * factor)

def reference(params, increments, w_in, b_in, w_mid, b_mid, w_out, b_out):
    groups = params.reshape(SETS // 8, 8, 4)
    sums = lax.map(lambda group: payoff_sums(group, increments), groups)
    prices = sums.reshape(SETS, PAIRS) / PATHS
    inv_sets = 1.0 / SETS
    width = w_mid.shape[0]

    def accumulate(carry, element):
        group, target = element
        small, hidden_in, delta_mid = local_terms(features(group), target.reshape(-1), w_in, b_in, w_mid, b_mid, w_out, b_out, inv_sets)
        totals = small + (contract_rows(hidden_in, delta_mid),)
        return (tuple((value + extra for value, extra in zip(carry, totals))), None)
    initial = (jnp.zeros((6, width), jnp.float32), jnp.zeros((width,), jnp.float32), jnp.zeros((width,), jnp.float32), jnp.zeros((width,), jnp.float32), jnp.zeros((1,), jnp.float32), jnp.zeros((width, width), jnp.float32))
    totals, unused = lax.scan(accumulate, initial, (groups, prices.reshape(SETS // 8, 8, PAIRS)))
    grad_in, grad_bin, grad_bmid, grad_out, grad_bout, grad_mid = totals
    direction_w_in, direction_b_in = directions(grad_in, grad_bin)
    direction_w_mid, direction_b_mid = directions(grad_mid, grad_bmid)
    direction_w_out, direction_b_out = directions(grad_out, grad_bout)
    return (prices, direction_w_in, direction_b_in, direction_w_mid, direction_b_mid, direction_w_out, direction_b_out)
```

```python
import math

import jax
import jax.numpy as jnp
from jax import lax
from jax.experimental import pallas as pl
from jax.experimental.pallas import tpu as pltpu
from jax.sharding import PartitionSpec as P

STEPS = 64
MATS = 8
STRIKES = 11
PAIRS = 88
EPSILON = 1e-06
LOG2E = 1.4426950408889634
NX, NY, NZ, NC = 4, 4, 8, 2
OWN = 8
BLOCK = NY * NZ * OWN
BLOCKS = NX * NC
MESH = pl.DeviceIdType.MESH


def strike_grid():
    tenors = (jnp.arange(MATS, dtype=jnp.float32) + 1.0) / MATS
    offsets = jnp.arange(STRIKES, dtype=jnp.float32) - (STRIKES - 1) / 2.0
    log_strike = 0.05 * offsets[None, :] * jnp.sqrt(tenors)[:, None]
    return (tenors, log_strike)


def strike_values():
    return [
        [math.exp(0.05 * (j - 5) * math.sqrt((m + 1) / MATS)) for j in range(STRIKES)]
        for m in range(MATS)
    ]


def round_bf16(x):
    return lax.reduce_precision(x, 8, 7)


def coords(index):
    core = index % NC
    z = (index // NC) % NZ
    y = (index // (NC * NZ)) % NY
    x = index // (NC * NZ * NY)
    return x, y, z, core


def device_at(x, y, z, core):
    return ((x * NY + y) * NZ + z) * NC + core


def set_operands(params):
    hurst, vol, correl, forward = (params[:, k : k + 1] for k in range(4))
    delta_t = 1.0 / STEPS
    lag = jnp.arange(STEPS, dtype=jnp.float32)[None, :]
    high = jnp.maximum(lag, 1.0)
    expo = hurst + 0.5
    powers = jnp.power(high, expo) - jnp.power(high - 1.0, expo)
    front = jnp.sqrt(2.0 * hurst) * jnp.power(delta_t, hurst) / (hurst + 0.5)
    kern = round_bf16(jnp.where(lag >= 1.0, powers * front, 0.0))
    half = (0.5 * LOG2E) * vol
    weight = kern * half
    times = lag * delta_t
    comp = -0.5 * vol * half * jnp.power(times, 2.0 * hurst)
    mix = jnp.sqrt(1.0 - correl * correl)
    const = 0.5 * jnp.log2(forward * delta_t) - 1.0 - jnp.log2(mix)
    w_hi = round_bf16(weight)
    w_lo = round_bf16(weight - w_hi)
    c_hi = round_bf16(comp)
    c_lo = round_bf16(comp - c_hi)
    k_hi = round_bf16(const)
    k_lo = round_bf16(const - k_hi)
    k_ll = const - k_hi - k_lo
    first = lag < 0.5
    rows = jnp.concatenate(
        [
            jnp.where(first, k_hi, w_hi),
            jnp.where(first, k_lo, w_lo),
            jnp.where(first, k_ll, c_hi),
            jnp.where(first, 0.0, c_lo),
        ],
        axis=1,
    ).astype(jnp.bfloat16)
    ratio = jnp.broadcast_to(correl / mix, (params.shape[0], 128))
    scale = (2.0 * LOG2E) * (mix * mix)
    return rows, ratio, scale.reshape(1, -1)


def price_peers(x, y, z, core):
    mine = x * NC + core
    blocks = []
    for b in range(BLOCKS - 1):
        other = (mine + 1 + b) % BLOCKS
        blocks.append(device_at(other // NC, y, z, other % NC))
    along_y = [device_at(x, (y + d) % NY, z, core) for d in range(1, NY)]
    along_z = [device_at(x, y, (z + d) % NZ, core) for d in range(1, NZ)]
    return blocks, along_y, along_z


def prices_kernel(
    rows_ref,
    ratio_ref,
    scale_ref,
    inc_ref,
    out_ref,
    noise,
    table,
    walk,
    part,
    sent,
    got,
    got_y,
    got_z,
    send_sem,
    got_sem,
    send_y,
    got_y_sem,
    send_z,
    got_z_sem,
):
    step = pl.program_id(0)
    x, y, z, core = coords(lax.axis_index("paths"))
    blocks, along_y, along_z = price_peers(x, y, z, core)

    @pl.when(step == 0)
    def _():
        barrier = pltpu.get_barrier_semaphore()
        for peer in blocks + along_y + along_z:
            pl.semaphore_signal(barrier, inc=1, device_id=(peer,), device_id_type=MESH)
        noise[0] = inc_ref[0].astype(jnp.float32)
        noise[1] = inc_ref[1].astype(jnp.float32)
        part[...] = jnp.zeros_like(part)
        row = lax.broadcasted_iota(jnp.int32, (STEPS, 128), 0)
        for j in range(STEPS):
            walk[pl.ds(STEPS - 1 - j, 1), :] = noise[0, pl.ds(j, 1), :]
        walk[pl.ds(STEPS, STEPS), :] = jnp.zeros((STEPS, 128), jnp.float32)
        one = jnp.ones((STEPS, 128), jnp.float32)
        for i in range(STEPS):
            past = walk[pl.ds(STEPS - 1 - i, STEPS), :]
            past = jnp.where(row == 0, one, past).astype(jnp.bfloat16)
            pick = jnp.where(row == i, 1.0, 0.0)
            hot = jnp.where(row == 0, one, pick).astype(jnp.bfloat16)
            hot_lo = jnp.where(row == 0, 0.0, pick).astype(jnp.bfloat16)
            cols = pl.ds((i % 2) * 128, 128)
            table[i // 2, pl.ds(0, STEPS), cols] = past
            table[i // 2, pl.ds(STEPS, STEPS), cols] = past
            table[i // 2, pl.ds(2 * STEPS, STEPS), cols] = hot
            table[i // 2, pl.ds(3 * STEPS, STEPS), cols] = hot_lo

    strikes = strike_values()
    walk[...] = jnp.zeros_like(walk)
    scale = scale_ref[...]
    for m in range(MATS):
        for q in range(4):
            pair = jnp.dot(
                rows_ref[...], table[m * 4 + q], preferred_element_type=jnp.float32
            )
            for h in range(2):
                i = m * 8 + q * 2 + h
                vol = jnp.exp2(pair[:, h * 128 : (h + 1) * 128])
                shock = ratio_ref[...] * noise[0, pl.ds(i, 1), :] + noise[1, pl.ds(i, 1), :]
                walk[...] += vol * (shock - vol)
        spot = jnp.exp2(walk[...].T * scale)
        for j in range(STRIKES):
            k = strikes[m][j]
            top = jnp.sum(jnp.maximum(spot, k).reshape(16, 8, BLOCK), axis=0)
            part[pl.ds(m * STRIKES + j, 1), :] = jnp.sum(top - 16.0 * k, axis=0, keepdims=True)
    sent[step] = part[...].T

    @pl.when(step == 0)
    def _():
        pl.semaphore_wait(pltpu.get_barrier_semaphore(), len(blocks + along_y + along_z))

    def block_copy(b):
        other = (x * NC + core + 1 + b) % BLOCKS
        return pltpu.make_async_remote_copy(
            src_ref=sent.at[b],
            dst_ref=got.at[b],
            send_sem=send_sem.at[b],
            recv_sem=got_sem.at[b],
            device_id=(device_at(other // NC, y, z, other % NC),),
            device_id_type=MESH,
        )

    @pl.when(step < BLOCKS - 1)
    def _():
        block_copy(step).start()

    @pl.when(step == BLOCKS - 1)
    def _():
        total = sent.at[BLOCKS - 1]
        for b in range(BLOCKS - 1):
            block_copy(b).wait_recv()
            total[...] += got[b]
        rows_y = NZ * OWN

        def y_rows(d):
            return pl.ds(pl.multiple_of(((y + d) % NY) * rows_y, rows_y), rows_y)

        copies = []
        for d in range(1, NY):
            copy = pltpu.make_async_remote_copy(
                src_ref=total.at[y_rows(d), :],
                dst_ref=got_y.at[d],
                send_sem=send_y.at[d],
                recv_sem=got_y_sem.at[d],
                device_id=(along_y[d - 1],),
                device_id_type=MESH,
            )
            copy.start()
            copies.append(copy)
        own = total[y_rows(0), :]
        for d in range(1, NY):
            copies[d - 1].wait_recv()
            own = own + got_y[d]
        got_y[0] = own

        def z_rows(d):
            return pl.ds(pl.multiple_of(((z + d) % NZ) * OWN, OWN), OWN)

        for d in range(1, NZ):
            copy = pltpu.make_async_remote_copy(
                src_ref=got_y.at[0, z_rows(d), :],
                dst_ref=got_z.at[d],
                send_sem=send_z.at[d],
                recv_sem=got_z_sem.at[d],
                device_id=(along_z[d - 1],),
                device_id_type=MESH,
            )
            copy.start()
            copies.append(copy)
        final = got_y[0, z_rows(0), :]
        for d in range(1, NZ):
            copies[NY - 1 + d - 1].wait_recv()
            final = final + got_z[d]
        out_ref[...] = final
        for b in range(BLOCKS - 1):
            block_copy(b).wait_send()
        for copy in copies:
            copy.wait_send()


def price_sums(params, increments):
    index = lax.axis_index("paths")
    x, y, z, core = coords(index)
    order = params.reshape(NX, NY, NZ, NC, OWN, 4).transpose(0, 3, 1, 2, 4, 5)
    order = order.reshape(BLOCKS, BLOCK, 4)
    order = jnp.concatenate([order, order], axis=0)
    order = lax.dynamic_slice_in_dim(order, x * NC + core + 1, BLOCKS, 0)
    rows, ratio, scale = set_operands(order.reshape(BLOCKS * BLOCK, 4))
    return pl.pallas_call(
        prices_kernel,
        grid=(BLOCKS,),
        in_specs=[
            pl.BlockSpec((BLOCK, 256), lambda b: (b, 0)),
            pl.BlockSpec((BLOCK, 128), lambda b: (b, 0)),
            pl.BlockSpec((1, BLOCK), lambda b: (0, b)),
            pl.BlockSpec((2, STEPS, 128), lambda b: (0, 0, 0)),
        ],
        out_specs=pl.BlockSpec((OWN, 128), lambda b: (0, 0)),
        out_shape=jax.ShapeDtypeStruct((OWN, 128), jnp.float32),
        scratch_shapes=[
            pltpu.VMEM((2, STEPS, 128), jnp.float32),
            pltpu.VMEM((STEPS // 2, 256, 256), jnp.bfloat16),
            pltpu.VMEM((BLOCK, 128), jnp.float32),
            pltpu.VMEM((128, BLOCK), jnp.float32),
            pltpu.VMEM((BLOCKS, BLOCK, 128), jnp.float32),
            pltpu.VMEM((BLOCKS - 1, BLOCK, 128), jnp.float32),
            pltpu.VMEM((NY, NZ * OWN, 128), jnp.float32),
            pltpu.VMEM((NZ, OWN, 128), jnp.float32),
            pltpu.SemaphoreType.DMA((BLOCKS,)),
            pltpu.SemaphoreType.DMA((BLOCKS,)),
            pltpu.SemaphoreType.DMA((NY,)),
            pltpu.SemaphoreType.DMA((NY,)),
            pltpu.SemaphoreType.DMA((NZ,)),
            pltpu.SemaphoreType.DMA((NZ,)),
        ],
        compiler_params=pltpu.CompilerParams(collective_id=0, has_side_effects=True),
        name="prices",
    )(rows, ratio, scale, increments)


WIDE = 1024
HALF = WIDE // NC
ROWS_A = WIDE // NX
ROWS_B = ROWS_A // NY
ROWS_Z = ROWS_B // NZ
SMALL = 16
SLICE = HALF // NX


def sum_kernel(
    big_ref,
    small_ref,
    big_out,
    small_out,
    got_c,
    half,
    got_a,
    mid,
    got_b,
    low,
    got_z,
    s_got_c,
    s_got_a,
    s_b,
    s_z,
    s_sum,
    send_sem,
    recv_sem,
):
    x, y, z, core = coords(lax.axis_index("paths"))
    a = x * (1 - core) + y * core
    b = y * (1 - core) + x * core

    def at(aa, bb, zz):
        return device_at(aa * (1 - core) + bb * core, bb * (1 - core) + aa * core, zz, core)

    partner = device_at(x, y, z, 1 - core)
    along_a = [at((a + d) % NX, b, z) for d in range(1, NX)]
    along_b = [at(a, (b + d) % NY, z) for d in range(1, NY)]
    along_z = [at(a, b, (z + d) % NZ) for d in range(1, NZ)]
    peers = [partner] + along_a + along_b + along_z
    barrier = pltpu.get_barrier_semaphore()
    for peer in peers:
        pl.semaphore_signal(barrier, inc=1, device_id=(peer,), device_id_type=MESH)
    pl.semaphore_wait(barrier, len(peers))

    count = [0]
    started = []

    def send(src, dst, peer):
        k = count[0]
        count[0] += 1
        copy = pltpu.make_async_remote_copy(
            src_ref=src,
            dst_ref=dst,
            send_sem=send_sem.at[k],
            recv_sem=recv_sem.at[k],
            device_id=(peer,),
            device_id_type=MESH,
        )
        copy.start()
        started.append(copy)
        return copy

    def part(index, size):
        return pl.ds(pl.multiple_of(index * size, size), size)

    own_cols, other_cols = part(core, HALF), part(1 - core, HALF)
    big = send(big_ref.at[:, other_cols], got_c, partner)
    little = send(small_ref.at[:, other_cols], s_got_c, partner)
    little.wait_recv()
    s_got_c[...] += small_ref[:, own_cols]
    big.wait_recv()
    half[...] = big_ref[:, own_cols] + got_c[...]

    bigs, littles = [], []
    for d in range(1, NX):
        aa = (a + d) % NX
        bigs.append(send(half.at[part(aa, ROWS_A), :], got_a.at[d - 1], along_a[d - 1]))
        littles.append(send(s_got_c.at[:, part(aa, SLICE)], s_got_a.at[d - 1], along_a[d - 1]))
    for d in range(1, NX):
        littles[d - 1].wait_recv()
    s_b[b] = s_got_c[:, part(a, SLICE)] + s_got_a[0] + s_got_a[1] + s_got_a[2]
    for d in range(1, NX):
        bigs[d - 1].wait_recv()
    mid[...] = half[part(a, ROWS_A), :] + got_a[0] + got_a[1] + got_a[2]

    bigs, littles = [], []
    for d in range(1, NY):
        bb = (b + d) % NY
        bigs.append(send(mid.at[part(bb, ROWS_B), :], got_b.at[d - 1], along_b[d - 1]))
        littles.append(send(s_b.at[b], s_b.at[b], along_b[d - 1]))
    for d in range(1, NY):
        littles[d - 1].wait_recv()
    s_z[z] = (s_b[0] + s_b[1]) + (s_b[2] + s_b[3])
    for d in range(1, NY):
        bigs[d - 1].wait_recv()
    low[...] = mid[part(b, ROWS_B), :] + got_b[0] + got_b[1] + got_b[2]

    bigs, littles = [], []
    for d in range(1, NZ):
        zz = (z + d) % NZ
        bigs.append(send(low.at[part(zz, ROWS_Z), :], got_z.at[d - 1], along_z[d - 1]))
        littles.append(send(s_z.at[z], s_z.at[z], along_z[d - 1]))
    for d in range(1, NZ):
        littles[d - 1].wait_recv()
    s_all = ((s_z[0] + s_z[1]) + (s_z[2] + s_z[3])) + ((s_z[4] + s_z[5]) + (s_z[6] + s_z[7]))
    s_sum[:, part(a, SLICE)] = s_all
    final = low[part(z, ROWS_Z), :]
    for d in range(1, NZ):
        bigs[d - 1].wait_recv()
        final = final + got_z[d - 1]

    base_b = a * ROWS_A + b * ROWS_B
    mine = pl.ds(pl.multiple_of(base_b + z * ROWS_Z, ROWS_Z), ROWS_Z)
    half_out = big_out.at[core]
    half_out[mine, :] = final
    bigs = [send(half_out.at[mine, :], half_out.at[mine, :], peer) for peer in along_z]
    littles = [
        send(s_sum.at[:, part(a, SLICE)], s_sum.at[:, part(a, SLICE)], peer) for peer in along_a
    ]
    for copy in bigs:
        copy.wait_recv()
    rows_b = pl.ds(pl.multiple_of(base_b, ROWS_B), ROWS_B)
    bigs = [send(half_out.at[rows_b, :], half_out.at[rows_b, :], peer) for peer in along_b]
    for copy in littles:
        copy.wait_recv()
    small_out[core] = s_sum[...]
    little = send(small_out.at[core], small_out.at[core], partner)
    for copy in bigs:
        copy.wait_recv()
    rows_a = part(a, ROWS_A)
    bigs = [send(half_out.at[rows_a, :], half_out.at[rows_a, :], peer) for peer in along_a]
    for copy in bigs:
        copy.wait_recv()
    big = send(half_out, half_out, partner)
    little.wait_recv()
    big.wait_recv()
    for copy in started:
        copy.wait_send()


SENDS = 2 + 2 * (NX - 1) + 2 * (NY - 1) + 2 * (NZ - 1) + (NZ - 1) + (NX - 1) + (NY - 1) + (NX - 1) + 2


def sum_gradients(big, small):
    f32 = jnp.float32
    vmem = pl.BlockSpec(memory_space=pltpu.VMEM)
    return pl.pallas_call(
        sum_kernel,
        in_specs=[vmem, vmem],
        out_specs=[vmem, vmem],
        out_shape=[
            jax.ShapeDtypeStruct((NC, WIDE, HALF), f32),
            jax.ShapeDtypeStruct((NC, SMALL, HALF), f32),
        ],
        scratch_shapes=[
            pltpu.VMEM((WIDE, HALF), f32),
            pltpu.VMEM((WIDE, HALF), f32),
            pltpu.VMEM((NX - 1, ROWS_A, HALF), f32),
            pltpu.VMEM((ROWS_A, HALF), f32),
            pltpu.VMEM((NY - 1, ROWS_B, HALF), f32),
            pltpu.VMEM((ROWS_B, HALF), f32),
            pltpu.VMEM((NZ - 1, ROWS_Z, HALF), f32),
            pltpu.VMEM((SMALL, HALF), f32),
            pltpu.VMEM((NX - 1, SMALL, SLICE), f32),
            pltpu.VMEM((NY, SMALL, SLICE), f32),
            pltpu.VMEM((NZ, SMALL, SLICE), f32),
            pltpu.VMEM((SMALL, HALF), f32),
            pltpu.SemaphoreType.DMA((SENDS,)),
            pltpu.SemaphoreType.DMA((SENDS,)),
        ],
        compiler_params=pltpu.CompilerParams(collective_id=1, has_side_effects=True),
        name="gradients",
    )(big, small)


def features(set_rows):
    count = set_rows.shape[0]
    tenors, log_strike = strike_grid()
    scaled = set_rows * jnp.array([4.0, 1.0, 1.0, 20.0], dtype=jnp.float32)
    per_pair = jnp.stack([4.0 * log_strike.reshape(PAIRS), jnp.repeat(tenors, STRIKES)], axis=1)
    left = jnp.broadcast_to(scaled[:, None, :], (count, PAIRS, 4))
    right = jnp.broadcast_to(per_pair[None], (count, PAIRS, 2))
    return jnp.concatenate([left, right], axis=2).reshape(count * PAIRS, 6).astype(jnp.bfloat16)


def silu_slope(value):
    logistic = jax.nn.sigmoid(value)
    return logistic * (1.0 + value * (1.0 - logistic))


def contract_rows(left, right):
    return lax.dot_general(
        left, right, (((0,), (0,)), ((), ())), preferred_element_type=jnp.float32
    )


def local_terms(inputs, target, w_in, b_in, w_mid, b_mid, w_out, b_out, inv_sets):
    raw_in = jnp.dot(inputs, w_in, preferred_element_type=jnp.float32) + b_in
    hidden_in = jax.nn.silu(raw_in).astype(jnp.bfloat16)
    raw_mid = jnp.dot(hidden_in, w_mid, preferred_element_type=jnp.float32) + b_mid
    hidden_mid = jax.nn.silu(raw_mid).astype(jnp.bfloat16)
    predicted = jnp.dot(hidden_mid, w_out, preferred_element_type=jnp.float32) + b_out[0]
    slope = (predicted - target) * inv_sets
    grad_out = jnp.sum(hidden_mid.astype(jnp.float32) * slope[:, None], axis=0)
    grad_bout = jnp.sum(slope, keepdims=True)
    delta_mid = (slope[:, None] * w_out.astype(jnp.float32)[None, :] * silu_slope(raw_mid)).astype(
        jnp.bfloat16
    )
    grad_bmid = jnp.sum(delta_mid.astype(jnp.float32), axis=0)
    backward = lax.dot_general(
        delta_mid, w_mid, (((1,), (1,)), ((), ())), preferred_element_type=jnp.float32
    )
    delta_in = (backward * silu_slope(raw_in)).astype(jnp.bfloat16)
    grad_in = contract_rows(inputs, delta_in)
    grad_bin = jnp.sum(delta_in.astype(jnp.float32), axis=0)
    return ((grad_in, grad_bin, grad_bmid, grad_out, grad_bout), hidden_in, delta_mid)


def directions(grad_w, grad_b):
    entries = grad_w.size + grad_b.size
    mean_square = (jnp.sum(grad_w * grad_w) + jnp.sum(grad_b * grad_b)) / entries
    factor = lax.rsqrt(mean_square + EPSILON)
    return (grad_w * factor, grad_b * factor)


def on_device(params, increments, w_in, b_in, w_mid, b_mid, w_out, b_out):
    devices = lax.axis_size("paths")
    total_paths = increments.shape[2] * devices
    set_count = params.shape[0]
    owner = lax.axis_index("paths")
    prices = price_sums(params, increments)[:, :PAIRS] / total_paths
    own_params = lax.dynamic_slice_in_dim(params, owner * OWN, OWN, 0)
    small, hidden_in, delta_mid = local_terms(
        features(own_params),
        prices.reshape(-1),
        w_in,
        b_in,
        w_mid,
        b_mid,
        w_out,
        b_out,
        1.0 / set_count,
    )
    grad_mid = contract_rows(hidden_in, delta_mid)
    pad_out = jnp.pad(small[4], (0, WIDE - 1))
    packed = jnp.concatenate(
        [small[0], jnp.stack([small[1], small[2], small[3], pad_out]), jnp.zeros((6, WIDE), jnp.float32)]
    )
    big, little = sum_gradients(grad_mid, packed)
    grad_mid = jnp.concatenate([big[0], big[1]], axis=1)
    little = jnp.concatenate([little[0], little[1]], axis=1)
    direction_w_mid, direction_b_mid = directions(grad_mid, little[7])
    direction_w_in, direction_b_in = directions(little[:6], little[6])
    direction_w_out, direction_b_out = directions(little[8], little[9, :1])
    return (
        prices,
        direction_w_in,
        direction_b_in,
        direction_w_mid,
        direction_b_mid,
        direction_w_out,
        direction_b_out,
    )


def solution(mesh):
    in_specs = (P(), P(None, None, "paths"), P(), P(), P(), P(), P(), P())
    out_specs = (P("paths", None), P(), P(), P(), P(), P(), P())
    return jax.shard_map(
        on_device, mesh=mesh, in_specs=in_specs, out_specs=out_specs, check_vma=False
    )
```

```python
import math

import jax
import jax.numpy as jnp
import numpy as np
from jax import lax
from jax.experimental import pallas as pl
from jax.experimental.pallas import tpu as pltpu
from jax.sharding import PartitionSpec as P

STEPS = 64
MATS = 8
STRIKES = 11
PAIRS = 88
EPSILON = 1e-06
LOG2E = 1.4426950408889634
NX, NY, NZ, NC = 4, 4, 8, 2
OWN = 8
BLOCK = NY * NZ * OWN
BLOCKS = NX * NC
SETS = 2048
TOTAL_PATHS = 32768
MESH = pl.DeviceIdType.MESH


def strike_values():
    return [
        [math.exp(0.05 * (j - 5) * math.sqrt((m + 1) / MATS)) for j in range(STRIKES)]
        for m in range(MATS)
    ]


def coords(index):
    core = index % NC
    z = (index // NC) % NZ
    y = (index // (NC * NZ)) % NY
    x = index // (NC * NZ * NY)
    return x, y, z, core


def device_at(x, y, z, core):
    return ((x * NY + y) * NZ + z) * NC + core


def lag_tables():
    lag = np.tile(np.arange(STEPS, dtype=np.float64), 2)
    table = np.zeros((8, 128), np.float32)
    table[0] = np.log2(np.maximum(lag, 1.0))
    table[1] = np.log2(np.maximum(lag - 1.0, 1.0))
    table[2] = np.log2(np.maximum(lag, 1.0) / STEPS)
    return table


def set_operands(sets, lag_ref, rows, ratio, scale):
    f32, bf16 = jnp.float32, jnp.bfloat16
    shape = (sets.shape[0], 128)
    hurst, vol, correl, forward = (
        jnp.broadcast_to(sets[:, k : k + 1], shape) for k in range(4)
    )
    lane = lax.broadcasted_iota(jnp.int32, shape, 1)
    upper = lane >= STEPS
    lag = jnp.where(upper, lane - STEPS, lane)
    expo = hurst + 0.5
    late = jnp.where(lag >= 2, jnp.exp2(expo * lag_ref[1:2, :]), 0.0)
    powers = jnp.exp2(expo * lag_ref[0:1, :]) - late
    front = jnp.sqrt(2.0 * hurst) * jnp.exp2(-6.0 * hurst) / expo
    kern = jnp.where(lag >= 1, powers * front, 0.0).astype(bf16).astype(f32)
    half = (0.5 * LOG2E) * vol
    weight = kern * half
    comp = (-0.5 * vol * half) * jnp.exp2((2.0 * hurst) * lag_ref[2:3, :])
    rest = 1.0 - correl * correl
    const = (0.5 * LOG2E) * jnp.log(forward * (1.0 / STEPS) / rest) - 1.0
    w_hi = weight.astype(bf16).astype(f32)
    c_hi = comp.astype(bf16).astype(f32)
    k_hi = const.astype(bf16).astype(f32)
    k_rest = const - k_hi
    k_lo = k_rest.astype(bf16).astype(f32)
    first = lag == 0
    kern_row = jnp.where(first, jnp.where(upper, k_lo, k_hi), jnp.where(upper, weight - w_hi, w_hi))
    comp_row = jnp.where(
        first, jnp.where(upper, 0.0, k_rest - k_lo), jnp.where(upper, comp - c_hi, c_hi)
    )
    rows[:, 0:128] = kern_row.astype(bf16)
    rows[:, 128:256] = comp_row.astype(bf16)
    ratio[...] = correl * lax.rsqrt(rest)
    scale[...] = (2.0 * LOG2E) * rest


def price_peers(x, y, z, core):
    mine = x * NC + core
    blocks = []
    for b in range(BLOCKS - 1):
        other = (mine + 1 + b) % BLOCKS
        blocks.append(device_at(other // NC, y, z, other % NC))
    along_y = [device_at(x, (y + d) % NY, z, core) for d in range(1, NY)]
    along_z = [device_at(x, y, (z + d) % NZ, core) for d in range(1, NZ)]
    return blocks, along_y, along_z


def prices_kernel(
    params_ref,
    lag_ref,
    inc_ref,
    out_ref,
    own_ref,
    sets,
    rows_ref,
    ratio_ref,
    scale_ref,
    noise,
    table,
    walk,
    part,
    sent,
    got,
    got_y,
    got_z,
    send_sem,
    got_sem,
    send_y,
    got_y_sem,
    send_z,
    got_z_sem,
):
    step = pl.program_id(0)
    x, y, z, core = coords(lax.axis_index("paths"))
    blocks, along_y, along_z = price_peers(x, y, z, core)

    @pl.when(step == 0)
    def _():
        barrier = pltpu.get_barrier_semaphore()
        for peer in blocks + along_y + along_z:
            pl.semaphore_signal(barrier, inc=1, device_id=(peer,), device_id_type=MESH)
        for k in range(NX * NY):
            some = params_ref[:, pl.ds(k * 128, 128)]
            some = jnp.concatenate([some, jnp.zeros((120, 128), jnp.float32)], axis=0).T
            sets[k // NY, pl.ds((k % NY) * NZ, NZ)] = some.reshape(NZ, NC, OWN, 128)
        own_ref[...] = sets[x, y * NZ + z, core]
        noise[0] = inc_ref[0].astype(jnp.float32)
        noise[1] = inc_ref[1].astype(jnp.float32)
        part[...] = jnp.zeros_like(part)
        row = lax.broadcasted_iota(jnp.int32, (STEPS, 128), 0)
        for j in range(STEPS):
            walk[pl.ds(STEPS - 1 - j, 1), :] = noise[0, pl.ds(j, 1), :]
        walk[pl.ds(STEPS, STEPS), :] = jnp.zeros((STEPS, 128), jnp.float32)
        one = jnp.ones((STEPS, 128), jnp.float32)
        for i in range(STEPS):
            past = walk[pl.ds(STEPS - 1 - i, STEPS), :]
            past = jnp.where(row == 0, one, past).astype(jnp.bfloat16)
            pick = jnp.where(row == i, 1.0, 0.0)
            hot = jnp.where(row == 0, one, pick).astype(jnp.bfloat16)
            hot_lo = jnp.where(row == 0, 0.0, pick).astype(jnp.bfloat16)
            cols = pl.ds((i % 2) * 128, 128)
            table[i // 2, pl.ds(0, STEPS), cols] = past
            table[i // 2, pl.ds(STEPS, STEPS), cols] = past
            table[i // 2, pl.ds(2 * STEPS, STEPS), cols] = hot
            table[i // 2, pl.ds(3 * STEPS, STEPS), cols] = hot_lo

    strikes = strike_values()
    other = (x * NC + core + 1 + step) % BLOCKS
    block = sets[other // NC, :, other % NC].reshape(BLOCK, 128)
    set_operands(block, lag_ref, rows_ref, ratio_ref, scale_ref)
    walk[...] = jnp.zeros_like(walk)
    for m in range(MATS):
        for q in range(4):
            pair = jnp.dot(
                rows_ref[...], table[m * 4 + q], preferred_element_type=jnp.float32
            )
            for h in range(2):
                i = m * 8 + q * 2 + h
                vol = jnp.exp2(pair[:, h * 128 : (h + 1) * 128])
                shock = ratio_ref[...] * noise[0, pl.ds(i, 1), :] + noise[1, pl.ds(i, 1), :]
                walk[...] += vol * (shock - vol)
        spot = jnp.exp2((walk[...] * scale_ref[...]).T)
        for j in range(STRIKES):
            k = strikes[m][j]
            top = jnp.sum(jnp.maximum(spot, k).reshape(16, 8, BLOCK), axis=0)
            part[pl.ds(m * STRIKES + j, 1), :] = jnp.sum(top - 16.0 * k, axis=0, keepdims=True)
    sent[step] = part[...].T

    @pl.when(step == 0)
    def _():
        pl.semaphore_wait(pltpu.get_barrier_semaphore(), len(blocks + along_y + along_z))

    def block_copy(b):
        other = (x * NC + core + 1 + b) % BLOCKS
        return pltpu.make_async_remote_copy(
            src_ref=sent.at[b],
            dst_ref=got.at[b],
            send_sem=send_sem.at[b],
            recv_sem=got_sem.at[b],
            device_id=(device_at(other // NC, y, z, other % NC),),
            device_id_type=MESH,
        )

    @pl.when(step < BLOCKS - 1)
    def _():
        block_copy(step).start()

    @pl.when(step == BLOCKS - 1)
    def _():
        total = sent.at[BLOCKS - 1]
        for b in range(BLOCKS - 1):
            block_copy(b).wait_recv()
            total[...] += got[b]
        rows_y = NZ * OWN

        def y_rows(d):
            return pl.ds(pl.multiple_of(((y + d) % NY) * rows_y, rows_y), rows_y)

        copies = []
        for d in range(1, NY):
            copy = pltpu.make_async_remote_copy(
                src_ref=total.at[y_rows(d), :],
                dst_ref=got_y.at[d],
                send_sem=send_y.at[d],
                recv_sem=got_y_sem.at[d],
                device_id=(along_y[d - 1],),
                device_id_type=MESH,
            )
            copy.start()
            copies.append(copy)
        own = total[y_rows(0), :]
        for d in range(1, NY):
            copies[d - 1].wait_recv()
            own = own + got_y[d]
        got_y[0] = own

        def z_rows(d):
            return pl.ds(pl.multiple_of(((z + d) % NZ) * OWN, OWN), OWN)

        for d in range(1, NZ):
            copy = pltpu.make_async_remote_copy(
                src_ref=got_y.at[0, z_rows(d), :],
                dst_ref=got_z.at[d],
                send_sem=send_z.at[d],
                recv_sem=got_z_sem.at[d],
                device_id=(along_z[d - 1],),
                device_id_type=MESH,
            )
            copy.start()
            copies.append(copy)
        final = got_y[0, z_rows(0), :]
        for d in range(1, NZ):
            copies[NY - 1 + d - 1].wait_recv()
            final = final + got_z[d]
        out_ref[...] = final
        for b in range(BLOCKS - 1):
            block_copy(b).wait_send()
        for copy in copies:
            copy.wait_send()


def price_sums(params, increments):
    f32 = jnp.float32
    own = jax.ShapeDtypeStruct((OWN, 128), f32)
    return pl.pallas_call(
        prices_kernel,
        grid=(BLOCKS,),
        in_specs=[
            pl.BlockSpec((8, BLOCKS * BLOCK), lambda b: (0, 0)),
            pl.BlockSpec((8, 128), lambda b: (0, 0)),
            pl.BlockSpec((2, STEPS, 128), lambda b: (0, 0, 0)),
        ],
        out_specs=[pl.BlockSpec((OWN, 128), lambda b: (0, 0))] * 2,
        out_shape=[own, own],
        scratch_shapes=[
            pltpu.VMEM((NX, NY * NZ, NC, OWN, 128), f32),
            pltpu.VMEM((BLOCK, 256), jnp.bfloat16),
            pltpu.VMEM((BLOCK, 128), f32),
            pltpu.VMEM((BLOCK, 128), f32),
            pltpu.VMEM((2, STEPS, 128), f32),
            pltpu.VMEM((STEPS // 2, 256, 256), jnp.bfloat16),
            pltpu.VMEM((BLOCK, 128), f32),
            pltpu.VMEM((128, BLOCK), f32),
            pltpu.VMEM((BLOCKS, BLOCK, 128), f32),
            pltpu.VMEM((BLOCKS - 1, BLOCK, 128), f32),
            pltpu.VMEM((NY, NZ * OWN, 128), f32),
            pltpu.VMEM((NZ, OWN, 128), f32),
            pltpu.SemaphoreType.DMA((BLOCKS,)),
            pltpu.SemaphoreType.DMA((BLOCKS,)),
            pltpu.SemaphoreType.DMA((NY,)),
            pltpu.SemaphoreType.DMA((NY,)),
            pltpu.SemaphoreType.DMA((NZ,)),
            pltpu.SemaphoreType.DMA((NZ,)),
        ],
        compiler_params=pltpu.CompilerParams(collective_id=0, has_side_effects=True),
        name="prices",
    )(jnp.pad(params.T, ((0, 4), (0, 0))), jnp.asarray(lag_tables()), increments)


WIDE = 1024
HALF = WIDE // NC
ROWS_A = WIDE // NX
ROWS_B = ROWS_A // NY
ROWS_Z = ROWS_B // NZ
SMALL = 16
SLICE = HALF // NX


def sum_kernel(
    big_ref,
    small_ref,
    big_out,
    small_out,
    got_c,
    half,
    got_a,
    mid,
    got_b,
    low,
    got_z,
    s_got_c,
    s_got_a,
    s_b,
    s_z,
    s_sum,
    send_sem,
    recv_sem,
):
    x, y, z, core = coords(lax.axis_index("paths"))
    a = x * (1 - core) + y * core
    b = y * (1 - core) + x * core

    def at(aa, bb, zz):
        return device_at(aa * (1 - core) + bb * core, bb * (1 - core) + aa * core, zz, core)

    partner = device_at(x, y, z, 1 - core)
    along_a = [at((a + d) % NX, b, z) for d in range(1, NX)]
    along_b = [at(a, (b + d) % NY, z) for d in range(1, NY)]
    along_z = [at(a, b, (z + d) % NZ) for d in range(1, NZ)]
    peers = [partner] + along_a + along_b + along_z
    barrier = pltpu.get_barrier_semaphore()
    for peer in peers:
        pl.semaphore_signal(barrier, inc=1, device_id=(peer,), device_id_type=MESH)
    pl.semaphore_wait(barrier, len(peers))

    count = [0]
    started = []

    def send(src, dst, peer):
        k = count[0]
        count[0] += 1
        copy = pltpu.make_async_remote_copy(
            src_ref=src,
            dst_ref=dst,
            send_sem=send_sem.at[k],
            recv_sem=recv_sem.at[k],
            device_id=(peer,),
            device_id_type=MESH,
        )
        copy.start()
        started.append(copy)
        return copy

    def part(index, size):
        return pl.ds(pl.multiple_of(index * size, size), size)

    own_cols, other_cols = part(core, HALF), part(1 - core, HALF)
    big = send(big_ref.at[:, other_cols], got_c, partner)
    little = send(small_ref.at[:, other_cols], s_got_c, partner)
    little.wait_recv()
    s_got_c[...] += small_ref[:, own_cols]
    big.wait_recv()
    half[...] = big_ref[:, own_cols] + got_c[...]

    bigs, littles = [], []
    for d in range(1, NX):
        aa = (a + d) % NX
        bigs.append(send(half.at[part(aa, ROWS_A), :], got_a.at[d - 1], along_a[d - 1]))
        littles.append(send(s_got_c.at[:, part(aa, SLICE)], s_got_a.at[d - 1], along_a[d - 1]))
    for d in range(1, NX):
        littles[d - 1].wait_recv()
    s_b[b] = s_got_c[:, part(a, SLICE)] + s_got_a[0] + s_got_a[1] + s_got_a[2]
    for d in range(1, NX):
        bigs[d - 1].wait_recv()
    mid[...] = half[part(a, ROWS_A), :] + got_a[0] + got_a[1] + got_a[2]

    bigs, littles = [], []
    for d in range(1, NY):
        bb = (b + d) % NY
        bigs.append(send(mid.at[part(bb, ROWS_B), :], got_b.at[d - 1], along_b[d - 1]))
        littles.append(send(s_b.at[b], s_b.at[b], along_b[d - 1]))
    for d in range(1, NY):
        littles[d - 1].wait_recv()
    s_z[z] = (s_b[0] + s_b[1]) + (s_b[2] + s_b[3])
    for d in range(1, NY):
        bigs[d - 1].wait_recv()
    low[...] = mid[part(b, ROWS_B), :] + got_b[0] + got_b[1] + got_b[2]

    bigs, littles = [], []
    for d in range(1, NZ):
        zz = (z + d) % NZ
        bigs.append(send(low.at[part(zz, ROWS_Z), :], got_z.at[d - 1], along_z[d - 1]))
        littles.append(send(s_z.at[z], s_z.at[z], along_z[d - 1]))
    for d in range(1, NZ):
        littles[d - 1].wait_recv()
    s_all = ((s_z[0] + s_z[1]) + (s_z[2] + s_z[3])) + ((s_z[4] + s_z[5]) + (s_z[6] + s_z[7]))
    s_sum[:, part(a, SLICE)] = s_all
    final = low[part(z, ROWS_Z), :]
    for d in range(1, NZ):
        bigs[d - 1].wait_recv()
        final = final + got_z[d - 1]

    base_b = a * ROWS_A + b * ROWS_B
    mine = pl.ds(pl.multiple_of(base_b + z * ROWS_Z, ROWS_Z), ROWS_Z)
    half_out = big_out.at[core]
    half_out[mine, :] = final
    bigs = [send(half_out.at[mine, :], half_out.at[mine, :], peer) for peer in along_z]
    littles = [
        send(s_sum.at[:, part(a, SLICE)], s_sum.at[:, part(a, SLICE)], peer) for peer in along_a
    ]
    for copy in bigs:
        copy.wait_recv()
    rows_b = pl.ds(pl.multiple_of(base_b, ROWS_B), ROWS_B)
    bigs = [send(half_out.at[rows_b, :], half_out.at[rows_b, :], peer) for peer in along_b]
    for copy in littles:
        copy.wait_recv()
    small_out[core] = s_sum[...]
    little = send(small_out.at[core], small_out.at[core], partner)
    for copy in bigs:
        copy.wait_recv()
    rows_a = part(a, ROWS_A)
    bigs = [send(half_out.at[rows_a, :], half_out.at[rows_a, :], peer) for peer in along_a]
    for copy in bigs:
        copy.wait_recv()
    big = send(half_out, half_out, partner)
    little.wait_recv()
    big.wait_recv()
    for copy in started:
        copy.wait_send()


SENDS = 2 + 2 * (NX - 1) + 2 * (NY - 1) + 2 * (NZ - 1) + (NZ - 1) + (NX - 1) + (NY - 1) + (NX - 1) + 2


def sum_gradients(big, small):
    f32 = jnp.float32
    vmem = pl.BlockSpec(memory_space=pltpu.VMEM)
    return pl.pallas_call(
        sum_kernel,
        in_specs=[vmem, vmem],
        out_specs=[vmem, vmem],
        out_shape=[
            jax.ShapeDtypeStruct((NC, WIDE, HALF), f32),
            jax.ShapeDtypeStruct((NC, SMALL, HALF), f32),
        ],
        scratch_shapes=[
            pltpu.VMEM((WIDE, HALF), f32),
            pltpu.VMEM((WIDE, HALF), f32),
            pltpu.VMEM((NX - 1, ROWS_A, HALF), f32),
            pltpu.VMEM((ROWS_A, HALF), f32),
            pltpu.VMEM((NY - 1, ROWS_B, HALF), f32),
            pltpu.VMEM((ROWS_B, HALF), f32),
            pltpu.VMEM((NZ - 1, ROWS_Z, HALF), f32),
            pltpu.VMEM((SMALL, HALF), f32),
            pltpu.VMEM((NX - 1, SMALL, SLICE), f32),
            pltpu.VMEM((NY, SMALL, SLICE), f32),
            pltpu.VMEM((NZ, SMALL, SLICE), f32),
            pltpu.VMEM((SMALL, HALF), f32),
            pltpu.SemaphoreType.DMA((SENDS,)),
            pltpu.SemaphoreType.DMA((SENDS,)),
        ],
        compiler_params=pltpu.CompilerParams(collective_id=1, has_side_effects=True),
        name="gradients",
    )(big, small)


ROWS = PAIRS * OWN
CHUNK = ROWS // 4


def pair_table():
    tenors = (np.arange(MATS, dtype=np.float32) + np.float32(1.0)) / np.float32(MATS)
    offsets = np.arange(STRIKES, dtype=np.float32) - np.float32((STRIKES - 1) / 2.0)
    log_strike = np.float32(0.05) * offsets[None, :] * np.sqrt(tenors)[:, None]
    table = np.zeros((PAIRS, 128), np.float32)
    table[:, 4] = np.float32(4.0) * log_strike.reshape(PAIRS)
    table[:, 5] = np.repeat(tenors, STRIKES)
    table[:, 6] = 1.0
    return table


def network_kernel(
    sets_ref,
    table_ref,
    prices_ref,
    w_in_ref,
    b_in_ref,
    w_mid_ref,
    b_mid_ref,
    w_out_ref,
    b_out_ref,
    prices_out,
    big_ref,
    small_ref,
    feats,
    hid_in,
    slope_in,
    delta_mid,
    delta_in,
):
    f32, bf16 = jnp.float32, jnp.bfloat16
    pairs = CHUNK // OWN
    lane = lax.broadcasted_iota(jnp.int32, (OWN, 128), 1)
    factor = jnp.where(lane == 0, 4.0, jnp.where(lane == 3, 20.0, 1.0))
    scaled = (sets_ref[...] * factor)[None, :, :]
    prices = prices_ref[:, :PAIRS] / TOTAL_PATHS
    prices_out[...] = prices
    w_out = w_out_ref[...].astype(f32)
    g_out = jnp.zeros((8, WIDE), f32)
    g_bmid = jnp.zeros((8, WIDE), f32)
    g_bin = jnp.zeros((8, WIDE), f32)
    g_bout = jnp.zeros((8, 1), f32)
    for c in range(ROWS // CHUNK):
        rows = pl.ds(c * CHUNK, CHUNK)
        table = table_ref[pl.ds(c * pairs, pairs), :]
        x = (table[:, None, :] + scaled).reshape(CHUNK, 128).astype(bf16)
        feats[rows, :] = x
        raw = jnp.dot(x[:, :6], w_in_ref[...], preferred_element_type=f32) + b_in_ref[...]
        g = jax.nn.sigmoid(raw)
        hid = (raw * g).astype(bf16)
        hid_in[rows, :] = hid
        slope_in[rows, :] = g * (1.0 + raw * (1.0 - g))
        raw = jnp.dot(hid, w_mid_ref[...], preferred_element_type=f32) + b_mid_ref[...]
        g = jax.nn.sigmoid(raw)
        mid = (raw * g).astype(bf16).astype(f32)
        pred = jnp.sum(mid * w_out, axis=1, keepdims=True) + b_out_ref[0, 0]
        target = jnp.concatenate(
            [prices[:, k : k + 1] for k in range(c * pairs, (c + 1) * pairs)], axis=0
        )
        slope = (pred - target) * (1.0 / SETS)
        g_bout = g_bout + jnp.sum(slope.reshape(pairs, 8, 1), axis=0)
        g_out = g_out + jnp.sum((mid * slope).reshape(pairs, 8, WIDE), axis=0)
        delta = (slope * w_out * (g * (1.0 + raw * (1.0 - g)))).astype(bf16)
        delta_mid[rows, :] = delta
        g_bmid = g_bmid + jnp.sum(delta.astype(f32).reshape(pairs, 8, WIDE), axis=0)
        back = lax.dot_general(
            delta, w_mid_ref[...], (((1,), (1,)), ((), ())), preferred_element_type=f32
        )
        inner = (back * slope_in[rows, :]).astype(bf16)
        delta_in[rows, :] = inner
        g_bin = g_bin + jnp.sum(inner.astype(f32).reshape(pairs, 8, WIDE), axis=0)
    small_ref[pl.ds(0, 8), :] = lax.dot_general(
        feats[:, :8], delta_in[...], (((0,), (0,)), ((), ())), preferred_element_type=f32
    )
    small_ref[pl.ds(6, 1), :] = jnp.sum(g_bin, axis=0, keepdims=True)
    small_ref[pl.ds(7, 1), :] = jnp.sum(g_bmid, axis=0, keepdims=True)
    small_ref[pl.ds(8, 1), :] = jnp.sum(g_out, axis=0, keepdims=True)
    small_ref[pl.ds(9, 1), :] = jnp.broadcast_to(jnp.sum(g_bout, axis=0, keepdims=True), (1, WIDE))
    small_ref[pl.ds(10, 6), :] = jnp.zeros((6, WIDE), f32)
    big_ref[...] = lax.dot_general(
        hid_in[...], delta_mid[...], (((0,), (0,)), ((), ())), preferred_element_type=f32
    )


def network(sets, prices, w_in, b_in, w_mid, b_mid, w_out, b_out):
    f32, bf16 = jnp.float32, jnp.bfloat16
    vmem = pl.BlockSpec(memory_space=pltpu.VMEM)
    smem = pl.BlockSpec(memory_space=pltpu.SMEM)
    return pl.pallas_call(
        network_kernel,
        in_specs=[vmem] * 8 + [smem],
        out_specs=[vmem, vmem, vmem],
        out_shape=[
            jax.ShapeDtypeStruct((OWN, PAIRS), f32),
            jax.ShapeDtypeStruct((WIDE, WIDE), f32),
            jax.ShapeDtypeStruct((SMALL, WIDE), f32),
        ],
        scratch_shapes=[
            pltpu.VMEM((ROWS, 128), bf16),
            pltpu.VMEM((ROWS, WIDE), bf16),
            pltpu.VMEM((ROWS, WIDE), f32),
            pltpu.VMEM((ROWS, WIDE), bf16),
            pltpu.VMEM((ROWS, WIDE), bf16),
        ],
        name="network",
    )(
        sets,
        jnp.asarray(pair_table()),
        prices,
        w_in,
        b_in.reshape(1, WIDE),
        w_mid,
        b_mid.reshape(1, WIDE),
        w_out.reshape(1, WIDE),
        b_out.reshape(1, 1),
    )


def finish_kernel(
    big_ref, small_ref, w_in_out, b_in_out, w_mid_out, b_mid_out, w_out_out, b_out_out
):
    def factor(total, entries):
        return lax.rsqrt(total * (1.0 / entries) + EPSILON)

    def sumsq(value):
        return jnp.sum(jnp.sum(value * value, axis=1, keepdims=True), axis=0, keepdims=True)

    small = jnp.concatenate([small_ref[0], small_ref[1]], axis=1)
    g_bout = small[9:10, 0:1]
    s_mid = sumsq(small[7:8])
    for k in range(8):
        for c in range(NC):
            s_mid = s_mid + sumsq(big_ref[c, pl.ds(k * 128, 128), :])
    f_in = factor(sumsq(small[0:7]), 7 * WIDE)
    f_mid = factor(s_mid, (WIDE + 1) * WIDE)
    f_out = factor(sumsq(small[8:9]) + g_bout * g_bout, WIDE + 1)
    w_in_out[...] = small[0:6] * f_in
    b_in_out[...] = small[6:7] * f_in
    b_mid_out[...] = small[7:8] * f_mid
    w_out_out[...] = small[8:9] * f_out
    b_out_out[...] = g_bout * f_out
    for c in range(NC):
        w_mid_out[:, pl.ds(c * HALF, HALF)] = big_ref[c] * f_mid


def finish(big, small):
    f32 = jnp.float32
    vmem = pl.BlockSpec(memory_space=pltpu.VMEM)
    shapes = [(6, WIDE), (1, WIDE), (WIDE, WIDE), (1, WIDE), (1, WIDE), (1, 1)]
    w_in, b_in, w_mid, b_mid, w_out, b_out = pl.pallas_call(
        finish_kernel,
        in_specs=[vmem] * 2,
        out_specs=[vmem] * 6,
        out_shape=[jax.ShapeDtypeStruct(shape, f32) for shape in shapes],
        name="finish",
    )(big, small)
    return w_in, b_in.reshape(WIDE), w_mid, b_mid.reshape(WIDE), w_out.reshape(WIDE), b_out.reshape(1)


def on_device(params, increments, w_in, b_in, w_mid, b_mid, w_out, b_out):
    sums, sets = price_sums(params, increments)
    prices, big, small = network(sets, sums, w_in, b_in, w_mid, b_mid, w_out, b_out)
    return (prices, *finish(*sum_gradients(big, small)))


def solution(mesh):
    in_specs = (P(), P(None, None, "paths"), P(), P(), P(), P(), P(), P())
    out_specs = (P("paths", None), P(), P(), P(), P(), P(), P())
    return jax.shard_map(
        on_device, mesh=mesh, in_specs=in_specs, out_specs=out_specs, check_vma=False
    )
```

```python
import math

import jax
import jax.numpy as jnp
import numpy as np
from jax import lax
from jax.experimental import pallas as pl
from jax.experimental.pallas import tpu as pltpu
from jax.sharding import PartitionSpec as P

STEPS = 64
MATS = 8
STRIKES = 11
PAIRS = 88
EPSILON = 1e-06
LOG2E = 1.4426950408889634
NX, NY, NZ, NC = 4, 4, 8, 2
OWN = 8
BLOCK = NY * NZ * OWN
BLOCKS = NX * NC
SETS = 2048
TOTAL_PATHS = 32768
MESH = pl.DeviceIdType.MESH


def strike_values():
    return [
        [math.exp(0.05 * (j - 5) * math.sqrt((m + 1) / MATS)) for j in range(STRIKES)]
        for m in range(MATS)
    ]


def coords(index):
    core = index % NC
    z = (index // NC) % NZ
    y = (index // (NC * NZ)) % NY
    x = index // (NC * NZ * NY)
    return x, y, z, core


def device_at(x, y, z, core):
    return ((x * NY + y) * NZ + z) * NC + core


def lag_tables():
    lag = np.tile(np.arange(STEPS, dtype=np.float64), 2)
    table = np.zeros((8, 128), np.float32)
    table[0] = np.log2(np.maximum(lag, 1.0))
    table[1] = np.log2(np.maximum(lag - 1.0, 1.0))
    table[2] = np.log2(np.maximum(lag, 1.0) / STEPS)
    return table


def set_operands(sets, lag_ref, rows, ratio, scale):
    f32, bf16 = jnp.float32, jnp.bfloat16
    shape = (sets.shape[0], 128)
    hurst, vol, correl, forward = (
        jnp.broadcast_to(sets[:, k : k + 1], shape) for k in range(4)
    )
    lane = lax.broadcasted_iota(jnp.int32, shape, 1)
    upper = lane >= STEPS
    lag = jnp.where(upper, lane - STEPS, lane)
    expo = hurst + 0.5
    late = jnp.where(lag >= 2, jnp.exp2(expo * lag_ref[1:2, :]), 0.0)
    powers = jnp.exp2(expo * lag_ref[0:1, :]) - late
    front = jnp.sqrt(2.0 * hurst) * jnp.exp2(-6.0 * hurst) / expo
    kern = jnp.where(lag >= 1, powers * front, 0.0).astype(bf16).astype(f32)
    half = (0.5 * LOG2E) * vol
    weight = kern * half
    comp = (-0.5 * vol * half) * jnp.exp2((2.0 * hurst) * lag_ref[2:3, :])
    rest = 1.0 - correl * correl
    const = (0.5 * LOG2E) * jnp.log(forward * (1.0 / STEPS) / rest) - 1.0
    w_hi = weight.astype(bf16).astype(f32)
    c_hi = comp.astype(bf16).astype(f32)
    k_hi = const.astype(bf16).astype(f32)
    k_rest = const - k_hi
    k_lo = k_rest.astype(bf16).astype(f32)
    first = lag == 0
    kern_row = jnp.where(first, jnp.where(upper, k_lo, k_hi), jnp.where(upper, weight - w_hi, w_hi))
    comp_row = jnp.where(
        first, jnp.where(upper, 0.0, k_rest - k_lo), jnp.where(upper, comp - c_hi, c_hi)
    )
    rows[:, 0:128] = kern_row.astype(bf16)
    rows[:, 128:256] = comp_row.astype(bf16)
    ratio[...] = correl * lax.rsqrt(rest)
    scale[...] = (2.0 * LOG2E) * rest


def price_peers(x, y, z, core):
    mine = x * NC + core
    blocks = []
    for b in range(BLOCKS - 1):
        other = (mine + 1 + b) % BLOCKS
        blocks.append(device_at(other // NC, y, z, other % NC))
    along_y = [device_at(x, (y + d) % NY, z, core) for d in range(1, NY)]
    along_z = [device_at(x, y, (z + d) % NZ, core) for d in range(1, NZ)]
    return blocks, along_y, along_z


def prices_kernel(
    params_ref,
    lag_ref,
    inc_ref,
    out_ref,
    own_ref,
    sets,
    rows_ref,
    ratio_ref,
    scale_ref,
    noise,
    table,
    walk,
    part,
    sent,
    got,
    got_y,
    got_z,
    send_sem,
    got_sem,
    send_y,
    got_y_sem,
    send_z,
    got_z_sem,
):
    step = pl.program_id(0)
    x, y, z, core = coords(lax.axis_index("paths"))
    blocks, along_y, along_z = price_peers(x, y, z, core)

    @pl.when(step == 0)
    def _():
        barrier = pltpu.get_barrier_semaphore()
        for peer in blocks + along_y + along_z:
            pl.semaphore_signal(barrier, inc=1, device_id=(peer,), device_id_type=MESH)
        for k in range(NX * NY):
            some = params_ref[:, pl.ds(k * 128, 128)]
            some = jnp.concatenate([some, jnp.zeros((124, 128), jnp.float32)], axis=0).T
            sets[k // NY, pl.ds((k % NY) * NZ, NZ)] = some.reshape(NZ, NC, OWN, 128)
        own_ref[...] = sets[x, y * NZ + z, core]
        noise[0] = inc_ref[0].astype(jnp.float32)
        noise[1] = inc_ref[1].astype(jnp.float32)
        part[...] = jnp.zeros_like(part)
        row = lax.broadcasted_iota(jnp.int32, (STEPS, 128), 0)
        for j in range(STEPS):
            walk[pl.ds(STEPS - 1 - j, 1), :] = noise[0, pl.ds(j, 1), :]
        walk[pl.ds(STEPS, STEPS), :] = jnp.zeros((STEPS, 128), jnp.float32)
        one = jnp.ones((STEPS, 128), jnp.float32)
        for i in range(STEPS):
            past = walk[pl.ds(STEPS - 1 - i, STEPS), :]
            past = jnp.where(row == 0, one, past).astype(jnp.bfloat16)
            pick = jnp.where(row == i, 1.0, 0.0)
            hot = jnp.where(row == 0, one, pick).astype(jnp.bfloat16)
            hot_lo = jnp.where(row == 0, 0.0, pick).astype(jnp.bfloat16)
            cols = pl.ds((i % 2) * 128, 128)
            table[i // 2, pl.ds(0, STEPS), cols] = past
            table[i // 2, pl.ds(STEPS, STEPS), cols] = past
            table[i // 2, pl.ds(2 * STEPS, STEPS), cols] = hot
            table[i // 2, pl.ds(3 * STEPS, STEPS), cols] = hot_lo

    strikes = strike_values()
    other = (x * NC + core + 1 + step) % BLOCKS
    block = sets[other // NC, :, other % NC].reshape(BLOCK, 128)
    set_operands(block, lag_ref, rows_ref, ratio_ref, scale_ref)
    walk[...] = jnp.zeros_like(walk)
    for m in range(MATS):
        for q in range(4):
            pair = jnp.dot(
                rows_ref[...], table[m * 4 + q], preferred_element_type=jnp.float32
            )
            for h in range(2):
                i = m * 8 + q * 2 + h
                vol = jnp.exp2(pair[:, h * 128 : (h + 1) * 128])
                shock = ratio_ref[...] * noise[0, pl.ds(i, 1), :] + noise[1, pl.ds(i, 1), :]
                walk[...] += vol * (shock - vol)
        spot = jnp.exp2((walk[...] * scale_ref[...]).T)
        for j in range(STRIKES):
            k = strikes[m][j]
            top = jnp.sum(jnp.maximum(spot, k).reshape(16, 8, BLOCK), axis=0)
            part[pl.ds(m * STRIKES + j, 1), :] = jnp.sum(top - 16.0 * k, axis=0, keepdims=True)
    sent[step] = part[...].T

    @pl.when(step == 0)
    def _():
        pl.semaphore_wait(pltpu.get_barrier_semaphore(), len(blocks + along_y + along_z))

    def block_copy(b):
        other = (x * NC + core + 1 + b) % BLOCKS
        return pltpu.make_async_remote_copy(
            src_ref=sent.at[b],
            dst_ref=got.at[b],
            send_sem=send_sem.at[b],
            recv_sem=got_sem.at[b],
            device_id=(device_at(other // NC, y, z, other % NC),),
            device_id_type=MESH,
        )

    @pl.when(step < BLOCKS - 1)
    def _():
        block_copy(step).start()

    @pl.when(step == BLOCKS - 1)
    def _():
        total = sent.at[BLOCKS - 1]
        for b in range(BLOCKS - 1):
            block_copy(b).wait_recv()
            total[...] += got[b]
        rows_y = NZ * OWN

        def y_rows(d):
            return pl.ds(pl.multiple_of(((y + d) % NY) * rows_y, rows_y), rows_y)

        copies = []
        for d in range(1, NY):
            copy = pltpu.make_async_remote_copy(
                src_ref=total.at[y_rows(d), :],
                dst_ref=got_y.at[d],
                send_sem=send_y.at[d],
                recv_sem=got_y_sem.at[d],
                device_id=(along_y[d - 1],),
                device_id_type=MESH,
            )
            copy.start()
            copies.append(copy)
        own = total[y_rows(0), :]
        for d in range(1, NY):
            copies[d - 1].wait_recv()
            own = own + got_y[d]
        got_y[0] = own

        def z_rows(d):
            return pl.ds(pl.multiple_of(((z + d) % NZ) * OWN, OWN), OWN)

        for d in range(1, NZ):
            copy = pltpu.make_async_remote_copy(
                src_ref=got_y.at[0, z_rows(d), :],
                dst_ref=got_z.at[d],
                send_sem=send_z.at[d],
                recv_sem=got_z_sem.at[d],
                device_id=(along_z[d - 1],),
                device_id_type=MESH,
            )
            copy.start()
            copies.append(copy)
        final = got_y[0, z_rows(0), :]
        for d in range(1, NZ):
            copies[NY - 1 + d - 1].wait_recv()
            final = final + got_z[d]
        out_ref[...] = final
        for b in range(BLOCKS - 1):
            block_copy(b).wait_send()
        for copy in copies:
            copy.wait_send()


def price_sums(params, increments):
    f32 = jnp.float32
    own = jax.ShapeDtypeStruct((OWN, 128), f32)
    return pl.pallas_call(
        prices_kernel,
        grid=(BLOCKS,),
        in_specs=[
            pl.BlockSpec((4, BLOCKS * BLOCK), lambda b: (0, 0)),
            pl.BlockSpec((8, 128), lambda b: (0, 0)),
            pl.BlockSpec((2, STEPS, 128), lambda b: (0, 0, 0)),
        ],
        out_specs=[pl.BlockSpec((OWN, 128), lambda b: (0, 0))] * 2,
        out_shape=[own, own],
        scratch_shapes=[
            pltpu.VMEM((NX, NY * NZ, NC, OWN, 128), f32),
            pltpu.VMEM((BLOCK, 256), jnp.bfloat16),
            pltpu.VMEM((BLOCK, 128), f32),
            pltpu.VMEM((BLOCK, 128), f32),
            pltpu.VMEM((2, STEPS, 128), f32),
            pltpu.VMEM((STEPS // 2, 256, 256), jnp.bfloat16),
            pltpu.VMEM((BLOCK, 128), f32),
            pltpu.VMEM((128, BLOCK), f32),
            pltpu.VMEM((BLOCKS, BLOCK, 128), f32),
            pltpu.VMEM((BLOCKS - 1, BLOCK, 128), f32),
            pltpu.VMEM((NY, NZ * OWN, 128), f32),
            pltpu.VMEM((NZ, OWN, 128), f32),
            pltpu.SemaphoreType.DMA((BLOCKS,)),
            pltpu.SemaphoreType.DMA((BLOCKS,)),
            pltpu.SemaphoreType.DMA((NY,)),
            pltpu.SemaphoreType.DMA((NY,)),
            pltpu.SemaphoreType.DMA((NZ,)),
            pltpu.SemaphoreType.DMA((NZ,)),
        ],
        compiler_params=pltpu.CompilerParams(collective_id=0, has_side_effects=True),
        name="prices",
    )(params.T, jnp.asarray(lag_tables()), increments)


WIDE = 1024
HALF = WIDE // NC
ROWS_A = WIDE // NX
ROWS_B = ROWS_A // NY
ROWS_Z = ROWS_B // NZ
SMALL = 16
SLICE = HALF // NX


ROWS = PAIRS * OWN
CHUNK = ROWS // 4
DEPTH = 768


def pair_table():
    tenors = (np.arange(MATS, dtype=np.float32) + np.float32(1.0)) / np.float32(MATS)
    offsets = np.arange(STRIKES, dtype=np.float32) - np.float32((STRIKES - 1) / 2.0)
    log_strike = np.float32(0.05) * offsets[None, :] * np.sqrt(tenors)[:, None]
    table = np.zeros((PAIRS, 128), np.float32)
    table[:, 4] = np.float32(4.0) * log_strike.reshape(PAIRS)
    table[:, 5] = np.repeat(tenors, STRIKES)
    table[:, 6] = 1.0
    return table


def network_part(
    sets_ref,
    table_ref,
    prices_ref,
    w_in_ref,
    b_in_ref,
    w_mid_ref,
    b_mid_ref,
    w_out_ref,
    b_out_ref,
    prices_out,
    small_ref,
    feats,
    hid_in,
    slope_in,
    delta_mid,
    delta_in,
    hid_turn,
):
    f32, bf16 = jnp.float32, jnp.bfloat16
    pairs = CHUNK // OWN
    lane = lax.broadcasted_iota(jnp.int32, (OWN, 128), 1)
    factor = jnp.where(lane == 0, 4.0, jnp.where(lane == 3, 20.0, 1.0))
    scaled = (sets_ref[...] * factor)[None, :, :]
    prices = prices_ref[:, :PAIRS] / TOTAL_PATHS
    prices_out[...] = prices
    w_out = w_out_ref[...].astype(f32)
    g_out = jnp.zeros((8, WIDE), f32)
    g_bmid = jnp.zeros((8, WIDE), f32)
    g_bin = jnp.zeros((8, WIDE), f32)
    g_bout = jnp.zeros((8, 1), f32)
    hid_in[pl.ds(ROWS, DEPTH - ROWS), :] = jnp.zeros((DEPTH - ROWS, WIDE), bf16)
    delta_mid[pl.ds(ROWS, DEPTH - ROWS), :] = jnp.zeros((DEPTH - ROWS, WIDE), bf16)
    for c in range(ROWS // CHUNK):
        rows = pl.ds(c * CHUNK, CHUNK)
        table = table_ref[pl.ds(c * pairs, pairs), :]
        x = (table[:, None, :] + scaled).reshape(CHUNK, 128).astype(bf16)
        feats[rows, :] = x
        raw = jnp.dot(x[:, :6], w_in_ref[...], preferred_element_type=f32) + b_in_ref[...]
        g = jax.nn.sigmoid(raw)
        hid = (raw * g).astype(bf16)
        hid_in[rows, :] = hid
        slope_in[rows, :] = g * (1.0 + raw * (1.0 - g))
        raw = jnp.dot(hid, w_mid_ref[...], preferred_element_type=f32) + b_mid_ref[...]
        g = jax.nn.sigmoid(raw)
        mid = (raw * g).astype(bf16).astype(f32)
        pred = jnp.sum(mid * w_out, axis=1, keepdims=True) + b_out_ref[0, 0]
        target = jnp.concatenate(
            [prices[:, k : k + 1] for k in range(c * pairs, (c + 1) * pairs)], axis=0
        )
        slope = (pred - target) * (1.0 / SETS)
        g_bout = g_bout + jnp.sum(slope.reshape(pairs, 8, 1), axis=0)
        g_out = g_out + jnp.sum((mid * slope).reshape(pairs, 8, WIDE), axis=0)
        delta = (slope * w_out * (g * (1.0 + raw * (1.0 - g)))).astype(bf16)
        delta_mid[rows, :] = delta
        g_bmid = g_bmid + jnp.sum(delta.astype(f32).reshape(pairs, 8, WIDE), axis=0)
        back = lax.dot_general(
            delta, w_mid_ref[...], (((1,), (1,)), ((), ())), preferred_element_type=f32
        )
        inner = (back * slope_in[rows, :]).astype(bf16)
        delta_in[rows, :] = inner
        g_bin = g_bin + jnp.sum(inner.astype(f32).reshape(pairs, 8, WIDE), axis=0)
    small_ref[pl.ds(0, 8), :] = lax.dot_general(
        feats[:, :8], delta_in[...], (((0,), (0,)), ((), ())), preferred_element_type=f32
    )
    small_ref[pl.ds(6, 1), :] = jnp.sum(g_bin, axis=0, keepdims=True)
    small_ref[pl.ds(7, 1), :] = jnp.sum(g_bmid, axis=0, keepdims=True)
    small_ref[pl.ds(8, 1), :] = jnp.sum(g_out, axis=0, keepdims=True)
    small_ref[pl.ds(9, 1), :] = jnp.broadcast_to(jnp.sum(g_bout, axis=0, keepdims=True), (1, WIDE))
    small_ref[pl.ds(10, 6), :] = jnp.zeros((6, WIDE), f32)
    hid_turn[...] = hid_in[...].T


LATER = (1, 2, 3, 0)
SENDS = 84


def train_kernel(
    sets_ref,
    table_ref,
    prices_ref,
    w_in_ref,
    b_in_ref,
    w_mid_ref,
    b_mid_ref,
    w_out_ref,
    b_out_ref,
    prices_out,
    big_out,
    small_out,
    small,
    feats,
    hid_in,
    slope_in,
    delta_mid,
    delta_in,
    hid_turn,
    other,
    got_c,
    work,
    got_a,
    mid,
    got_b,
    low,
    got_z,
    s_got_c,
    s_got_a,
    s_b,
    s_z,
    s_sum,
    send_sem,
    recv_sem,
):
    x, y, z, core = coords(lax.axis_index("paths"))
    a = x * (1 - core) + y * core
    b = y * (1 - core) + x * core

    def at(aa, bb, zz):
        return device_at(aa * (1 - core) + bb * core, bb * (1 - core) + aa * core, zz, core)

    partner = device_at(x, y, z, 1 - core)
    along_a = [at((a + d) % NX, b, z) for d in range(1, NX)]
    along_b = [at(a, (b + d) % NY, z) for d in range(1, NY)]
    along_z = [at(a, b, (z + d) % NZ) for d in range(1, NZ)]
    peers = [partner] + along_a + along_b + along_z
    barrier = pltpu.get_barrier_semaphore()
    for peer in peers:
        pl.semaphore_signal(barrier, inc=1, device_id=(peer,), device_id_type=MESH)

    network_part(
        sets_ref,
        table_ref,
        prices_ref,
        w_in_ref,
        b_in_ref,
        w_mid_ref,
        b_mid_ref,
        w_out_ref,
        b_out_ref,
        prices_out,
        small,
        feats,
        hid_in,
        slope_in,
        delta_mid,
        delta_in,
        hid_turn,
    )
    pl.semaphore_wait(barrier, len(peers))

    count = [0]
    started = []

    def send(src, dst, peer):
        k = count[0]
        count[0] += 1
        copy = pltpu.make_async_remote_copy(
            src_ref=src,
            dst_ref=dst,
            send_sem=send_sem.at[k],
            recv_sem=recv_sem.at[k],
            device_id=(peer,),
            device_id_type=MESH,
        )
        copy.start()
        started.append(copy)
        return copy

    def part(index, size):
        return pl.ds(pl.multiple_of(index * size, size), size)

    def rows_of(aa, bb):
        return part((aa % NX) * NY + bb % NY, ROWS_B)

    def product(first, second, e, cols):
        left = jnp.concatenate(
            [hid_turn[rows_of(first + d, second + e), :] for d in range(NX)], axis=0
        )
        out = jnp.dot(left, delta_mid[:, cols], preferred_element_type=jnp.float32)
        return out.reshape(NX, ROWS_B, HALF)

    own_cols, other_cols = part(core, HALF), part(1 - core, HALF)
    little = send(small.at[:, other_cols], s_got_c, partner)
    pair = {}
    for e in LATER:
        other[e] = product(b, a, e, other_cols)
        pair[e] = send(other.at[e], got_c.at[e], partner)
    little.wait_recv()
    s_got_c[...] += small[:, own_cols]
    littles = []
    for d in range(1, NX):
        littles.append(
            send(s_got_c.at[:, part((a + d) % NX, SLICE)], s_got_a.at[d - 1], along_a[d - 1])
        )
    steps = {}
    for e in LATER:
        mine = product(a, b, e, own_cols)
        pair[e].wait_recv()
        work[e] = mine + got_c[e]
        steps[e] = [
            send(work.at[e, d], got_a.at[e, d - 1], along_a[d - 1]) for d in range(1, NX)
        ]
    for copy in littles:
        copy.wait_recv()
    s_b[b] = s_got_c[:, part(a, SLICE)] + s_got_a[0] + s_got_a[1] + s_got_a[2]
    littles = [send(s_b.at[b], s_b.at[b], peer) for peer in along_b]
    across = []
    for e in LATER:
        for copy in steps[e]:
            copy.wait_recv()
        mid[e] = work[e, 0] + got_a[e, 0] + got_a[e, 1] + got_a[e, 2]
        if e > 0:
            across.append(send(mid.at[e], got_b.at[e - 1], along_b[e - 1]))
    for copy in littles:
        copy.wait_recv()
    s_z[z] = (s_b[0] + s_b[1]) + (s_b[2] + s_b[3])
    littles = [send(s_z.at[z], s_z.at[z], peer) for peer in along_z]
    for copy in across:
        copy.wait_recv()
    low[...] = mid[0] + got_b[0] + got_b[1] + got_b[2]
    deep = [
        send(low.at[part((z + d) % NZ, ROWS_Z), :], got_z.at[d - 1], along_z[d - 1])
        for d in range(1, NZ)
    ]
    for copy in littles:
        copy.wait_recv()
    s_all = ((s_z[0] + s_z[1]) + (s_z[2] + s_z[3])) + ((s_z[4] + s_z[5]) + (s_z[6] + s_z[7]))
    s_sum[:, part(a, SLICE)] = s_all
    littles = [
        send(s_sum.at[:, part(a, SLICE)], s_sum.at[:, part(a, SLICE)], peer) for peer in along_a
    ]
    final = low[part(z, ROWS_Z), :]
    for d in range(1, NZ):
        deep[d - 1].wait_recv()
        final = final + got_z[d - 1]

    half_out = big_out.at[core]
    mine = part((a * NY + b) * NZ + z, ROWS_Z)
    half_out[mine, :] = final
    deep = [send(half_out.at[mine, :], half_out.at[mine, :], peer) for peer in along_z]
    for copy in littles:
        copy.wait_recv()
    small_out[core] = s_sum[...]
    little = send(small_out.at[core], small_out.at[core], partner)
    for copy in deep:
        copy.wait_recv()

    def spread(rows, targets):
        return [send(half_out.at[rows, :], half_out.at[rows, :], peer) for peer in targets]

    across = spread(rows_of(a, b), along_b)
    steps = [spread(rows_of(a, b), along_a)]
    pairs = spread(rows_of(a, b), [partner])
    for d in range(1, NY):
        across[d - 1].wait_recv()
        rows = rows_of(a, b + NY - d)
        steps.append(spread(rows, along_a))
        pairs += spread(rows, [partner])
    for e in range(NY):
        for d in range(1, NX):
            steps[e][d - 1].wait_recv()
            pairs += spread(rows_of(a + NX - d, b + NY - e), [partner])
    little.wait_recv()
    for copy in pairs:
        copy.wait_recv()
    for copy in started:
        copy.wait_send()


def train(sets, sums, w_in, b_in, w_mid, b_mid, w_out, b_out):
    f32, bf16 = jnp.float32, jnp.bfloat16
    vmem = pl.BlockSpec(memory_space=pltpu.VMEM)
    smem = pl.BlockSpec(memory_space=pltpu.SMEM)
    return pl.pallas_call(
        train_kernel,
        in_specs=[vmem] * 8 + [smem],
        out_specs=[vmem, vmem, vmem],
        out_shape=[
            jax.ShapeDtypeStruct((OWN, PAIRS), f32),
            jax.ShapeDtypeStruct((NC, WIDE, HALF), f32),
            jax.ShapeDtypeStruct((NC, SMALL, HALF), f32),
        ],
        scratch_shapes=[
            pltpu.VMEM((SMALL, WIDE), f32),
            pltpu.VMEM((ROWS, 128), bf16),
            pltpu.VMEM((DEPTH, WIDE), bf16),
            pltpu.VMEM((ROWS, WIDE), f32),
            pltpu.VMEM((DEPTH, WIDE), bf16),
            pltpu.VMEM((ROWS, WIDE), bf16),
            pltpu.VMEM((WIDE, DEPTH), bf16),
            pltpu.VMEM((NY, NX, ROWS_B, HALF), f32),
            pltpu.VMEM((NY, NX, ROWS_B, HALF), f32),
            pltpu.VMEM((NY, NX, ROWS_B, HALF), f32),
            pltpu.VMEM((NY, NX - 1, ROWS_B, HALF), f32),
            pltpu.VMEM((NY, ROWS_B, HALF), f32),
            pltpu.VMEM((NY - 1, ROWS_B, HALF), f32),
            pltpu.VMEM((ROWS_B, HALF), f32),
            pltpu.VMEM((NZ - 1, ROWS_Z, HALF), f32),
            pltpu.VMEM((SMALL, HALF), f32),
            pltpu.VMEM((NX - 1, SMALL, SLICE), f32),
            pltpu.VMEM((NY, SMALL, SLICE), f32),
            pltpu.VMEM((NZ, SMALL, SLICE), f32),
            pltpu.VMEM((SMALL, HALF), f32),
            pltpu.SemaphoreType.DMA((SENDS,)),
            pltpu.SemaphoreType.DMA((SENDS,)),
        ],
        compiler_params=pltpu.CompilerParams(collective_id=1, has_side_effects=True),
        name="train",
    )(
        sets,
        jnp.asarray(pair_table()),
        sums,
        w_in,
        b_in.reshape(1, WIDE),
        w_mid,
        b_mid.reshape(1, WIDE),
        w_out.reshape(1, WIDE),
        b_out.reshape(1, 1),
    )


def finish_kernel(
    big_ref, small_ref, w_in_out, b_in_out, w_mid_out, b_mid_out, w_out_out, b_out_out
):
    def factor(total, entries):
        return lax.rsqrt(total * (1.0 / entries) + EPSILON)

    def sumsq(value):
        return jnp.sum(jnp.sum(value * value, axis=1, keepdims=True), axis=0, keepdims=True)

    small = jnp.concatenate([small_ref[0], small_ref[1]], axis=1)
    g_bout = small[9:10, 0:1]
    s_mid = sumsq(small[7:8])
    for k in range(8):
        for c in range(NC):
            s_mid = s_mid + sumsq(big_ref[c, pl.ds(k * 128, 128), :])
    f_in = factor(sumsq(small[0:7]), 7 * WIDE)
    f_mid = factor(s_mid, (WIDE + 1) * WIDE)
    f_out = factor(sumsq(small[8:9]) + g_bout * g_bout, WIDE + 1)
    w_in_out[...] = small[0:6] * f_in
    b_in_out[...] = small[6:7] * f_in
    b_mid_out[...] = small[7:8] * f_mid
    w_out_out[...] = small[8:9] * f_out
    b_out_out[...] = g_bout * f_out
    for c in range(NC):
        w_mid_out[:, pl.ds(c * HALF, HALF)] = big_ref[c] * f_mid


def finish(big, small):
    f32 = jnp.float32
    vmem = pl.BlockSpec(memory_space=pltpu.VMEM)
    shapes = [(6, WIDE), (1, WIDE), (WIDE, WIDE), (1, WIDE), (1, WIDE), (1, 1)]
    w_in, b_in, w_mid, b_mid, w_out, b_out = pl.pallas_call(
        finish_kernel,
        in_specs=[vmem] * 2,
        out_specs=[vmem] * 6,
        out_shape=[jax.ShapeDtypeStruct(shape, f32) for shape in shapes],
        name="finish",
    )(big, small)
    return w_in, b_in.reshape(WIDE), w_mid, b_mid.reshape(WIDE), w_out.reshape(WIDE), b_out.reshape(1)


def on_device(params, increments, w_in, b_in, w_mid, b_mid, w_out, b_out):
    sums, sets = price_sums(params, increments)
    prices, big, small = train(sets, sums, w_in, b_in, w_mid, b_mid, w_out, b_out)
    return (prices, *finish(big, small))


def solution(mesh):
    in_specs = (P(), P(None, None, "paths"), P(), P(), P(), P(), P(), P())
    out_specs = (P("paths", None), P(), P(), P(), P(), P(), P())
    return jax.shard_map(
        on_device, mesh=mesh, in_specs=in_specs, out_specs=out_specs, check_vma=False
    )
```

```python
import math

import jax
import jax.numpy as jnp
import numpy as np
from jax import lax
from jax.experimental import pallas as pl
from jax.experimental.pallas import tpu as pltpu
from jax.sharding import PartitionSpec as P

STEPS = 64
MATS = 8
STRIKES = 11
PAIRS = 88
EPSILON = 1e-06
LOG2E = 1.4426950408889634
NX, NY, NZ, NC = 4, 4, 8, 2
OWN = 8
BLOCK = NY * NZ * OWN
BLOCKS = NX * NC
SETS = 2048
TOTAL_PATHS = 32768
MESH = pl.DeviceIdType.MESH


def strike_values():
    return [
        [math.exp(0.05 * (j - 5) * math.sqrt((m + 1) / MATS)) for j in range(STRIKES)]
        for m in range(MATS)
    ]


def coords(index):
    core = index % NC
    z = (index // NC) % NZ
    y = (index // (NC * NZ)) % NY
    x = index // (NC * NZ * NY)
    return x, y, z, core


def device_at(x, y, z, core):
    return ((x * NY + y) * NZ + z) * NC + core


def lag_tables():
    lag = np.tile(np.arange(STEPS, dtype=np.float64), 2)
    table = np.zeros((8, 128), np.float32)
    table[0] = np.log2(np.maximum(lag, 1.0))
    table[1] = np.log2(np.maximum(lag - 1.0, 1.0))
    table[2] = np.log2(np.maximum(lag, 1.0) / STEPS)
    return table


def set_operands(sets, lag_ref, rows, ratio, scale):
    f32, bf16 = jnp.float32, jnp.bfloat16
    shape = (sets.shape[0], 128)
    hurst, vol, correl, forward = (
        jnp.broadcast_to(sets[:, k : k + 1], shape) for k in range(4)
    )
    lane = lax.broadcasted_iota(jnp.int32, shape, 1)
    upper = lane >= STEPS
    lag = jnp.where(upper, lane - STEPS, lane)
    expo = hurst + 0.5
    late = jnp.where(lag >= 2, jnp.exp2(expo * lag_ref[1:2, :]), 0.0)
    powers = jnp.exp2(expo * lag_ref[0:1, :]) - late
    front = jnp.sqrt(2.0 * hurst) * jnp.exp2(-6.0 * hurst) / expo
    kern = jnp.where(lag >= 1, powers * front, 0.0).astype(bf16).astype(f32)
    half = (0.5 * LOG2E) * vol
    weight = kern * half
    comp = (-0.5 * vol * half) * jnp.exp2((2.0 * hurst) * lag_ref[2:3, :])
    rest = 1.0 - correl * correl
    const = (0.5 * LOG2E) * jnp.log(forward * (1.0 / STEPS) / rest) - 1.0
    w_hi = weight.astype(bf16).astype(f32)
    c_hi = comp.astype(bf16).astype(f32)
    k_hi = const.astype(bf16).astype(f32)
    k_rest = const - k_hi
    k_lo = k_rest.astype(bf16).astype(f32)
    first = lag == 0
    kern_row = jnp.where(first, jnp.where(upper, k_lo, k_hi), jnp.where(upper, weight - w_hi, w_hi))
    comp_row = jnp.where(
        first, jnp.where(upper, 0.0, k_rest - k_lo), jnp.where(upper, comp - c_hi, c_hi)
    )
    rows[:, 0:128] = kern_row.astype(bf16)
    rows[:, 128:256] = comp_row.astype(bf16)
    ratio[...] = correl * lax.rsqrt(rest)
    scale[...] = (2.0 * LOG2E) * rest


def price_peers(x, y, z, core):
    mine = x * NC + core
    blocks = []
    for b in range(BLOCKS - 1):
        other = (mine + 1 + b) % BLOCKS
        blocks.append(device_at(other // NC, y, z, other % NC))
    along_y = [device_at(x, (y + d) % NY, z, core) for d in range(1, NY)]
    along_z = [device_at(x, y, (z + d) % NZ, core) for d in range(1, NZ)]
    return blocks, along_y, along_z


def prices_kernel(
    params_ref,
    lag_ref,
    inc_ref,
    out_ref,
    own_ref,
    sets,
    rows_ref,
    ratio_ref,
    scale_ref,
    noise,
    table,
    walk,
    part,
    sent,
    got,
    got_y,
    got_z,
    send_sem,
    got_sem,
    send_y,
    got_y_sem,
    send_z,
    got_z_sem,
):
    step = pl.program_id(0)
    x, y, z, core = coords(lax.axis_index("paths"))
    blocks, along_y, along_z = price_peers(x, y, z, core)

    @pl.when(step == 0)
    def _():
        barrier = pltpu.get_barrier_semaphore()
        for peer in blocks + along_y + along_z:
            pl.semaphore_signal(barrier, inc=1, device_id=(peer,), device_id_type=MESH)
        for k in range(NX * NY):
            some = params_ref[:, pl.ds(k * 128, 128)]
            some = jnp.concatenate([some, jnp.zeros((124, 128), jnp.float32)], axis=0).T
            sets[k // NY, pl.ds((k % NY) * NZ, NZ)] = some.reshape(NZ, NC, OWN, 128)
        own_ref[...] = sets[x, y * NZ + z, core]
        noise[0] = inc_ref[0].astype(jnp.float32)
        noise[1] = inc_ref[1].astype(jnp.float32)
        part[...] = jnp.zeros_like(part)
        row = lax.broadcasted_iota(jnp.int32, (STEPS, 128), 0)
        for j in range(STEPS):
            walk[pl.ds(STEPS - 1 - j, 1), :] = noise[0, pl.ds(j, 1), :]
        walk[pl.ds(STEPS, STEPS), :] = jnp.zeros((STEPS, 128), jnp.float32)
        one = jnp.ones((STEPS, 128), jnp.float32)
        for i in range(STEPS):
            past = walk[pl.ds(STEPS - 1 - i, STEPS), :]
            past = jnp.where(row == 0, one, past).astype(jnp.bfloat16)
            pick = jnp.where(row == i, 1.0, 0.0)
            hot = jnp.where(row == 0, one, pick).astype(jnp.bfloat16)
            hot_lo = jnp.where(row == 0, 0.0, pick).astype(jnp.bfloat16)
            cols = pl.ds((i % 2) * 128, 128)
            table[i // 2, pl.ds(0, STEPS), cols] = past
            table[i // 2, pl.ds(STEPS, STEPS), cols] = past
            table[i // 2, pl.ds(2 * STEPS, STEPS), cols] = hot
            table[i // 2, pl.ds(3 * STEPS, STEPS), cols] = hot_lo

    strikes = strike_values()
    other = (x * NC + core + 1 + step) % BLOCKS
    block = sets[other // NC, :, other % NC].reshape(BLOCK, 128)
    set_operands(block, lag_ref, rows_ref, ratio_ref, scale_ref)
    walk[...] = jnp.zeros_like(walk)
    for m in range(MATS):
        for q in range(4):
            pair = jnp.dot(
                rows_ref[...], table[m * 4 + q], preferred_element_type=jnp.float32
            )
            for h in range(2):
                i = m * 8 + q * 2 + h
                vol = jnp.exp2(pair[:, h * 128 : (h + 1) * 128])
                shock = ratio_ref[...] * noise[0, pl.ds(i, 1), :] + noise[1, pl.ds(i, 1), :]
                walk[...] += vol * (shock - vol)
        spot = jnp.exp2((walk[...] * scale_ref[...]).T)
        for j in range(STRIKES):
            k = strikes[m][j]
            top = jnp.sum(jnp.maximum(spot, k).reshape(16, 8, BLOCK), axis=0)
            part[pl.ds(m * STRIKES + j, 1), :] = jnp.sum(top - 16.0 * k, axis=0, keepdims=True)
    sent[step] = part[...].T

    @pl.when(step == 0)
    def _():
        pl.semaphore_wait(pltpu.get_barrier_semaphore(), len(blocks + along_y + along_z))

    def block_copy(b):
        other = (x * NC + core + 1 + b) % BLOCKS
        return pltpu.make_async_remote_copy(
            src_ref=sent.at[b],
            dst_ref=got.at[b],
            send_sem=send_sem.at[b],
            recv_sem=got_sem.at[b],
            device_id=(device_at(other // NC, y, z, other % NC),),
            device_id_type=MESH,
        )

    @pl.when(step < BLOCKS - 1)
    def _():
        block_copy(step).start()

    @pl.when(step == BLOCKS - 1)
    def _():
        total = sent.at[BLOCKS - 1]
        for b in range(BLOCKS - 1):
            block_copy(b).wait_recv()
            total[...] += got[b]
        rows_y = NZ * OWN

        def y_rows(d):
            return pl.ds(pl.multiple_of(((y + d) % NY) * rows_y, rows_y), rows_y)

        copies = []
        for d in range(1, NY):
            copy = pltpu.make_async_remote_copy(
                src_ref=total.at[y_rows(d), :],
                dst_ref=got_y.at[d],
                send_sem=send_y.at[d],
                recv_sem=got_y_sem.at[d],
                device_id=(along_y[d - 1],),
                device_id_type=MESH,
            )
            copy.start()
            copies.append(copy)
        own = total[y_rows(0), :]
        for d in range(1, NY):
            copies[d - 1].wait_recv()
            own = own + got_y[d]
        got_y[0] = own

        def z_rows(d):
            return pl.ds(pl.multiple_of(((z + d) % NZ) * OWN, OWN), OWN)

        for d in range(1, NZ):
            copy = pltpu.make_async_remote_copy(
                src_ref=got_y.at[0, z_rows(d), :],
                dst_ref=got_z.at[d],
                send_sem=send_z.at[d],
                recv_sem=got_z_sem.at[d],
                device_id=(along_z[d - 1],),
                device_id_type=MESH,
            )
            copy.start()
            copies.append(copy)
        final = got_y[0, z_rows(0), :]
        for d in range(1, NZ):
            copies[NY - 1 + d - 1].wait_recv()
            final = final + got_z[d]
        out_ref[...] = final
        for b in range(BLOCKS - 1):
            block_copy(b).wait_send()
        for copy in copies:
            copy.wait_send()


def price_sums(params, increments):
    f32 = jnp.float32
    own = jax.ShapeDtypeStruct((OWN, 128), f32)
    return pl.pallas_call(
        prices_kernel,
        grid=(BLOCKS,),
        in_specs=[
            pl.BlockSpec((4, BLOCKS * BLOCK), lambda b: (0, 0)),
            pl.BlockSpec((8, 128), lambda b: (0, 0)),
            pl.BlockSpec((2, STEPS, 128), lambda b: (0, 0, 0)),
        ],
        out_specs=[pl.BlockSpec((OWN, 128), lambda b: (0, 0))] * 2,
        out_shape=[own, own],
        scratch_shapes=[
            pltpu.VMEM((NX, NY * NZ, NC, OWN, 128), f32),
            pltpu.VMEM((BLOCK, 256), jnp.bfloat16),
            pltpu.VMEM((BLOCK, 128), f32),
            pltpu.VMEM((BLOCK, 128), f32),
            pltpu.VMEM((2, STEPS, 128), f32),
            pltpu.VMEM((STEPS // 2, 256, 256), jnp.bfloat16),
            pltpu.VMEM((BLOCK, 128), f32),
            pltpu.VMEM((128, BLOCK), f32),
            pltpu.VMEM((BLOCKS, BLOCK, 128), f32),
            pltpu.VMEM((BLOCKS - 1, BLOCK, 128), f32),
            pltpu.VMEM((NY, NZ * OWN, 128), f32),
            pltpu.VMEM((NZ, OWN, 128), f32),
            pltpu.SemaphoreType.DMA((BLOCKS,)),
            pltpu.SemaphoreType.DMA((BLOCKS,)),
            pltpu.SemaphoreType.DMA((NY,)),
            pltpu.SemaphoreType.DMA((NY,)),
            pltpu.SemaphoreType.DMA((NZ,)),
            pltpu.SemaphoreType.DMA((NZ,)),
        ],
        compiler_params=pltpu.CompilerParams(collective_id=0, has_side_effects=True),
        name="prices",
    )(params.T, jnp.asarray(lag_tables()), increments)


WIDE = 1024
HALF = WIDE // NC
ROWS_A = WIDE // NX
ROWS_B = ROWS_A // NY
ROWS_Z = ROWS_B // NZ
SMALL = 16
SLICE = HALF // NX


ROWS = PAIRS * OWN
CHUNK = ROWS // 4
DEPTH = 768


def pair_table():
    tenors = (np.arange(MATS, dtype=np.float32) + np.float32(1.0)) / np.float32(MATS)
    offsets = np.arange(STRIKES, dtype=np.float32) - np.float32((STRIKES - 1) / 2.0)
    log_strike = np.float32(0.05) * offsets[None, :] * np.sqrt(tenors)[:, None]
    table = np.zeros((PAIRS, 128), np.float32)
    table[:, 4] = np.float32(4.0) * log_strike.reshape(PAIRS)
    table[:, 5] = np.repeat(tenors, STRIKES)
    table[:, 6] = 1.0
    return table


def network_part(
    sets_ref,
    table_ref,
    prices_ref,
    w_in_ref,
    b_in_ref,
    w_mid_ref,
    b_mid_ref,
    w_out_ref,
    b_out_ref,
    prices_out,
    small_ref,
    feats,
    hid_in,
    slope_in,
    delta_mid,
    delta_in,
    hid_turn,
):
    f32, bf16 = jnp.float32, jnp.bfloat16
    pairs = CHUNK // OWN
    lane = lax.broadcasted_iota(jnp.int32, (OWN, 128), 1)
    factor = jnp.where(lane == 0, 4.0, jnp.where(lane == 3, 20.0, 1.0))
    scaled = (sets_ref[...] * factor)[None, :, :]
    prices = prices_ref[:, :PAIRS] / TOTAL_PATHS
    prices_out[...] = prices
    w_out = w_out_ref[...].astype(f32)
    g_out = jnp.zeros((8, WIDE), f32)
    g_bmid = jnp.zeros((8, WIDE), f32)
    g_bin = jnp.zeros((8, WIDE), f32)
    g_bout = jnp.zeros((8, 1), f32)
    hid_in[pl.ds(ROWS, DEPTH - ROWS), :] = jnp.zeros((DEPTH - ROWS, WIDE), bf16)
    delta_mid[pl.ds(ROWS, DEPTH - ROWS), :] = jnp.zeros((DEPTH - ROWS, WIDE), bf16)
    for c in range(ROWS // CHUNK):
        rows = pl.ds(c * CHUNK, CHUNK)
        table = table_ref[pl.ds(c * pairs, pairs), :]
        x = (table[:, None, :] + scaled).reshape(CHUNK, 128).astype(bf16)
        feats[rows, :] = x
        raw = jnp.dot(x[:, :6], w_in_ref[...], preferred_element_type=f32) + b_in_ref[...]
        g = jax.nn.sigmoid(raw)
        hid = (raw * g).astype(bf16)
        hid_in[rows, :] = hid
        slope_in[rows, :] = g * (1.0 + raw * (1.0 - g))
        raw = jnp.dot(hid, w_mid_ref[...], preferred_element_type=f32) + b_mid_ref[...]
        g = jax.nn.sigmoid(raw)
        mid = (raw * g).astype(bf16).astype(f32)
        pred = jnp.sum(mid * w_out, axis=1, keepdims=True) + b_out_ref[0, 0]
        target = jnp.concatenate(
            [prices[:, k : k + 1] for k in range(c * pairs, (c + 1) * pairs)], axis=0
        )
        slope = (pred - target) * (1.0 / SETS)
        g_bout = g_bout + jnp.sum(slope.reshape(pairs, 8, 1), axis=0)
        g_out = g_out + jnp.sum((mid * slope).reshape(pairs, 8, WIDE), axis=0)
        delta = (slope * w_out * (g * (1.0 + raw * (1.0 - g)))).astype(bf16)
        delta_mid[rows, :] = delta
        g_bmid = g_bmid + jnp.sum(delta.astype(f32).reshape(pairs, 8, WIDE), axis=0)
        back = lax.dot_general(
            delta, w_mid_ref[...], (((1,), (1,)), ((), ())), preferred_element_type=f32
        )
        inner = (back * slope_in[rows, :]).astype(bf16)
        delta_in[rows, :] = inner
        g_bin = g_bin + jnp.sum(inner.astype(f32).reshape(pairs, 8, WIDE), axis=0)
    small_ref[pl.ds(0, 8), :] = lax.dot_general(
        feats[:, :8], delta_in[...], (((0,), (0,)), ((), ())), preferred_element_type=f32
    )
    small_ref[pl.ds(6, 1), :] = jnp.sum(g_bin, axis=0, keepdims=True)
    small_ref[pl.ds(7, 1), :] = jnp.sum(g_bmid, axis=0, keepdims=True)
    small_ref[pl.ds(8, 1), :] = jnp.sum(g_out, axis=0, keepdims=True)
    small_ref[pl.ds(9, 1), :] = jnp.broadcast_to(jnp.sum(g_bout, axis=0, keepdims=True), (1, WIDE))
    small_ref[pl.ds(10, 6), :] = jnp.zeros((6, WIDE), f32)
    hid_turn[...] = hid_in[...].T


LATER = (1, 2, 3, 0)
PARTS = 2
COLS = HALF // PARTS
SENDS = 64 * PARTS + 18


def train_kernel(
    sets_ref,
    table_ref,
    prices_ref,
    w_in_ref,
    b_in_ref,
    w_mid_ref,
    b_mid_ref,
    w_out_ref,
    b_out_ref,
    prices_out,
    big_out,
    small_out,
    square_out,
    big,
    small,
    feats,
    hid_in,
    slope_in,
    delta_mid,
    delta_in,
    hid_turn,
    other,
    got_c,
    work,
    got_a,
    mid,
    got_b,
    low,
    got_z,
    s_got_c,
    s_got_a,
    s_b,
    s_z,
    s_sum,
    send_sem,
    recv_sem,
    out_sem,
):
    x, y, z, core = coords(lax.axis_index("paths"))
    a = x * (1 - core) + y * core
    b = y * (1 - core) + x * core

    def at(aa, bb, zz):
        return device_at(aa * (1 - core) + bb * core, bb * (1 - core) + aa * core, zz, core)

    partner = device_at(x, y, z, 1 - core)
    along_a = [at((a + d) % NX, b, z) for d in range(1, NX)]
    along_b = [at(a, (b + d) % NY, z) for d in range(1, NY)]
    along_z = [at(a, b, (z + d) % NZ) for d in range(1, NZ)]
    peers = [partner] + along_a + along_b + along_z
    barrier = pltpu.get_barrier_semaphore()
    for peer in peers:
        pl.semaphore_signal(barrier, inc=1, device_id=(peer,), device_id_type=MESH)

    network_part(
        sets_ref,
        table_ref,
        prices_ref,
        w_in_ref,
        b_in_ref,
        w_mid_ref,
        b_mid_ref,
        w_out_ref,
        b_out_ref,
        prices_out,
        small,
        feats,
        hid_in,
        slope_in,
        delta_mid,
        delta_in,
        hid_turn,
    )
    pl.semaphore_wait(barrier, len(peers))

    count = [0]
    started = []

    def send(src, dst, peer):
        k = count[0]
        count[0] += 1
        copy = pltpu.make_async_remote_copy(
            src_ref=src,
            dst_ref=dst,
            send_sem=send_sem.at[k],
            recv_sem=recv_sem.at[k],
            device_id=(peer,),
            device_id_type=MESH,
        )
        copy.start()
        started.append(copy)
        return copy

    def part(index, size):
        return pl.ds(pl.multiple_of(index * size, size), size)

    def rows_of(aa, bb):
        return part((aa % NX) * NY + bb % NY, ROWS_B)

    def product(first, second, e, column):
        left = jnp.concatenate(
            [hid_turn[rows_of(first + d, second + e), :] for d in range(NX)], axis=0
        )
        right = delta_mid[:, part(column, COLS)]
        out = jnp.dot(left, right, preferred_element_type=jnp.float32)
        return out.reshape(NX, ROWS_B, COLS)

    mine = part((a * NY + b) * NZ + z, ROWS_Z)
    own_cols, other_cols = part(core, HALF), part(1 - core, HALF)
    pair, steps, across, deep, pairs = {}, {}, {}, {}, {}

    def to_partner(h):
        for e in LATER:
            other[h, e] = product(b, a, e, (1 - core) * PARTS + h)
            pair[h, e] = send(other.at[h, e], got_c.at[h, e], partner)

    def along_first(h):
        for e in LATER:
            value = product(a, b, e, core * PARTS + h)
            pair[h, e].wait_recv()
            work[h, e] = value + got_c[h, e]
            steps[h, e] = [
                send(work.at[h, e, d], got_a.at[h, e, d - 1], along_a[d - 1])
                for d in range(1, NX)
            ]

    def along_second(h):
        across[h] = []
        for e in LATER:
            for copy in steps[h, e]:
                copy.wait_recv()
            mid[h, e] = work[h, e, 0] + got_a[h, e, 0] + got_a[h, e, 1] + got_a[h, e, 2]
            if e > 0:
                across[h].append(send(mid.at[h, e], got_b.at[h, e - 1], along_b[e - 1]))

    def along_third(h):
        for copy in across[h]:
            copy.wait_recv()
        low[h] = mid[h, 0] + got_b[h, 0] + got_b[h, 1] + got_b[h, 2]
        deep[h] = [
            send(low.at[h, part((z + d) % NZ, ROWS_Z), :], got_z.at[h, d - 1], along_z[d - 1])
            for d in range(1, NZ)
        ]

    def spread(h, rows, targets):
        half = big.at[core, h]
        return [send(half.at[rows, :], half.at[rows, :], peer) for peer in targets]

    def gather_third(h):
        final = low[h, part(z, ROWS_Z), :]
        for d in range(1, NZ):
            deep[h][d - 1].wait_recv()
            final = final + got_z[h, d - 1]
        big[core, h, mine, :] = final
        deep[h] = spread(h, mine, along_z)

    def gather_second(h):
        for copy in deep[h]:
            copy.wait_recv()
        rows = rows_of(a, b)
        across[h] = spread(h, rows, along_b)
        steps[h] = [spread(h, rows, along_a)]
        pairs[h] = spread(h, rows, [partner])

    def gather_first(h):
        for d in range(1, NY):
            across[h][d - 1].wait_recv()
            rows = rows_of(a, b + NY - d)
            steps[h].append(spread(h, rows, along_a))
            pairs[h] += spread(h, rows, [partner])

    def share(h):
        for e in range(NY):
            for d in range(1, NX):
                steps[h][e][d - 1].wait_recv()
                pairs[h] += spread(h, rows_of(a + NX - d, b + NY - e), [partner])

    def store(h, c):
        copy = pltpu.make_async_copy(big.at[c, h], big_out.at[c, h], out_sem.at[h, c])
        copy.start()
        total = jnp.zeros((8, COLS), jnp.float32)
        for k in range(8):
            block = big[c, h, pl.ds(k * 128, 128), :].reshape(16, 8, COLS)
            total = total + jnp.sum(block * block, axis=0)
        return copy, total

    little = send(small.at[:, other_cols], s_got_c, partner)
    to_partner(0)
    to_partner(1)
    little.wait_recv()
    s_got_c[...] += small[:, own_cols]
    littles = [
        send(s_got_c.at[:, part((a + d) % NX, SLICE)], s_got_a.at[d - 1], along_a[d - 1])
        for d in range(1, NX)
    ]
    along_first(0)
    along_first(1)
    for copy in littles:
        copy.wait_recv()
    s_b[b] = s_got_c[:, part(a, SLICE)] + s_got_a[0] + s_got_a[1] + s_got_a[2]
    littles = [send(s_b.at[b], s_b.at[b], peer) for peer in along_b]
    along_second(0)
    for copy in littles:
        copy.wait_recv()
    s_z[z] = (s_b[0] + s_b[1]) + (s_b[2] + s_b[3])
    littles = [send(s_z.at[z], s_z.at[z], peer) for peer in along_z]
    along_third(0)
    gather_third(0)
    along_second(1)
    for copy in littles:
        copy.wait_recv()
    s_all = ((s_z[0] + s_z[1]) + (s_z[2] + s_z[3])) + ((s_z[4] + s_z[5]) + (s_z[6] + s_z[7]))
    s_sum[:, part(a, SLICE)] = s_all
    littles = [
        send(s_sum.at[:, part(a, SLICE)], s_sum.at[:, part(a, SLICE)], peer) for peer in along_a
    ]
    gather_second(0)
    along_third(1)
    gather_first(0)
    for copy in littles:
        copy.wait_recv()
    small_out[core] = s_sum[...]
    little = send(small_out.at[core], small_out.at[core], partner)
    gather_third(1)
    share(0)
    gather_second(1)
    gather_first(1)
    stores = [store(0, core)]
    for copy in pairs[0]:
        copy.wait_recv()
    stores.append(store(0, 1 - core))
    share(1)
    stores.append(store(1, core))
    little.wait_recv()
    for copy in pairs[1]:
        copy.wait_recv()
    stores.append(store(1, 1 - core))
    squares = [total for copy, total in stores]
    own_squares = squares[0] + squares[2]
    other_squares = squares[1] + squares[3]
    first = own_squares * (1 - core).astype(jnp.float32) + other_squares * core.astype(jnp.float32)
    second = own_squares * core.astype(jnp.float32) + other_squares * (1 - core).astype(jnp.float32)
    square_out[0] = first
    square_out[1] = second
    for copy, total in stores:
        copy.wait()
    for copy in started:
        copy.wait_send()


def train(sets, sums, w_in, b_in, w_mid, b_mid, w_out, b_out):
    f32, bf16 = jnp.float32, jnp.bfloat16
    vmem = pl.BlockSpec(memory_space=pltpu.VMEM)
    smem = pl.BlockSpec(memory_space=pltpu.SMEM)
    return pl.pallas_call(
        train_kernel,
        in_specs=[vmem] * 8 + [smem],
        out_specs=[vmem, pl.BlockSpec(memory_space=pl.ANY), vmem, vmem],
        out_shape=[
            jax.ShapeDtypeStruct((OWN, PAIRS), f32),
            jax.ShapeDtypeStruct((NC, PARTS, WIDE, COLS), f32),
            jax.ShapeDtypeStruct((NC, SMALL, HALF), f32),
            jax.ShapeDtypeStruct((NC, 8, COLS), f32),
        ],
        scratch_shapes=[
            pltpu.VMEM((NC, PARTS, WIDE, COLS), f32),
            pltpu.VMEM((SMALL, WIDE), f32),
            pltpu.VMEM((ROWS, 128), bf16),
            pltpu.VMEM((DEPTH, WIDE), bf16),
            pltpu.VMEM((ROWS, WIDE), f32),
            pltpu.VMEM((DEPTH, WIDE), bf16),
            pltpu.VMEM((ROWS, WIDE), bf16),
            pltpu.VMEM((WIDE, DEPTH), bf16),
            pltpu.VMEM((PARTS, NY, NX, ROWS_B, COLS), f32),
            pltpu.VMEM((PARTS, NY, NX, ROWS_B, COLS), f32),
            pltpu.VMEM((PARTS, NY, NX, ROWS_B, COLS), f32),
            pltpu.VMEM((PARTS, NY, NX - 1, ROWS_B, COLS), f32),
            pltpu.VMEM((PARTS, NY, ROWS_B, COLS), f32),
            pltpu.VMEM((PARTS, NY - 1, ROWS_B, COLS), f32),
            pltpu.VMEM((PARTS, ROWS_B, COLS), f32),
            pltpu.VMEM((PARTS, NZ - 1, ROWS_Z, COLS), f32),
            pltpu.VMEM((SMALL, HALF), f32),
            pltpu.VMEM((NX - 1, SMALL, SLICE), f32),
            pltpu.VMEM((NY, SMALL, SLICE), f32),
            pltpu.VMEM((NZ, SMALL, SLICE), f32),
            pltpu.VMEM((SMALL, HALF), f32),
            pltpu.SemaphoreType.DMA((SENDS,)),
            pltpu.SemaphoreType.DMA((SENDS,)),
            pltpu.SemaphoreType.DMA((PARTS, NC)),
        ],
        compiler_params=pltpu.CompilerParams(collective_id=1, has_side_effects=True),
        name="train",
    )(
        sets,
        jnp.asarray(pair_table()),
        sums,
        w_in,
        b_in.reshape(1, WIDE),
        w_mid,
        b_mid.reshape(1, WIDE),
        w_out.reshape(1, WIDE),
        b_out.reshape(1, 1),
    )


TILES = 4
TILE = WIDE // TILES


def finish_kernel(
    big_ref, small_ref, square_ref, w_in_out, b_in_out, w_mid_out, b_mid_out, w_out_out, b_out_out
):
    def factor(total, entries):
        return lax.rsqrt(total * (1.0 / entries) + EPSILON)

    def total(value):
        return jnp.sum(jnp.sum(value, axis=1, keepdims=True), axis=0, keepdims=True)

    def sumsq(value):
        return total(value * value)

    bias = sumsq(small_ref[0, 7:8, :]) + sumsq(small_ref[1, 7:8, :])
    f_mid = factor(total(square_ref[0] + square_ref[1]) + bias, (WIDE + 1) * WIDE)
    for c in range(NC):
        for h in range(PARTS):
            w_mid_out[:, pl.ds((c * PARTS + h) * COLS, COLS)] = big_ref[c, h] * f_mid

    @pl.when(pl.program_id(0) == 0)
    def _():
        small = jnp.concatenate([small_ref[0], small_ref[1]], axis=1)
        g_bout = small[9:10, 0:1]
        f_in = factor(sumsq(small[0:7]), 7 * WIDE)
        f_out = factor(sumsq(small[8:9]) + g_bout * g_bout, WIDE + 1)
        w_in_out[...] = small[0:6] * f_in
        b_in_out[...] = small[6:7] * f_in
        b_mid_out[...] = small[7:8] * f_mid
        w_out_out[...] = small[8:9] * f_out
        b_out_out[...] = g_bout * f_out


def finish(big, small, squares):
    f32 = jnp.float32
    shapes = [(6, WIDE), (1, WIDE), (WIDE, WIDE), (1, WIDE), (1, WIDE), (1, 1)]
    blocks = [(6, WIDE), (1, WIDE), (TILE, WIDE), (1, WIDE), (1, WIDE), (1, 1)]
    moves = [lambda i: (0, 0)] * 2 + [lambda i: (i, 0)] + [lambda i: (0, 0)] * 3
    w_in, b_in, w_mid, b_mid, w_out, b_out = pl.pallas_call(
        finish_kernel,
        grid=(TILES,),
        in_specs=[
            pl.BlockSpec((NC, PARTS, TILE, COLS), lambda i: (0, 0, i, 0)),
            pl.BlockSpec((NC, SMALL, HALF), lambda i: (0, 0, 0)),
            pl.BlockSpec((NC, 8, COLS), lambda i: (0, 0, 0)),
        ],
        out_specs=[pl.BlockSpec(block, move) for block, move in zip(blocks, moves)],
        out_shape=[jax.ShapeDtypeStruct(shape, f32) for shape in shapes],
        name="finish",
    )(big, small, squares)
    return w_in, b_in.reshape(WIDE), w_mid, b_mid.reshape(WIDE), w_out.reshape(WIDE), b_out.reshape(1)


def on_device(params, increments, w_in, b_in, w_mid, b_mid, w_out, b_out):
    sums, sets = price_sums(params, increments)
    prices, big, small, squares = train(sets, sums, w_in, b_in, w_mid, b_mid, w_out, b_out)
    return (prices, *finish(big, small, squares))


def solution(mesh):
    in_specs = (P(), P(None, None, "paths"), P(), P(), P(), P(), P(), P())
    out_specs = (P("paths", None), P(), P(), P(), P(), P(), P())
    return jax.shard_map(
        on_device, mesh=mesh, in_specs=in_specs, out_specs=out_specs, check_vma=False
    )
```

```python
import math

import jax
import jax.numpy as jnp
import numpy as np
from jax import lax
from jax.experimental import pallas as pl
from jax.experimental.pallas import tpu as pltpu
from jax.sharding import PartitionSpec as P

STEPS = 64
MATS = 8
STRIKES = 11
PAIRS = 88
EPSILON = 1e-06
LOG2E = 1.4426950408889634
NX, NY, NZ, NC = 4, 4, 8, 2
OWN = 8
BLOCK = NY * NZ * OWN
BLOCKS = NX * NC
SETS = 2048
TOTAL_PATHS = 32768
MESH = pl.DeviceIdType.MESH


def strike_values():
    return [
        [math.exp(0.05 * (j - 5) * math.sqrt((m + 1) / MATS)) for j in range(STRIKES)]
        for m in range(MATS)
    ]


def coords(index):
    core = index % NC
    z = (index // NC) % NZ
    y = (index // (NC * NZ)) % NY
    x = index // (NC * NZ * NY)
    return x, y, z, core


def device_at(x, y, z, core):
    return ((x * NY + y) * NZ + z) * NC + core


def lag_tables():
    lag = np.tile(np.arange(STEPS, dtype=np.float64), 2)
    table = np.zeros((8, 128), np.float32)
    table[0] = np.log2(np.maximum(lag, 1.0))
    table[1] = np.log2(np.maximum(lag - 1.0, 1.0))
    table[2] = np.log2(np.maximum(lag, 1.0) / STEPS)
    return table


def set_operands(sets, lag_ref, rows, ratio, scale):
    f32, bf16 = jnp.float32, jnp.bfloat16
    shape = (sets.shape[0], 128)
    hurst, vol, correl, forward = (
        jnp.broadcast_to(sets[:, k : k + 1], shape) for k in range(4)
    )
    lane = lax.broadcasted_iota(jnp.int32, shape, 1)
    upper = lane >= STEPS
    lag = jnp.where(upper, lane - STEPS, lane)
    expo = hurst + 0.5
    late = jnp.where(lag >= 2, jnp.exp2(expo * lag_ref[1:2, :]), 0.0)
    powers = jnp.exp2(expo * lag_ref[0:1, :]) - late
    front = jnp.sqrt(2.0 * hurst) * jnp.exp2(-6.0 * hurst) / expo
    kern = jnp.where(lag >= 1, powers * front, 0.0).astype(bf16).astype(f32)
    half = (0.5 * LOG2E) * vol
    weight = kern * half
    comp = (-0.5 * vol * half) * jnp.exp2((2.0 * hurst) * lag_ref[2:3, :])
    rest = 1.0 - correl * correl
    const = (0.5 * LOG2E) * jnp.log(forward * (1.0 / STEPS) / rest) - 1.0
    w_hi = weight.astype(bf16).astype(f32)
    c_hi = comp.astype(bf16).astype(f32)
    k_hi = const.astype(bf16).astype(f32)
    k_rest = const - k_hi
    k_lo = k_rest.astype(bf16).astype(f32)
    first = lag == 0
    kern_row = jnp.where(first, jnp.where(upper, k_lo, k_hi), jnp.where(upper, weight - w_hi, w_hi))
    comp_row = jnp.where(
        first, jnp.where(upper, 0.0, k_rest - k_lo), jnp.where(upper, comp - c_hi, c_hi)
    )
    rows[:, 0:128] = kern_row.astype(bf16)
    rows[:, 128:256] = comp_row.astype(bf16)
    ratio[...] = correl * lax.rsqrt(rest)
    scale[...] = (2.0 * LOG2E) * rest


def price_peers(x, y, z, core):
    mine = x * NC + core
    blocks = []
    for b in range(BLOCKS - 1):
        other = (mine + 1 + b) % BLOCKS
        blocks.append(device_at(other // NC, y, z, other % NC))
    along_y = [device_at(x, (y + d) % NY, z, core) for d in range(1, NY)]
    along_z = [device_at(x, y, (z + d) % NZ, core) for d in range(1, NZ)]
    return blocks, along_y, along_z


def prices_kernel(
    params_ref,
    lag_ref,
    inc_ref,
    out_ref,
    own_ref,
    sets,
    rows_ref,
    ratio_ref,
    scale_ref,
    noise,
    table,
    walk,
    part,
    sent,
    got,
    got_y,
    got_z,
    send_sem,
    got_sem,
    send_y,
    got_y_sem,
    send_z,
    got_z_sem,
):
    step = pl.program_id(0)
    x, y, z, core = coords(lax.axis_index("paths"))
    blocks, along_y, along_z = price_peers(x, y, z, core)

    @pl.when(step == 0)
    def _():
        barrier = pltpu.get_barrier_semaphore()
        for peer in blocks + along_y + along_z:
            pl.semaphore_signal(barrier, inc=1, device_id=(peer,), device_id_type=MESH)
        for k in range(NX * NY):
            some = params_ref[:, pl.ds(k * 128, 128)]
            some = jnp.concatenate([some, jnp.zeros((124, 128), jnp.float32)], axis=0).T
            sets[k // NY, pl.ds((k % NY) * NZ, NZ)] = some.reshape(NZ, NC, OWN, 128)
        own_ref[...] = sets[x, y * NZ + z, core]
        noise[0] = inc_ref[0].astype(jnp.float32)
        noise[1] = inc_ref[1].astype(jnp.float32)
        part[...] = jnp.zeros_like(part)
        row = lax.broadcasted_iota(jnp.int32, (STEPS, 128), 0)
        for j in range(STEPS):
            walk[pl.ds(STEPS - 1 - j, 1), :] = noise[0, pl.ds(j, 1), :]
        walk[pl.ds(STEPS, STEPS), :] = jnp.zeros((STEPS, 128), jnp.float32)
        one = jnp.ones((STEPS, 128), jnp.float32)
        for i in range(STEPS):
            past = walk[pl.ds(STEPS - 1 - i, STEPS), :]
            past = jnp.where(row == 0, one, past).astype(jnp.bfloat16)
            pick = jnp.where(row == i, 1.0, 0.0)
            hot = jnp.where(row == 0, one, pick).astype(jnp.bfloat16)
            hot_lo = jnp.where(row == 0, 0.0, pick).astype(jnp.bfloat16)
            cols = pl.ds((i % 2) * 128, 128)
            table[i // 2, pl.ds(0, STEPS), cols] = past
            table[i // 2, pl.ds(STEPS, STEPS), cols] = past
            table[i // 2, pl.ds(2 * STEPS, STEPS), cols] = hot
            table[i // 2, pl.ds(3 * STEPS, STEPS), cols] = hot_lo

    strikes = strike_values()
    other = (x * NC + core + 1 + step) % BLOCKS
    block = sets[other // NC, :, other % NC].reshape(BLOCK, 128)
    set_operands(block, lag_ref, rows_ref, ratio_ref, scale_ref)
    walk[...] = jnp.zeros_like(walk)
    for m in range(MATS):
        for q in range(4):
            pair = jnp.dot(
                rows_ref[...], table[m * 4 + q], preferred_element_type=jnp.float32
            )
            for h in range(2):
                i = m * 8 + q * 2 + h
                vol = jnp.exp2(pair[:, h * 128 : (h + 1) * 128])
                shock = ratio_ref[...] * noise[0, pl.ds(i, 1), :] + noise[1, pl.ds(i, 1), :]
                walk[...] += vol * (shock - vol)
        spot = jnp.exp2((walk[...] * scale_ref[...]).T)
        for j in range(STRIKES):
            k = strikes[m][j]
            top = jnp.sum(jnp.maximum(spot, k).reshape(16, 8, BLOCK), axis=0)
            part[pl.ds(m * STRIKES + j, 1), :] = jnp.sum(top - 16.0 * k, axis=0, keepdims=True)
    sent[step] = part[...].T

    @pl.when(step == 0)
    def _():
        pl.semaphore_wait(pltpu.get_barrier_semaphore(), len(blocks + along_y + along_z))

    def block_copy(b):
        other = (x * NC + core + 1 + b) % BLOCKS
        return pltpu.make_async_remote_copy(
            src_ref=sent.at[b],
            dst_ref=got.at[b],
            send_sem=send_sem.at[b],
            recv_sem=got_sem.at[b],
            device_id=(device_at(other // NC, y, z, other % NC),),
            device_id_type=MESH,
        )

    @pl.when(step < BLOCKS - 1)
    def _():
        block_copy(step).start()

    @pl.when(step == BLOCKS - 1)
    def _():
        total = sent.at[BLOCKS - 1]
        for b in range(BLOCKS - 1):
            block_copy(b).wait_recv()
            total[...] += got[b]
        rows_y = NZ * OWN

        def y_rows(d):
            return pl.ds(pl.multiple_of(((y + d) % NY) * rows_y, rows_y), rows_y)

        copies = []
        for d in range(1, NY):
            copy = pltpu.make_async_remote_copy(
                src_ref=total.at[y_rows(d), :],
                dst_ref=got_y.at[d],
                send_sem=send_y.at[d],
                recv_sem=got_y_sem.at[d],
                device_id=(along_y[d - 1],),
                device_id_type=MESH,
            )
            copy.start()
            copies.append(copy)
        own = total[y_rows(0), :]
        for d in range(1, NY):
            copies[d - 1].wait_recv()
            own = own + got_y[d]
        got_y[0] = own

        def z_rows(d):
            return pl.ds(pl.multiple_of(((z + d) % NZ) * OWN, OWN), OWN)

        for d in range(1, NZ):
            copy = pltpu.make_async_remote_copy(
                src_ref=got_y.at[0, z_rows(d), :],
                dst_ref=got_z.at[d],
                send_sem=send_z.at[d],
                recv_sem=got_z_sem.at[d],
                device_id=(along_z[d - 1],),
                device_id_type=MESH,
            )
            copy.start()
            copies.append(copy)
        final = got_y[0, z_rows(0), :]
        for d in range(1, NZ):
            copies[NY - 1 + d - 1].wait_recv()
            final = final + got_z[d]
        out_ref[...] = final
        for b in range(BLOCKS - 1):
            block_copy(b).wait_send()
        for copy in copies:
            copy.wait_send()


def price_sums(params, increments):
    f32 = jnp.float32
    own = jax.ShapeDtypeStruct((OWN, 128), f32)
    return pl.pallas_call(
        prices_kernel,
        grid=(BLOCKS,),
        in_specs=[
            pl.BlockSpec((4, BLOCKS * BLOCK), lambda b: (0, 0)),
            pl.BlockSpec((8, 128), lambda b: (0, 0)),
            pl.BlockSpec((2, STEPS, 128), lambda b: (0, 0, 0)),
        ],
        out_specs=[pl.BlockSpec((OWN, 128), lambda b: (0, 0))] * 2,
        out_shape=[own, own],
        scratch_shapes=[
            pltpu.VMEM((NX, NY * NZ, NC, OWN, 128), f32),
            pltpu.VMEM((BLOCK, 256), jnp.bfloat16),
            pltpu.VMEM((BLOCK, 128), f32),
            pltpu.VMEM((BLOCK, 128), f32),
            pltpu.VMEM((2, STEPS, 128), f32),
            pltpu.VMEM((STEPS // 2, 256, 256), jnp.bfloat16),
            pltpu.VMEM((BLOCK, 128), f32),
            pltpu.VMEM((128, BLOCK), f32),
            pltpu.VMEM((BLOCKS, BLOCK, 128), f32),
            pltpu.VMEM((BLOCKS - 1, BLOCK, 128), f32),
            pltpu.VMEM((NY, NZ * OWN, 128), f32),
            pltpu.VMEM((NZ, OWN, 128), f32),
            pltpu.SemaphoreType.DMA((BLOCKS,)),
            pltpu.SemaphoreType.DMA((BLOCKS,)),
            pltpu.SemaphoreType.DMA((NY,)),
            pltpu.SemaphoreType.DMA((NY,)),
            pltpu.SemaphoreType.DMA((NZ,)),
            pltpu.SemaphoreType.DMA((NZ,)),
        ],
        compiler_params=pltpu.CompilerParams(collective_id=0, has_side_effects=True, vmem_limit_bytes=24 * 1024 * 1024),
        cost_estimate=pl.CostEstimate(
            flops=20 * 1000 * 1000 * 1000, bytes_accessed=1000 * 1000, transcendentals=18 * 1000 * 1000
        ),
        name="prices",
    )(params.T, jnp.asarray(lag_tables()), increments)


WIDE = 1024
HALF = WIDE // NC
ROWS_A = WIDE // NX
ROWS_B = ROWS_A // NY
ROWS_Z = ROWS_B // NZ
SMALL = 16
SLICE = HALF // NX


ROWS = PAIRS * OWN
CHUNK = ROWS // 4
DEPTH = 768


def pair_table():
    tenors = (np.arange(MATS, dtype=np.float32) + np.float32(1.0)) / np.float32(MATS)
    offsets = np.arange(STRIKES, dtype=np.float32) - np.float32((STRIKES - 1) / 2.0)
    log_strike = np.float32(0.05) * offsets[None, :] * np.sqrt(tenors)[:, None]
    table = np.zeros((PAIRS, 128), np.float32)
    table[:, 4] = np.float32(4.0) * log_strike.reshape(PAIRS)
    table[:, 5] = np.repeat(tenors, STRIKES)
    table[:, 6] = 1.0
    return table


def network_part(
    sets_ref,
    table_ref,
    prices_ref,
    w_in_ref,
    b_in_ref,
    w_mid_ref,
    b_mid_ref,
    w_out_ref,
    b_out_ref,
    prices_out,
    small_ref,
    feats,
    hid_in,
    slope_in,
    delta_mid,
    delta_in,
    hid_turn,
):
    f32, bf16 = jnp.float32, jnp.bfloat16
    pairs = CHUNK // OWN
    lane = lax.broadcasted_iota(jnp.int32, (OWN, 128), 1)
    factor = jnp.where(lane == 0, 4.0, jnp.where(lane == 3, 20.0, 1.0))
    scaled = (sets_ref[...] * factor)[None, :, :]
    prices = prices_ref[:, :PAIRS] / TOTAL_PATHS
    prices_out[...] = prices
    w_out = w_out_ref[...].reshape(1, WIDE).astype(f32)
    g_out = jnp.zeros((8, WIDE), f32)
    g_bmid = jnp.zeros((8, WIDE), f32)
    g_bin = jnp.zeros((8, WIDE), f32)
    g_bout = jnp.zeros((8, 1), f32)
    hid_in[pl.ds(ROWS, DEPTH - ROWS), :] = jnp.zeros((DEPTH - ROWS, WIDE), bf16)
    delta_mid[pl.ds(ROWS, DEPTH - ROWS), :] = jnp.zeros((DEPTH - ROWS, WIDE), bf16)
    for c in range(ROWS // CHUNK):
        rows = pl.ds(c * CHUNK, CHUNK)
        table = table_ref[pl.ds(c * pairs, pairs), :]
        x = (table[:, None, :] + scaled).reshape(CHUNK, 128).astype(bf16)
        feats[rows, :] = x
        raw = jnp.dot(x[:, :6], w_in_ref[...], preferred_element_type=f32) + b_in_ref[...]
        g = jax.nn.sigmoid(raw)
        hid = (raw * g).astype(bf16)
        hid_in[rows, :] = hid
        slope_in[rows, :] = g * (1.0 + raw * (1.0 - g))
        raw = jnp.dot(hid, w_mid_ref[...], preferred_element_type=f32) + b_mid_ref[...]
        g = jax.nn.sigmoid(raw)
        mid = (raw * g).astype(bf16).astype(f32)
        pred = jnp.sum(mid * w_out, axis=1, keepdims=True) + b_out_ref[0, 0]
        target = jnp.concatenate(
            [prices[:, k : k + 1] for k in range(c * pairs, (c + 1) * pairs)], axis=0
        )
        slope = (pred - target) * (1.0 / SETS)
        g_bout = g_bout + jnp.sum(slope.reshape(pairs, 8, 1), axis=0)
        g_out = g_out + jnp.sum((mid * slope).reshape(pairs, 8, WIDE), axis=0)
        delta = (slope * w_out * (g * (1.0 + raw * (1.0 - g)))).astype(bf16)
        delta_mid[rows, :] = delta
        g_bmid = g_bmid + jnp.sum(delta.astype(f32).reshape(pairs, 8, WIDE), axis=0)
        back = lax.dot_general(
            delta, w_mid_ref[...], (((1,), (1,)), ((), ())), preferred_element_type=f32
        )
        inner = (back * slope_in[rows, :]).astype(bf16)
        delta_in[rows, :] = inner
        g_bin = g_bin + jnp.sum(inner.astype(f32).reshape(pairs, 8, WIDE), axis=0)
    small_ref[pl.ds(0, 8), :] = lax.dot_general(
        feats[:, :8], delta_in[...], (((0,), (0,)), ((), ())), preferred_element_type=f32
    )
    small_ref[pl.ds(6, 1), :] = jnp.sum(g_bin, axis=0, keepdims=True)
    small_ref[pl.ds(7, 1), :] = jnp.sum(g_bmid, axis=0, keepdims=True)
    small_ref[pl.ds(8, 1), :] = jnp.sum(g_out, axis=0, keepdims=True)
    small_ref[pl.ds(9, 1), :] = jnp.broadcast_to(jnp.sum(g_bout, axis=0, keepdims=True), (1, WIDE))
    small_ref[pl.ds(10, 6), :] = jnp.zeros((6, WIDE), f32)
    hid_turn[...] = hid_in[...].T


LATER = (1, 2, 3, 0)
SENDS = 84


def train_kernel(
    sets_ref,
    table_ref,
    prices_ref,
    w_in_ref,
    b_in_ref,
    w_mid_ref,
    b_mid_ref,
    w_out_ref,
    b_out_ref,
    prices_out,
    big_out,
    small_out,
    small,
    feats,
    hid_in,
    slope_in,
    delta_mid,
    delta_in,
    hid_turn,
    other,
    got_c,
    work,
    got_a,
    mid,
    got_b,
    low,
    got_z,
    s_got_c,
    s_got_a,
    s_b,
    s_z,
    s_sum,
    send_sem,
    recv_sem,
):
    x, y, z, core = coords(lax.axis_index("paths"))
    a = x * (1 - core) + y * core
    b = y * (1 - core) + x * core

    def at(aa, bb, zz):
        return device_at(aa * (1 - core) + bb * core, bb * (1 - core) + aa * core, zz, core)

    partner = device_at(x, y, z, 1 - core)
    along_a = [at((a + d) % NX, b, z) for d in range(1, NX)]
    along_b = [at(a, (b + d) % NY, z) for d in range(1, NY)]
    along_z = [at(a, b, (z + d) % NZ) for d in range(1, NZ)]
    peers = [partner] + along_a + along_b + along_z
    barrier = pltpu.get_barrier_semaphore()
    for peer in peers:
        pl.semaphore_signal(barrier, inc=1, device_id=(peer,), device_id_type=MESH)

    network_part(
        sets_ref,
        table_ref,
        prices_ref,
        w_in_ref,
        b_in_ref,
        w_mid_ref,
        b_mid_ref,
        w_out_ref,
        b_out_ref,
        prices_out,
        small,
        feats,
        hid_in,
        slope_in,
        delta_mid,
        delta_in,
        hid_turn,
    )
    pl.semaphore_wait(barrier, len(peers))

    count = [0]
    started = []

    def send(src, dst, peer):
        k = count[0]
        count[0] += 1
        copy = pltpu.make_async_remote_copy(
            src_ref=src,
            dst_ref=dst,
            send_sem=send_sem.at[k],
            recv_sem=recv_sem.at[k],
            device_id=(peer,),
            device_id_type=MESH,
        )
        copy.start()
        started.append(copy)
        return copy

    def part(index, size):
        return pl.ds(pl.multiple_of(index * size, size), size)

    def rows_of(aa, bb):
        return part((aa % NX) * NY + bb % NY, ROWS_B)

    def product(first, second, e, cols):
        left = jnp.concatenate(
            [hid_turn[rows_of(first + d, second + e), :] for d in range(NX)], axis=0
        )
        out = jnp.dot(left, delta_mid[:, cols], preferred_element_type=jnp.float32)
        return out.reshape(NX, ROWS_B, HALF)

    own_cols, other_cols = part(core, HALF), part(1 - core, HALF)
    little = send(small.at[:, other_cols], s_got_c, partner)
    pair = {}
    for e in LATER:
        other[e] = product(b, a, e, other_cols)
        pair[e] = send(other.at[e], got_c.at[e], partner)
    little.wait_recv()
    s_got_c[...] += small[:, own_cols]
    littles = []
    for d in range(1, NX):
        littles.append(
            send(s_got_c.at[:, part((a + d) % NX, SLICE)], s_got_a.at[d - 1], along_a[d - 1])
        )
    steps = {}
    for e in LATER:
        mine = product(a, b, e, own_cols)
        pair[e].wait_recv()
        work[e] = mine + got_c[e]
        steps[e] = [
            send(work.at[e, d], got_a.at[e, d - 1], along_a[d - 1]) for d in range(1, NX)
        ]
    for copy in littles:
        copy.wait_recv()
    s_b[b] = s_got_c[:, part(a, SLICE)] + s_got_a[0] + s_got_a[1] + s_got_a[2]
    littles = [send(s_b.at[b], s_b.at[b], peer) for peer in along_b]
    across = []
    for e in LATER:
        for copy in steps[e]:
            copy.wait_recv()
        mid[e] = work[e, 0] + got_a[e, 0] + got_a[e, 1] + got_a[e, 2]
        if e > 0:
            across.append(send(mid.at[e], got_b.at[e - 1], along_b[e - 1]))
    for copy in littles:
        copy.wait_recv()
    s_z[z] = (s_b[0] + s_b[1]) + (s_b[2] + s_b[3])
    littles = [send(s_z.at[z], s_z.at[z], peer) for peer in along_z]
    for copy in across:
        copy.wait_recv()
    low[...] = mid[0] + got_b[0] + got_b[1] + got_b[2]
    deep = [
        send(low.at[part((z + d) % NZ, ROWS_Z), :], got_z.at[d - 1], along_z[d - 1])
        for d in range(1, NZ)
    ]
    for copy in littles:
        copy.wait_recv()
    s_all = ((s_z[0] + s_z[1]) + (s_z[2] + s_z[3])) + ((s_z[4] + s_z[5]) + (s_z[6] + s_z[7]))
    s_sum[:, part(a, SLICE)] = s_all
    littles = [
        send(s_sum.at[:, part(a, SLICE)], s_sum.at[:, part(a, SLICE)], peer) for peer in along_a
    ]
    final = low[part(z, ROWS_Z), :]
    for d in range(1, NZ):
        deep[d - 1].wait_recv()
        final = final + got_z[d - 1]

    half_out = big_out.at[core]
    mine = part((a * NY + b) * NZ + z, ROWS_Z)
    half_out[mine, :] = final
    deep = [send(half_out.at[mine, :], half_out.at[mine, :], peer) for peer in along_z]
    for copy in littles:
        copy.wait_recv()
    small_out[core] = s_sum[...]
    little = send(small_out.at[core], small_out.at[core], partner)
    for copy in deep:
        copy.wait_recv()

    def spread(rows, targets):
        return [send(half_out.at[rows, :], half_out.at[rows, :], peer) for peer in targets]

    across = spread(rows_of(a, b), along_b)
    steps = [spread(rows_of(a, b), along_a)]
    pairs = spread(rows_of(a, b), [partner])
    for d in range(1, NY):
        across[d - 1].wait_recv()
        rows = rows_of(a, b + NY - d)
        steps.append(spread(rows, along_a))
        pairs += spread(rows, [partner])
    for e in range(NY):
        for d in range(1, NX):
            steps[e][d - 1].wait_recv()
            pairs += spread(rows_of(a + NX - d, b + NY - e), [partner])
    little.wait_recv()
    for copy in pairs:
        copy.wait_recv()
    for copy in started:
        copy.wait_send()


def train(sets, sums, w_in, b_in, w_mid, b_mid, w_out, b_out):
    f32, bf16 = jnp.float32, jnp.bfloat16
    vmem = pl.BlockSpec(memory_space=pltpu.VMEM)
    smem = pl.BlockSpec(memory_space=pltpu.SMEM)
    return pl.pallas_call(
        train_kernel,
        in_specs=[vmem] * 8 + [smem],
        out_specs=[vmem, vmem, vmem],
        out_shape=[
            jax.ShapeDtypeStruct((OWN, PAIRS), f32),
            jax.ShapeDtypeStruct((NC, WIDE, HALF), f32),
            jax.ShapeDtypeStruct((NC, SMALL, HALF), f32),
        ],
        scratch_shapes=[
            pltpu.VMEM((SMALL, WIDE), f32),
            pltpu.VMEM((ROWS, 128), bf16),
            pltpu.VMEM((DEPTH, WIDE), bf16),
            pltpu.VMEM((ROWS, WIDE), f32),
            pltpu.VMEM((DEPTH, WIDE), bf16),
            pltpu.VMEM((ROWS, WIDE), bf16),
            pltpu.VMEM((WIDE, DEPTH), bf16),
            pltpu.VMEM((NY, NX, ROWS_B, HALF), f32),
            pltpu.VMEM((NY, NX, ROWS_B, HALF), f32),
            pltpu.VMEM((NY, NX, ROWS_B, HALF), f32),
            pltpu.VMEM((NY, NX - 1, ROWS_B, HALF), f32),
            pltpu.VMEM((NY, ROWS_B, HALF), f32),
            pltpu.VMEM((NY - 1, ROWS_B, HALF), f32),
            pltpu.VMEM((ROWS_B, HALF), f32),
            pltpu.VMEM((NZ - 1, ROWS_Z, HALF), f32),
            pltpu.VMEM((SMALL, HALF), f32),
            pltpu.VMEM((NX - 1, SMALL, SLICE), f32),
            pltpu.VMEM((NY, SMALL, SLICE), f32),
            pltpu.VMEM((NZ, SMALL, SLICE), f32),
            pltpu.VMEM((SMALL, HALF), f32),
            pltpu.SemaphoreType.DMA((SENDS,)),
            pltpu.SemaphoreType.DMA((SENDS,)),
        ],
        compiler_params=pltpu.CompilerParams(collective_id=1, has_side_effects=True, vmem_limit_bytes=36 * 1024 * 1024),
        name="train",
    )(
        sets,
        jnp.asarray(pair_table()),
        sums,
        w_in,
        b_in.reshape(1, WIDE),
        w_mid,
        b_mid.reshape(1, WIDE),
        w_out,
        b_out.reshape(1, 1),
    )


def finish_kernel(
    prices_ref,
    big_ref,
    small_ref,
    prices_out,
    w_in_out,
    b_in_out,
    w_mid_out,
    b_mid_out,
    w_out_out,
    b_out_out,
):
    prices_out[...] = prices_ref[...]

    def factor(total, entries):
        return lax.rsqrt(total * (1.0 / entries) + EPSILON)

    def sumsq(value):
        return jnp.sum(jnp.sum(value * value, axis=1, keepdims=True), axis=0, keepdims=True)

    small = jnp.concatenate([small_ref[0], small_ref[1]], axis=1)
    g_bout = small[9:10, 0:1]
    s_mid = sumsq(small[7:8])
    for k in range(8):
        for c in range(NC):
            s_mid = s_mid + sumsq(big_ref[c, pl.ds(k * 128, 128), :])
    f_in = factor(sumsq(small[0:7]), 7 * WIDE)
    f_mid = factor(s_mid, (WIDE + 1) * WIDE)
    f_out = factor(sumsq(small[8:9]) + g_bout * g_bout, WIDE + 1)
    w_in_out[...] = small[0:6] * f_in
    b_in_out[...] = small[6:7] * f_in
    b_mid_out[...] = small[7:8] * f_mid
    w_out_out[...] = small[8:9] * f_out
    b_out_out[...] = g_bout * f_out
    for c in range(NC):
        w_mid_out[:, pl.ds(c * HALF, HALF)] = big_ref[c] * f_mid


def finish(prices, big, small):
    f32 = jnp.float32
    vmem = pl.BlockSpec(memory_space=pltpu.VMEM)
    shapes = [(OWN, PAIRS), (6, WIDE), (1, WIDE), (WIDE, WIDE), (1, WIDE), (1, WIDE), (1, 1)]
    prices, w_in, b_in, w_mid, b_mid, w_out, b_out = pl.pallas_call(
        finish_kernel,
        in_specs=[vmem] * 3,
        out_specs=[vmem] * 7,
        out_shape=[jax.ShapeDtypeStruct(shape, f32) for shape in shapes],
        compiler_params=pltpu.CompilerParams(vmem_limit_bytes=16 * 1024 * 1024), name="finish",
    )(prices, big, small)
    b_in, b_mid, w_out = b_in.reshape(WIDE), b_mid.reshape(WIDE), w_out.reshape(WIDE)
    return prices, w_in, b_in, w_mid, b_mid, w_out, b_out.reshape(1)


def on_device(params, increments, w_in, b_in, w_mid, b_mid, w_out, b_out):
    sums, sets = price_sums(params, increments)
    prices, big, small = train(sets, sums, w_in, b_in, w_mid, b_mid, w_out, b_out)
    return finish(prices, big, small)


def solution(mesh):
    in_specs = (P(), P(None, None, "paths"), P(), P(), P(), P(), P(), P())
    out_specs = (P("paths", None), P(), P(), P(), P(), P(), P())
    return jax.shard_map(
        on_device, mesh=mesh, in_specs=in_specs, out_specs=out_specs, check_vma=False
    )
```

```python
import math

import jax
import jax.numpy as jnp
import numpy as np
from jax import lax
from jax.experimental import pallas as pl
from jax.experimental.pallas import tpu as pltpu
from jax.sharding import PartitionSpec as P

STEPS = 64
MATS = 8
STRIKES = 11
PAIRS = 88
EPSILON = 1e-06
LOG2E = 1.4426950408889634
NX, NY, NZ, NC = 4, 4, 8, 2
OWN = 8
BLOCK = NY * NZ * OWN
BLOCKS = NX * NC
SETS = 2048
TOTAL_PATHS = 32768
MESH = pl.DeviceIdType.MESH


def strike_values():
    return [
        [math.exp(0.05 * (j - 5) * math.sqrt((m + 1) / MATS)) for j in range(STRIKES)]
        for m in range(MATS)
    ]


def coords(index):
    core = index % NC
    z = (index // NC) % NZ
    y = (index // (NC * NZ)) % NY
    x = index // (NC * NZ * NY)
    return x, y, z, core


def device_at(x, y, z, core):
    return ((x * NY + y) * NZ + z) * NC + core


def lag_tables():
    lag = np.tile(np.arange(STEPS, dtype=np.float64), 2)
    table = np.zeros((8, 128), np.float32)
    table[0] = np.log2(np.maximum(lag, 1.0))
    table[1] = np.log2(np.maximum(lag - 1.0, 1.0))
    table[2] = np.log2(np.maximum(lag, 1.0) / STEPS)
    return table


def set_operands(sets, lag_ref, rows, ratio, scale):
    f32, bf16 = jnp.float32, jnp.bfloat16
    shape = (sets.shape[0], 128)
    hurst, vol, correl, forward = (
        jnp.broadcast_to(sets[:, k : k + 1], shape) for k in range(4)
    )
    lane = lax.broadcasted_iota(jnp.int32, shape, 1)
    upper = lane >= STEPS
    lag = jnp.where(upper, lane - STEPS, lane)
    expo = hurst + 0.5
    late = jnp.where(lag >= 2, jnp.exp2(expo * lag_ref[1:2, :]), 0.0)
    powers = jnp.exp2(expo * lag_ref[0:1, :]) - late
    front = jnp.sqrt(2.0 * hurst) * jnp.exp2(-6.0 * hurst) / expo
    kern = jnp.where(lag >= 1, powers * front, 0.0).astype(bf16).astype(f32)
    half = (0.5 * LOG2E) * vol
    weight = kern * half
    comp = (-0.5 * vol * half) * jnp.exp2((2.0 * hurst) * lag_ref[2:3, :])
    rest = 1.0 - correl * correl
    const = (0.5 * LOG2E) * jnp.log(forward * (1.0 / STEPS) / rest) - 1.0
    w_hi = weight.astype(bf16).astype(f32)
    c_hi = comp.astype(bf16).astype(f32)
    k_hi = const.astype(bf16).astype(f32)
    k_rest = const - k_hi
    k_lo = k_rest.astype(bf16).astype(f32)
    first = lag == 0
    kern_row = jnp.where(first, jnp.where(upper, k_lo, k_hi), jnp.where(upper, weight - w_hi, w_hi))
    comp_row = jnp.where(
        first, jnp.where(upper, 0.0, k_rest - k_lo), jnp.where(upper, comp - c_hi, c_hi)
    )
    rows[:, 0:128] = kern_row.astype(bf16)
    rows[:, 128:256] = comp_row.astype(bf16)
    ratio[...] = correl * lax.rsqrt(rest)
    scale[...] = (2.0 * LOG2E) * rest


def price_peers(x, y, z, core):
    mine = x * NC + core
    blocks = []
    for b in range(BLOCKS - 1):
        other = (mine + 1 + b) % BLOCKS
        blocks.append(device_at(other // NC, y, z, other % NC))
    along_y = [device_at(x, (y + d) % NY, z, core) for d in range(1, NY)]
    along_z = [device_at(x, y, (z + d) % NZ, core) for d in range(1, NZ)]
    return blocks, along_y, along_z


def prices_part(
    params_ref,
    lag_ref,
    inc_ref,
    between,
    sets,
    rows_ref,
    ratio_ref,
    scale_ref,
    noise,
    table,
    walk,
    part,
    sent,
    got,
    got_y,
    got_z,
    send_sem,
    got_sem,
    send_y,
    got_y_sem,
    send_z,
    got_z_sem,
):
    x, y, z, core = coords(lax.axis_index("paths"))
    blocks, along_y, along_z = price_peers(x, y, z, core)
    for k in range(NX * NY):
        some = params_ref[:, pl.ds(k * 128, 128)]
        some = jnp.concatenate([some, jnp.zeros((124, 128), jnp.float32)], axis=0).T
        sets[k // NY, pl.ds((k % NY) * NZ, NZ)] = some.reshape(NZ, NC, OWN, 128)
    noise[0] = inc_ref[0].astype(jnp.float32)
    noise[1] = inc_ref[1].astype(jnp.float32)
    part[...] = jnp.zeros_like(part)
    row = lax.broadcasted_iota(jnp.int32, (STEPS, 128), 0)
    for j in range(STEPS):
        walk[pl.ds(STEPS - 1 - j, 1), :] = noise[0, pl.ds(j, 1), :]
    walk[pl.ds(STEPS, STEPS), :] = jnp.zeros((STEPS, 128), jnp.float32)
    one = jnp.ones((STEPS, 128), jnp.float32)
    for i in range(STEPS):
        past = walk[pl.ds(STEPS - 1 - i, STEPS), :]
        past = jnp.where(row == 0, one, past).astype(jnp.bfloat16)
        pick = jnp.where(row == i, 1.0, 0.0)
        hot = jnp.where(row == 0, one, pick).astype(jnp.bfloat16)
        hot_lo = jnp.where(row == 0, 0.0, pick).astype(jnp.bfloat16)
        cols = pl.ds((i % 2) * 128, 128)
        table[i // 2, pl.ds(0, STEPS), cols] = past
        table[i // 2, pl.ds(STEPS, STEPS), cols] = past
        table[i // 2, pl.ds(2 * STEPS, STEPS), cols] = hot
        table[i // 2, pl.ds(3 * STEPS, STEPS), cols] = hot_lo

    def block_copy(b):
        other = (x * NC + core + 1 + b) % BLOCKS
        return pltpu.make_async_remote_copy(
            src_ref=sent.at[b],
            dst_ref=got.at[b],
            send_sem=send_sem.at[b],
            recv_sem=got_sem.at[b],
            device_id=(device_at(other // NC, y, z, other % NC),),
            device_id_type=MESH,
        )

    def one_block(step, carry):
        strikes = strike_values()
        other = (x * NC + core + 1 + step) % BLOCKS
        block = sets[other // NC, :, other % NC].reshape(BLOCK, 128)
        set_operands(block, lag_ref, rows_ref, ratio_ref, scale_ref)
        walk[...] = jnp.zeros_like(walk)
        for m in range(MATS):
            for q in range(4):
                pair = jnp.dot(
                    rows_ref[...], table[m * 4 + q], preferred_element_type=jnp.float32
                )
                for h in range(2):
                    i = m * 8 + q * 2 + h
                    vol = jnp.exp2(pair[:, h * 128 : (h + 1) * 128])
                    shock = ratio_ref[...] * noise[0, pl.ds(i, 1), :] + noise[1, pl.ds(i, 1), :]
                    walk[...] += vol * (shock - vol)
            spot = jnp.exp2((walk[...] * scale_ref[...]).T)
            for j in range(STRIKES):
                k = strikes[m][j]
                top = jnp.sum(jnp.maximum(spot, k).reshape(16, 8, BLOCK), axis=0)
                part[pl.ds(m * STRIKES + j, 1), :] = jnp.sum(top - 16.0 * k, axis=0, keepdims=True)
        sent[step] = part[...].T

        @pl.when(step == 0)
        def _():
            pl.semaphore_wait(pltpu.get_barrier_semaphore(), len(blocks + along_y + along_z))

        @pl.when(step < BLOCKS - 1)
        def _():
            block_copy(step).start()

        return carry

    lax.fori_loop(0, BLOCKS, one_block, 0)
    total = sent.at[BLOCKS - 1]
    for b in range(BLOCKS - 1):
        block_copy(b).wait_recv()
        total[...] += got[b]
    rows_y = NZ * OWN

    def y_rows(d):
        return pl.ds(pl.multiple_of(((y + d) % NY) * rows_y, rows_y), rows_y)

    copies = []
    for d in range(1, NY):
        copy = pltpu.make_async_remote_copy(
            src_ref=total.at[y_rows(d), :],
            dst_ref=got_y.at[d],
            send_sem=send_y.at[d],
            recv_sem=got_y_sem.at[d],
            device_id=(along_y[d - 1],),
            device_id_type=MESH,
        )
        copy.start()
        copies.append(copy)
    own = total[y_rows(0), :]
    for d in range(1, NY):
        copies[d - 1].wait_recv()
        own = own + got_y[d]
    got_y[0] = own

    def z_rows(d):
        return pl.ds(pl.multiple_of(((z + d) % NZ) * OWN, OWN), OWN)

    for d in range(1, NZ):
        copy = pltpu.make_async_remote_copy(
            src_ref=got_y.at[0, z_rows(d), :],
            dst_ref=got_z.at[d],
            send_sem=send_z.at[d],
            recv_sem=got_z_sem.at[d],
            device_id=(along_z[d - 1],),
            device_id_type=MESH,
        )
        copy.start()
        copies.append(copy)
    between(sets.at[x, y * NZ + z, core])
    final = got_y[0, z_rows(0), :]
    for d in range(1, NZ):
        copies[NY - 1 + d - 1].wait_recv()
        final = final + got_z[d]
    for b in range(BLOCKS - 1):
        block_copy(b).wait_send()
    for copy in copies:
        copy.wait_send()
    return final


WIDE = 1024
HALF = WIDE // NC
ROWS_A = WIDE // NX
ROWS_B = ROWS_A // NY
ROWS_Z = ROWS_B // NZ
SMALL = 16
SLICE = HALF // NX


ROWS = PAIRS * OWN
CHUNK = ROWS // 4
DEPTH = 768


def pair_table():
    tenors = (np.arange(MATS, dtype=np.float32) + np.float32(1.0)) / np.float32(MATS)
    offsets = np.arange(STRIKES, dtype=np.float32) - np.float32((STRIKES - 1) / 2.0)
    log_strike = np.float32(0.05) * offsets[None, :] * np.sqrt(tenors)[:, None]
    table = np.zeros((PAIRS, 128), np.float32)
    table[:, 4] = np.float32(4.0) * log_strike.reshape(PAIRS)
    table[:, 5] = np.repeat(tenors, STRIKES)
    table[:, 6] = 1.0
    return table


def forward_part(
    sets_ref, table_ref, w_in_ref, b_in_ref, w_mid_ref, b_mid_ref, w_out_ref, b_out_ref,
    feats, hid_in, slope_in, hid_mid, slope_mid, pred,
):
    f32, bf16 = jnp.float32, jnp.bfloat16
    pairs = CHUNK // OWN
    lane = lax.broadcasted_iota(jnp.int32, (OWN, 128), 1)
    factor = jnp.where(lane == 0, 4.0, jnp.where(lane == 3, 20.0, 1.0))
    scaled = (sets_ref[...] * factor)[None, :, :]
    w_out = w_out_ref[...].reshape(1, WIDE).astype(f32)
    for c in range(ROWS // CHUNK):
        rows = pl.ds(c * CHUNK, CHUNK)
        table = table_ref[pl.ds(c * pairs, pairs), :]
        x = (table[:, None, :] + scaled).reshape(CHUNK, 128).astype(bf16)
        feats[rows, :] = x
        raw = jnp.dot(x[:, :6], w_in_ref[...], preferred_element_type=f32) + b_in_ref[...]
        g = jax.nn.sigmoid(raw)
        hid = (raw * g).astype(bf16)
        hid_in[rows, :] = hid
        slope_in[rows, :] = g * (1.0 + raw * (1.0 - g))
        raw = jnp.dot(hid, w_mid_ref[...], preferred_element_type=f32) + b_mid_ref[...]
        g = jax.nn.sigmoid(raw)
        mid = (raw * g).astype(bf16)
        hid_mid[rows, :] = mid
        slope_mid[rows, :] = g * (1.0 + raw * (1.0 - g))
        pred[rows, :] = jnp.sum(mid.astype(f32) * w_out, axis=1, keepdims=True) + b_out_ref[0, 0]
    hid_in[pl.ds(ROWS, DEPTH - ROWS), :] = jnp.zeros((DEPTH - ROWS, WIDE), bf16)


def backward_part(
    prices, w_mid_ref, w_out_ref, small_ref,
    feats, hid_in, slope_in, hid_mid, slope_mid, pred, delta_mid, delta_in, hid_turn,
):
    f32, bf16 = jnp.float32, jnp.bfloat16
    pairs = CHUNK // OWN
    w_out = w_out_ref[...].reshape(1, WIDE).astype(f32)
    g_out = jnp.zeros((8, WIDE), f32)
    g_bmid = jnp.zeros((8, WIDE), f32)
    g_bin = jnp.zeros((8, WIDE), f32)
    g_bout = jnp.zeros((8, 1), f32)
    delta_mid[pl.ds(ROWS, DEPTH - ROWS), :] = jnp.zeros((DEPTH - ROWS, WIDE), bf16)
    for c in range(ROWS // CHUNK):
        rows = pl.ds(c * CHUNK, CHUNK)
        target = jnp.concatenate(
            [prices[:, k : k + 1] for k in range(c * pairs, (c + 1) * pairs)], axis=0
        )
        slope = (pred[rows, :] - target) * (1.0 / SETS)
        mid = hid_mid[rows, :].astype(f32)
        g_bout = g_bout + jnp.sum(slope.reshape(pairs, 8, 1), axis=0)
        g_out = g_out + jnp.sum((mid * slope).reshape(pairs, 8, WIDE), axis=0)
        delta = (slope * w_out * slope_mid[rows, :]).astype(bf16)
        delta_mid[rows, :] = delta
        g_bmid = g_bmid + jnp.sum(delta.astype(f32).reshape(pairs, 8, WIDE), axis=0)
        back = lax.dot_general(
            delta, w_mid_ref[...], (((1,), (1,)), ((), ())), preferred_element_type=f32
        )
        inner = (back * slope_in[rows, :]).astype(bf16)
        delta_in[rows, :] = inner
        g_bin = g_bin + jnp.sum(inner.astype(f32).reshape(pairs, 8, WIDE), axis=0)
    small_ref[pl.ds(0, 8), :] = lax.dot_general(
        feats[:, :8], delta_in[...], (((0,), (0,)), ((), ())), preferred_element_type=f32
    )
    small_ref[pl.ds(6, 1), :] = jnp.sum(g_bin, axis=0, keepdims=True)
    small_ref[pl.ds(7, 1), :] = jnp.sum(g_bmid, axis=0, keepdims=True)
    small_ref[pl.ds(8, 1), :] = jnp.sum(g_out, axis=0, keepdims=True)
    small_ref[pl.ds(9, 1), :] = jnp.broadcast_to(jnp.sum(g_bout, axis=0, keepdims=True), (1, WIDE))
    small_ref[pl.ds(10, 6), :] = jnp.zeros((6, WIDE), f32)


LATER = (2, 1, 3, 0)
SENDS = 100


def step_kernel(
    params_hbm,
    lag_hbm,
    inc_hbm,
    w_mid_hbm,
    table_hbm,
    w_in_hbm,
    b_in_hbm,
    b_mid_hbm,
    w_out_hbm,
    b_out_ref,
    prices_out,
    big_out,
    small_out,
    params_ref,
    lag_ref,
    inc_ref,
    w_mid_ref,
    table_ref,
    w_in_ref,
    b_in_ref,
    b_mid_ref,
    w_out_ref,
    load_sem,
    p_sets,
    p_rows_ref,
    p_ratio_ref,
    p_scale_ref,
    p_noise,
    p_table,
    p_walk,
    p_part,
    p_sent,
    p_got,
    p_got_y,
    p_got_z,
    p_send_sem,
    p_got_sem,
    p_send_y,
    p_got_y_sem,
    p_send_z,
    p_got_z_sem,
    small,
    feats,
    hid_in,
    slope_in,
    hid_mid,
    slope_mid,
    pred,
    delta_mid,
    delta_in,
    hid_turn,
    other,
    got_c,
    work,
    got_a,
    far_a,
    far_b,
    mid,
    got_b,
    low,
    got_z,
    s_got_c,
    s_got_a,
    s_b,
    s_z,
    s_sum,
    t_send_sem,
    t_recv_sem,
):
    x, y, z, core = coords(lax.axis_index("paths"))
    a = x * (1 - core) + y * core
    b = y * (1 - core) + x * core

    def at(aa, bb, zz):
        return device_at(aa * (1 - core) + bb * core, bb * (1 - core) + aa * core, zz, core)

    partner = device_at(x, y, z, 1 - core)
    along_a = [at((a + d) % NX, b, z) for d in range(1, NX)]
    along_b = [at(a, (b + d) % NY, z) for d in range(1, NY)]
    along_z = [at(a, b, (z + d) % NZ) for d in range(1, NZ)]
    barrier = pltpu.get_barrier_semaphore()
    for group in price_peers(x, y, z, core):
        for peer in group:
            pl.semaphore_signal(barrier, inc=1, device_id=(peer,), device_id_type=MESH)
    loads = []
    for k, (far, near) in enumerate(
        (
            (params_hbm, params_ref),
            (lag_hbm, lag_ref),
            (inc_hbm, inc_ref),
            (w_mid_hbm, w_mid_ref),
            (table_hbm, table_ref),
            (w_in_hbm, w_in_ref),
            (b_in_hbm, b_in_ref),
            (b_mid_hbm, b_mid_ref),
            (w_out_hbm, w_out_ref),
        )
    ):
        copy = pltpu.make_async_copy(far, near, load_sem.at[k])
        copy.start()
        loads.append(copy)
    for copy in loads[:3]:
        copy.wait()

    def forward(own):
        for copy in loads[3:]:
            copy.wait()
        forward_part(
            own, table_ref, w_in_ref, b_in_ref, w_mid_ref, b_mid_ref, w_out_ref, b_out_ref,
            feats, hid_in, slope_in, hid_mid, slope_mid, pred,
        )

    sums = prices_part(
        params_ref,
        lag_ref,
        inc_ref,
        forward,
        p_sets,
        p_rows_ref,
        p_ratio_ref,
        p_scale_ref,
        p_noise,
        p_table,
        p_walk,
        p_part,
        p_sent,
        p_got,
        p_got_y,
        p_got_z,
        p_send_sem,
        p_got_sem,
        p_send_y,
        p_got_y_sem,
        p_send_z,
        p_got_z_sem,
    )
    prices = sums[:, :PAIRS] / TOTAL_PATHS
    prices_out[...] = prices
    backward_part(
        prices, w_mid_ref, w_out_ref, small,
        feats, hid_in, slope_in, hid_mid, slope_mid, pred, delta_mid, delta_in, hid_turn,
    )
    hid_turn[...] = hid_in[...].T

    count = [0]
    started = []

    def send(src, dst, peer):
        k = count[0]
        count[0] += 1
        copy = pltpu.make_async_remote_copy(
            src_ref=src,
            dst_ref=dst,
            send_sem=t_send_sem.at[k],
            recv_sem=t_recv_sem.at[k],
            device_id=(peer,),
            device_id_type=MESH,
        )
        copy.start()
        started.append(copy)
        return copy

    def part(index, size):
        return pl.ds(pl.multiple_of(index * size, size), size)

    def rows_of(aa, bb):
        return part((aa % NX) * NY + bb % NY, ROWS_B)

    def product(first, second, e, cols):
        left = jnp.concatenate(
            [hid_turn[rows_of(first + d, second + e), :] for d in range(NX)], axis=0
        )
        out = jnp.dot(left, delta_mid[:, cols], preferred_element_type=jnp.float32)
        return out.reshape(NX, ROWS_B, HALF)

    own_cols, other_cols = part(core, HALF), part(1 - core, HALF)
    little = send(small.at[:, other_cols], s_got_c, partner)
    pair = {}
    for e in LATER:
        other[e] = product(b, a, e, other_cols)
        pair[e] = send(other.at[e], got_c.at[e], partner)
    little.wait_recv()
    s_got_c[...] += small[:, own_cols]
    littles = []
    for d in range(1, NX):
        littles.append(
            send(s_got_c.at[:, part((a + d) % NX, SLICE)], s_got_a.at[d - 1], along_a[d - 1])
        )
    near_a, near_b = [along_a[0], along_a[2]], [along_b[0], along_b[2]]
    top, bottom = pl.ds(0, ROWS_B // 2), pl.ds(ROWS_B // 2, ROWS_B // 2)
    steps, ahead = {}, {}
    for e in LATER:
        mine = product(a, b, e, own_cols)
        pair[e].wait_recv()
        work[e] = mine + got_c[e]
        ahead[e] = [
            send(work.at[e, 2, top], far_a.at[e, 0], near_a[0]),
            send(work.at[e, 2, bottom], far_a.at[e, 1], near_a[1]),
        ]
    for e in LATER:
        ahead[e][0].wait_recv()
        work[e, 1, top] += far_a[e, 0]
        steps[e] = [send(work.at[e, 1], got_a.at[e, 0], near_a[0])]
        ahead[e][1].wait_recv()
        work[e, 3, bottom] += far_a[e, 1]
        steps[e].append(send(work.at[e, 3], got_a.at[e, 1], near_a[1]))
    for copy in littles:
        copy.wait_recv()
    s_b[b] = s_got_c[:, part(a, SLICE)] + s_got_a[0] + s_got_a[1] + s_got_a[2]
    littles = [send(s_b.at[b], s_b.at[b], peer) for peer in along_b]
    for e in LATER:
        for copy in steps[e]:
            copy.wait_recv()
        mid[e] = work[e, 0] + got_a[e, 0] + got_a[e, 1]
        if e == 2:
            beyond = [
                send(mid.at[2, top], far_b.at[0], near_b[0]),
                send(mid.at[2, bottom], far_b.at[1], near_b[1]),
            ]
    beyond[0].wait_recv()
    mid[1, top] += far_b[0]
    across = [send(mid.at[1], got_b.at[0], near_b[0])]
    beyond[1].wait_recv()
    mid[3, bottom] += far_b[1]
    across.append(send(mid.at[3], got_b.at[1], near_b[1]))
    for copy in littles:
        copy.wait_recv()
    s_z[z] = (s_b[0] + s_b[1]) + (s_b[2] + s_b[3])
    littles = [send(s_z.at[z], s_z.at[z], peer) for peer in along_z]
    for copy in across:
        copy.wait_recv()
    low[...] = mid[0] + got_b[0] + got_b[1]
    deep = [
        send(low.at[part((z + d) % NZ, ROWS_Z), :], got_z.at[d - 1], along_z[d - 1])
        for d in range(1, NZ)
    ]
    for copy in littles:
        copy.wait_recv()
    s_all = ((s_z[0] + s_z[1]) + (s_z[2] + s_z[3])) + ((s_z[4] + s_z[5]) + (s_z[6] + s_z[7]))
    s_sum[:, part(a, SLICE)] = s_all
    littles = [
        send(s_sum.at[:, part(a, SLICE)], s_sum.at[:, part(a, SLICE)], peer) for peer in along_a
    ]
    final = low[part(z, ROWS_Z), :]
    for d in range(1, NZ):
        deep[d - 1].wait_recv()
        final = final + got_z[d - 1]

    half_out = big_out.at[core]
    mine = part((a * NY + b) * NZ + z, ROWS_Z)
    half_out[mine, :] = final
    deep = [send(half_out.at[mine, :], half_out.at[mine, :], peer) for peer in along_z]
    for copy in littles:
        copy.wait_recv()
    small_out[core] = s_sum[...]
    little = send(small_out.at[core], small_out.at[core], partner)
    for copy in deep:
        copy.wait_recv()

    def spread(rows, targets):
        return [send(half_out.at[rows, :], half_out.at[rows, :], peer) for peer in targets]

    def top_of(aa, bb):
        return part(((aa % NX) * NY + bb % NY) * 2, ROWS_B // 2)

    def bottom_of(aa, bb):
        return part(((aa % NX) * NY + bb % NY) * 2 + 1, ROWS_B // 2)

    near_a, near_b = [along_a[0], along_a[2]], [along_b[0], along_b[2]]
    across = spread(rows_of(a, b), near_b)
    steps = [spread(rows_of(a, b), near_a)]
    pairs = spread(rows_of(a, b), [partner])
    relays_b, relays_a = [], {}

    def pass_on(e, bb):
        steps[e][0].wait_recv()
        first = spread(top_of(a + 3, bb), near_a[:1])
        pairs.extend(spread(rows_of(a + 3, bb), [partner]))
        steps[e][1].wait_recv()
        second = spread(bottom_of(a + 1, bb), near_a[1:])
        pairs.extend(spread(rows_of(a + 1, bb), [partner]))
        relays_a[e] = first + second

    across[0].wait_recv()
    relays_b += spread(top_of(a, b + 3), near_b[:1])
    steps.append(spread(rows_of(a, b + 3), near_a))
    across[1].wait_recv()
    relays_b += spread(bottom_of(a, b + 1), near_b[1:])
    steps.append(spread(rows_of(a, b + 1), near_a))
    pairs += spread(rows_of(a, b + 3), [partner]) + spread(rows_of(a, b + 1), [partner])
    pass_on(0, b)
    for copy in relays_b:
        copy.wait_recv()
    steps.append(spread(rows_of(a, b + 2), near_a))
    pairs += spread(rows_of(a, b + 2), [partner])
    pass_on(1, b + 3)
    pass_on(2, b + 1)
    pass_on(3, b + 2)
    for e, bb in enumerate((b, b + 3, b + 1, b + 2)):
        for copy in relays_a[e]:
            copy.wait_recv()
        pairs += spread(rows_of(a + 2, bb), [partner])
    little.wait_recv()
    for copy in pairs:
        copy.wait_recv()
    for copy in started:
        copy.wait_send()


def train(params, increments, w_in, b_in, w_mid, b_mid, w_out, b_out):
    f32, bf16 = jnp.float32, jnp.bfloat16
    vmem = pl.BlockSpec(memory_space=pltpu.VMEM)
    smem = pl.BlockSpec(memory_space=pltpu.SMEM)
    hbm = pl.BlockSpec(memory_space=pltpu.HBM)
    loads = [
        params.T,
        jnp.asarray(lag_tables()),
        increments,
        w_mid,
        jnp.asarray(pair_table()),
        w_in,
        b_in.reshape(1, WIDE),
        b_mid.reshape(1, WIDE),
        w_out,
    ]
    return pl.pallas_call(
        step_kernel,
        in_specs=[hbm] * 9 + [smem],
        out_specs=[vmem, vmem, vmem],
        out_shape=[
            jax.ShapeDtypeStruct((OWN, PAIRS), f32),
            jax.ShapeDtypeStruct((NC, WIDE, HALF), f32),
            jax.ShapeDtypeStruct((NC, SMALL, HALF), f32),
        ],
        scratch_shapes=[
            pltpu.VMEM((4, SETS), f32),
            pltpu.VMEM((8, 128), f32),
            pltpu.VMEM((2, STEPS, 128), bf16),
            pltpu.VMEM((WIDE, WIDE), bf16),
            pltpu.VMEM((PAIRS, 128), f32),
            pltpu.VMEM((6, WIDE), bf16),
            pltpu.VMEM((1, WIDE), f32),
            pltpu.VMEM((1, WIDE), f32),
            pltpu.VMEM((WIDE,), bf16),
            pltpu.SemaphoreType.DMA((9,)),
            pltpu.VMEM((NX, NY * NZ, NC, OWN, 128), f32),
            pltpu.VMEM((BLOCK, 256), bf16),
            pltpu.VMEM((BLOCK, 128), f32),
            pltpu.VMEM((BLOCK, 128), f32),
            pltpu.VMEM((2, STEPS, 128), f32),
            pltpu.VMEM((STEPS // 2, 256, 256), bf16),
            pltpu.VMEM((BLOCK, 128), f32),
            pltpu.VMEM((128, BLOCK), f32),
            pltpu.VMEM((BLOCKS, BLOCK, 128), f32),
            pltpu.VMEM((BLOCKS - 1, BLOCK, 128), f32),
            pltpu.VMEM((NY, NZ * OWN, 128), f32),
            pltpu.VMEM((NZ, OWN, 128), f32),
            pltpu.SemaphoreType.DMA((BLOCKS,)),
            pltpu.SemaphoreType.DMA((BLOCKS,)),
            pltpu.SemaphoreType.DMA((NY,)),
            pltpu.SemaphoreType.DMA((NY,)),
            pltpu.SemaphoreType.DMA((NZ,)),
            pltpu.SemaphoreType.DMA((NZ,)),
            pltpu.VMEM((SMALL, WIDE), f32),
            pltpu.VMEM((ROWS, 128), bf16),
            pltpu.VMEM((DEPTH, WIDE), bf16),
            pltpu.VMEM((ROWS, WIDE), f32),
            pltpu.VMEM((ROWS, WIDE), bf16),
            pltpu.VMEM((ROWS, WIDE), f32),
            pltpu.VMEM((ROWS, 1), f32),
            pltpu.VMEM((DEPTH, WIDE), bf16),
            pltpu.VMEM((ROWS, WIDE), bf16),
            pltpu.VMEM((WIDE, DEPTH), bf16),
            pltpu.VMEM((NY, NX, ROWS_B, HALF), f32),
            pltpu.VMEM((NY, NX, ROWS_B, HALF), f32),
            pltpu.VMEM((NY, NX, ROWS_B, HALF), f32),
            pltpu.VMEM((NY, 2, ROWS_B, HALF), f32),
            pltpu.VMEM((NY, 2, ROWS_B // 2, HALF), f32),
            pltpu.VMEM((2, ROWS_B // 2, HALF), f32),
            pltpu.VMEM((NY, ROWS_B, HALF), f32),
            pltpu.VMEM((2, ROWS_B, HALF), f32),
            pltpu.VMEM((ROWS_B, HALF), f32),
            pltpu.VMEM((NZ - 1, ROWS_Z, HALF), f32),
            pltpu.VMEM((SMALL, HALF), f32),
            pltpu.VMEM((NX - 1, SMALL, SLICE), f32),
            pltpu.VMEM((NY, SMALL, SLICE), f32),
            pltpu.VMEM((NZ, SMALL, SLICE), f32),
            pltpu.VMEM((SMALL, HALF), f32),
            pltpu.SemaphoreType.DMA((SENDS,)),
            pltpu.SemaphoreType.DMA((SENDS,)),
        ],
        compiler_params=pltpu.CompilerParams(
            collective_id=0, has_side_effects=True, vmem_limit_bytes=46 * 1024 * 1024
        ),
        name="step",
    )(
        *[pltpu.with_memory_space_constraint(value, pltpu.HBM) for value in loads],
        b_out.reshape(1, 1),
    )


def finish_kernel(
    prices_ref,
    big_ref,
    small_ref,
    prices_out,
    w_in_out,
    b_in_out,
    w_mid_out,
    b_mid_out,
    w_out_out,
    b_out_out,
):
    prices_out[...] = prices_ref[...]

    def factor(total, entries):
        return lax.rsqrt(total * (1.0 / entries) + EPSILON)

    def sumsq(value):
        return jnp.sum(jnp.sum(value * value, axis=1, keepdims=True), axis=0, keepdims=True)

    small = jnp.concatenate([small_ref[0], small_ref[1]], axis=1)
    g_bout = small[9:10, 0:1]
    s_mid = sumsq(small[7:8])
    for k in range(8):
        for c in range(NC):
            s_mid = s_mid + sumsq(big_ref[c, pl.ds(k * 128, 128), :])
    f_in = factor(sumsq(small[0:7]), 7 * WIDE)
    f_mid = factor(s_mid, (WIDE + 1) * WIDE)
    f_out = factor(sumsq(small[8:9]) + g_bout * g_bout, WIDE + 1)
    w_in_out[...] = small[0:6] * f_in
    b_in_out[...] = small[6:7] * f_in
    b_mid_out[...] = small[7:8] * f_mid
    w_out_out[...] = small[8:9] * f_out
    b_out_out[...] = g_bout * f_out
    for c in range(NC):
        w_mid_out[:, pl.ds(c * HALF, HALF)] = big_ref[c] * f_mid


def finish(prices, big, small):
    f32 = jnp.float32
    vmem = pl.BlockSpec(memory_space=pltpu.VMEM)
    shapes = [(OWN, PAIRS), (6, WIDE), (1, WIDE), (WIDE, WIDE), (1, WIDE), (1, WIDE), (1, 1)]
    prices, w_in, b_in, w_mid, b_mid, w_out, b_out = pl.pallas_call(
        finish_kernel,
        in_specs=[vmem] * 3,
        out_specs=[vmem] * 7,
        out_shape=[jax.ShapeDtypeStruct(shape, f32) for shape in shapes],
        compiler_params=pltpu.CompilerParams(vmem_limit_bytes=16 * 1024 * 1024), name="finish",
    )(prices, big, small)
    b_in, b_mid, w_out = b_in.reshape(WIDE), b_mid.reshape(WIDE), w_out.reshape(WIDE)
    return prices, w_in, b_in, w_mid, b_mid, w_out, b_out.reshape(1)


def on_device(params, increments, w_in, b_in, w_mid, b_mid, w_out, b_out):
    prices, big, small = train(params, increments, w_in, b_in, w_mid, b_mid, w_out, b_out)
    return finish(prices, big, small)


def solution(mesh):
    in_specs = (P(), P(None, None, "paths"), P(), P(), P(), P(), P(), P())
    out_specs = (P("paths", None), P(), P(), P(), P(), P(), P())
    return jax.shard_map(
        on_device, mesh=mesh, in_specs=in_specs, out_specs=out_specs, check_vma=False
    )
```

```python
import math

import jax
import jax.numpy as jnp
import numpy as np
from jax import lax
from jax.experimental import pallas as pl
from jax.experimental.pallas import tpu as pltpu
from jax.sharding import PartitionSpec as P

STEPS = 64
MATS = 8
STRIKES = 11
PAIRS = 88
EPSILON = 1e-06
LOG2E = 1.4426950408889634
NX, NY, NZ, NC = 4, 4, 8, 2
OWN = 8
BLOCK = NY * NZ * OWN
BLOCKS = NX * NC
SETS = 2048
TOTAL_PATHS = 32768
MESH = pl.DeviceIdType.MESH


def strike_values():
    return [
        [math.exp(0.05 * (j - 5) * math.sqrt((m + 1) / MATS)) for j in range(STRIKES)]
        for m in range(MATS)
    ]


def coords(index):
    core = index % NC
    z = (index // NC) % NZ
    y = (index // (NC * NZ)) % NY
    x = index // (NC * NZ * NY)
    return x, y, z, core


def device_at(x, y, z, core):
    return ((x * NY + y) * NZ + z) * NC + core


def lag_tables():
    lag = np.tile(np.arange(STEPS, dtype=np.float64), 2)
    table = np.zeros((8, 128), np.float32)
    table[0] = np.log2(np.maximum(lag, 1.0))
    table[1] = np.log2(np.maximum(lag - 1.0, 1.0))
    table[2] = np.log2(np.maximum(lag, 1.0) / STEPS)
    return table


def set_operands(sets, lag_ref, rows, ratio, scale):
    f32, bf16 = jnp.float32, jnp.bfloat16
    shape = (sets.shape[0], 128)
    hurst, vol, correl, forward = (
        jnp.broadcast_to(sets[:, k : k + 1], shape) for k in range(4)
    )
    lane = lax.broadcasted_iota(jnp.int32, shape, 1)
    upper = lane >= STEPS
    lag = jnp.where(upper, lane - STEPS, lane)
    expo = hurst + 0.5
    late = jnp.where(lag >= 2, jnp.exp2(expo * lag_ref[1:2, :]), 0.0)
    powers = jnp.exp2(expo * lag_ref[0:1, :]) - late
    front = jnp.sqrt(2.0 * hurst) * jnp.exp2(-6.0 * hurst) / expo
    kern = jnp.where(lag >= 1, powers * front, 0.0).astype(bf16).astype(f32)
    half = (0.5 * LOG2E) * vol
    weight = kern * half
    comp = (-0.5 * vol * half) * jnp.exp2((2.0 * hurst) * lag_ref[2:3, :])
    rest = 1.0 - correl * correl
    const = (0.5 * LOG2E) * jnp.log(forward * (1.0 / STEPS) / rest) - 1.0
    w_hi = weight.astype(bf16).astype(f32)
    c_hi = comp.astype(bf16).astype(f32)
    k_hi = const.astype(bf16).astype(f32)
    k_rest = const - k_hi
    k_lo = k_rest.astype(bf16).astype(f32)
    first = lag == 0
    kern_row = jnp.where(first, jnp.where(upper, k_lo, k_hi), jnp.where(upper, weight - w_hi, w_hi))
    comp_row = jnp.where(
        first, jnp.where(upper, 0.0, k_rest - k_lo), jnp.where(upper, comp - c_hi, c_hi)
    )
    rows[:, 0:128] = kern_row.astype(bf16)
    rows[:, 128:256] = comp_row.astype(bf16)
    ratio[...] = correl * lax.rsqrt(rest)
    scale[...] = (2.0 * LOG2E) * rest


def price_peers(x, y, z, core):
    mine = x * NC + core
    blocks = []
    for b in range(BLOCKS - 1):
        other = (mine + 1 + b) % BLOCKS
        blocks.append(device_at(other // NC, y, z, other % NC))
    along_y = [device_at(x, (y + d) % NY, z, core) for d in range(1, NY)]
    along_z = [device_at(x, y, (z + d) % NZ, core) for d in range(1, NZ)]
    return blocks, along_y, along_z


def prices_part(
    params_ref,
    lag_ref,
    inc_ref,
    between,
    sets,
    rows_ref,
    ratio_ref,
    scale_ref,
    noise,
    table,
    walk,
    part,
    sent,
    got,
    got_y,
    got_z,
    send_sem,
    got_sem,
    send_y,
    got_y_sem,
    send_z,
    got_z_sem,
):
    x, y, z, core = coords(lax.axis_index("paths"))
    blocks, along_y, along_z = price_peers(x, y, z, core)
    for k in range(NX * NY):
        some = params_ref[:, pl.ds(k * 128, 128)]
        some = jnp.concatenate([some, jnp.zeros((124, 128), jnp.float32)], axis=0).T
        sets[k // NY, pl.ds((k % NY) * NZ, NZ)] = some.reshape(NZ, NC, OWN, 128)
    noise[0] = inc_ref[0].astype(jnp.float32)
    noise[1] = inc_ref[1].astype(jnp.float32)
    part[...] = jnp.zeros_like(part)
    row = lax.broadcasted_iota(jnp.int32, (STEPS, 128), 0)
    for j in range(STEPS):
        walk[pl.ds(STEPS - 1 - j, 1), :] = noise[0, pl.ds(j, 1), :]
    walk[pl.ds(STEPS, STEPS), :] = jnp.zeros((STEPS, 128), jnp.float32)
    one = jnp.ones((STEPS, 128), jnp.float32)
    for i in range(STEPS):
        past = walk[pl.ds(STEPS - 1 - i, STEPS), :]
        past = jnp.where(row == 0, one, past).astype(jnp.bfloat16)
        pick = jnp.where(row == i, 1.0, 0.0)
        hot = jnp.where(row == 0, one, pick).astype(jnp.bfloat16)
        hot_lo = jnp.where(row == 0, 0.0, pick).astype(jnp.bfloat16)
        cols = pl.ds((i % 2) * 128, 128)
        table[i // 2, pl.ds(0, STEPS), cols] = past
        table[i // 2, pl.ds(STEPS, STEPS), cols] = past
        table[i // 2, pl.ds(2 * STEPS, STEPS), cols] = hot
        table[i // 2, pl.ds(3 * STEPS, STEPS), cols] = hot_lo

    def block_copy(b):
        other = (x * NC + core + 1 + b) % BLOCKS
        return pltpu.make_async_remote_copy(
            src_ref=sent.at[b],
            dst_ref=got.at[b],
            send_sem=send_sem.at[b],
            recv_sem=got_sem.at[b],
            device_id=(device_at(other // NC, y, z, other % NC),),
            device_id_type=MESH,
        )

    def one_block(step, carry):
        strikes = strike_values()
        other = (x * NC + core + 1 + step) % BLOCKS
        block = sets[other // NC, :, other % NC].reshape(BLOCK, 128)
        set_operands(block, lag_ref, rows_ref, ratio_ref, scale_ref)
        walk[...] = jnp.zeros_like(walk)
        for m in range(MATS):
            for q in range(4):
                pair = jnp.dot(
                    rows_ref[...], table[m * 4 + q], preferred_element_type=jnp.float32
                )
                for h in range(2):
                    i = m * 8 + q * 2 + h
                    vol = jnp.exp2(pair[:, h * 128 : (h + 1) * 128])
                    shock = ratio_ref[...] * noise[0, pl.ds(i, 1), :] + noise[1, pl.ds(i, 1), :]
                    walk[...] += vol * (shock - vol)
            spot = jnp.exp2((walk[...] * scale_ref[...]).T)
            for j in range(STRIKES):
                k = strikes[m][j]
                top = jnp.sum(jnp.maximum(spot, k).reshape(16, 8, BLOCK), axis=0)
                part[pl.ds(m * STRIKES + j, 1), :] = jnp.sum(top - 16.0 * k, axis=0, keepdims=True)
        sent[step] = part[...].T

        @pl.when(step == 0)
        def _():
            pl.semaphore_wait(pltpu.get_barrier_semaphore(), len(blocks + along_y + along_z))

        @pl.when(step < BLOCKS - 1)
        def _():
            block_copy(step).start()

        return carry

    lax.fori_loop(0, BLOCKS, one_block, 0)
    total = sent.at[BLOCKS - 1]
    for b in range(BLOCKS - 1):
        block_copy(b).wait_recv()
        total[...] += got[b]
    rows_y = NZ * OWN

    def y_rows(d):
        return pl.ds(pl.multiple_of(((y + d) % NY) * rows_y, rows_y), rows_y)

    copies = []
    for d in range(1, NY):
        copy = pltpu.make_async_remote_copy(
            src_ref=total.at[y_rows(d), :],
            dst_ref=got_y.at[d],
            send_sem=send_y.at[d],
            recv_sem=got_y_sem.at[d],
            device_id=(along_y[d - 1],),
            device_id_type=MESH,
        )
        copy.start()
        copies.append(copy)
    own = total[y_rows(0), :]
    for d in range(1, NY):
        copies[d - 1].wait_recv()
        own = own + got_y[d]
    got_y[0] = own

    def z_rows(d):
        return pl.ds(pl.multiple_of(((z + d) % NZ) * OWN, OWN), OWN)

    for d in range(1, NZ):
        copy = pltpu.make_async_remote_copy(
            src_ref=got_y.at[0, z_rows(d), :],
            dst_ref=got_z.at[d],
            send_sem=send_z.at[d],
            recv_sem=got_z_sem.at[d],
            device_id=(along_z[d - 1],),
            device_id_type=MESH,
        )
        copy.start()
        copies.append(copy)
    between(sets.at[x, y * NZ + z, core])
    final = got_y[0, z_rows(0), :]
    for d in range(1, NZ):
        copies[NY - 1 + d - 1].wait_recv()
        final = final + got_z[d]
    for b in range(BLOCKS - 1):
        block_copy(b).wait_send()
    for copy in copies:
        copy.wait_send()
    return final


WIDE = 1024
HALF = WIDE // NC
ROWS_A = WIDE // NX
ROWS_B = ROWS_A // NY
ROWS_Z = ROWS_B // NZ
SMALL = 16
SLICE = HALF // NX


ROWS = PAIRS * OWN
CHUNK = ROWS // 2
DEPTH = 768


def pair_table():
    tenors = (np.arange(MATS, dtype=np.float32) + np.float32(1.0)) / np.float32(MATS)
    offsets = np.arange(STRIKES, dtype=np.float32) - np.float32((STRIKES - 1) / 2.0)
    log_strike = np.float32(0.05) * offsets[None, :] * np.sqrt(tenors)[:, None]
    table = np.zeros((PAIRS, 128), np.float32)
    table[:, 4] = np.float32(4.0) * log_strike.reshape(PAIRS)
    table[:, 5] = np.repeat(tenors, STRIKES)
    table[:, 6] = 1.0
    return table


def forward_part(
    sets_ref, table_ref, w_in_ref, b_in_ref, w_mid_ref, b_mid_ref, w_out_ref, b_out_ref,
    feats, hid_in, slope_in, hid_mid, slope_mid, pred, hid_turn,
):
    f32, bf16 = jnp.float32, jnp.bfloat16
    pairs = CHUNK // OWN
    lane = lax.broadcasted_iota(jnp.int32, (OWN, 128), 1)
    factor = jnp.where(lane == 0, 4.0, jnp.where(lane == 3, 20.0, 1.0))
    scaled = (sets_ref[...] * factor)[None, :, :]
    w_out = w_out_ref[...].reshape(1, WIDE).astype(f32)
    for c in range(ROWS // CHUNK):
        rows = pl.ds(c * CHUNK, CHUNK)
        table = table_ref[pl.ds(c * pairs, pairs), :]
        x = (table[:, None, :] + scaled).reshape(CHUNK, 128).astype(bf16)
        feats[rows, :] = x
        raw = jnp.dot(x[:, :6], w_in_ref[...], preferred_element_type=f32) + b_in_ref[...]
        g = jax.nn.sigmoid(raw)
        hid = (raw * g).astype(bf16)
        hid_in[rows, :] = hid
        slope_in[rows, :] = g * (1.0 + raw * (1.0 - g))
        raw = jnp.dot(hid, w_mid_ref[...], preferred_element_type=f32) + b_mid_ref[...]
        g = jax.nn.sigmoid(raw)
        mid = (raw * g).astype(bf16)
        hid_mid[rows, :] = mid
        slope_mid[rows, :] = g * (1.0 + raw * (1.0 - g))
        pred[rows, :] = jnp.sum(mid.astype(f32) * w_out, axis=1, keepdims=True) + b_out_ref[0, 0]
    hid_in[pl.ds(ROWS, DEPTH - ROWS), :] = jnp.zeros((DEPTH - ROWS, WIDE), bf16)
    hid_turn[...] = hid_in[...].T


def backward_part(
    prices, w_mid_ref, w_out_ref, small_ref,
    feats, hid_in, slope_in, hid_mid, slope_mid, pred, delta_mid, delta_in,
):
    f32, bf16 = jnp.float32, jnp.bfloat16
    pairs = CHUNK // OWN
    w_out = w_out_ref[...].reshape(1, WIDE).astype(f32)
    g_out = jnp.zeros((8, WIDE), f32)
    g_bmid = jnp.zeros((8, WIDE), f32)
    g_bin = jnp.zeros((8, WIDE), f32)
    g_bout = jnp.zeros((8, 1), f32)
    delta_mid[pl.ds(ROWS, DEPTH - ROWS), :] = jnp.zeros((DEPTH - ROWS, WIDE), bf16)
    for c in range(ROWS // CHUNK):
        rows = pl.ds(c * CHUNK, CHUNK)
        target = jnp.concatenate(
            [prices[:, k : k + 1] for k in range(c * pairs, (c + 1) * pairs)], axis=0
        )
        slope = (pred[rows, :] - target) * (1.0 / SETS)
        mid = hid_mid[rows, :].astype(f32)
        g_bout = g_bout + jnp.sum(slope.reshape(pairs, 8, 1), axis=0)
        g_out = g_out + jnp.sum((mid * slope).reshape(pairs, 8, WIDE), axis=0)
        delta = (slope * w_out * slope_mid[rows, :]).astype(bf16)
        delta_mid[rows, :] = delta
        g_bmid = g_bmid + jnp.sum(delta.astype(f32).reshape(pairs, 8, WIDE), axis=0)
        back = lax.dot_general(
            delta, w_mid_ref[...], (((1,), (1,)), ((), ())), preferred_element_type=f32
        )
        inner = (back * slope_in[rows, :]).astype(bf16)
        delta_in[rows, :] = inner
        g_bin = g_bin + jnp.sum(inner.astype(f32).reshape(pairs, 8, WIDE), axis=0)
    small_ref[pl.ds(0, 8), :] = lax.dot_general(
        feats[:, :8], delta_in[...], (((0,), (0,)), ((), ())), preferred_element_type=f32
    )
    small_ref[pl.ds(6, 1), :] = jnp.sum(g_bin, axis=0, keepdims=True)
    small_ref[pl.ds(7, 1), :] = jnp.sum(g_bmid, axis=0, keepdims=True)
    small_ref[pl.ds(8, 1), :] = jnp.sum(g_out, axis=0, keepdims=True)
    small_ref[pl.ds(9, 1), :] = jnp.broadcast_to(jnp.sum(g_bout, axis=0, keepdims=True), (1, WIDE))
    small_ref[pl.ds(10, 6), :] = jnp.zeros((6, WIDE), f32)


LATER = (2, 1, 3, 0)
SENDS = 100


def step_kernel(
    params_hbm,
    lag_hbm,
    inc_hbm,
    w_mid_hbm,
    table_hbm,
    w_in_hbm,
    b_in_hbm,
    b_mid_hbm,
    w_out_hbm,
    b_out_ref,
    prices_out,
    big_out,
    small_out,
    params_ref,
    lag_ref,
    inc_ref,
    w_mid_ref,
    table_ref,
    w_in_ref,
    b_in_ref,
    b_mid_ref,
    w_out_ref,
    load_sem,
    p_sets,
    p_rows_ref,
    p_ratio_ref,
    p_scale_ref,
    p_noise,
    p_table,
    p_walk,
    p_part,
    p_sent,
    p_got,
    p_got_y,
    p_got_z,
    p_send_sem,
    p_got_sem,
    p_send_y,
    p_got_y_sem,
    p_send_z,
    p_got_z_sem,
    small,
    feats,
    hid_in,
    slope_in,
    hid_mid,
    slope_mid,
    pred,
    delta_mid,
    delta_in,
    hid_turn,
    other,
    got_c,
    work,
    got_a,
    far_a,
    far_b,
    mid,
    got_b,
    low,
    got_z,
    s_got_c,
    s_got_a,
    s_b,
    s_z,
    s_sum,
    t_send_sem,
    t_recv_sem,
):
    x, y, z, core = coords(lax.axis_index("paths"))
    a = x * (1 - core) + y * core
    b = y * (1 - core) + x * core

    def at(aa, bb, zz):
        return device_at(aa * (1 - core) + bb * core, bb * (1 - core) + aa * core, zz, core)

    partner = device_at(x, y, z, 1 - core)
    along_a = [at((a + d) % NX, b, z) for d in range(1, NX)]
    along_b = [at(a, (b + d) % NY, z) for d in range(1, NY)]
    along_z = [at(a, b, (z + d) % NZ) for d in range(1, NZ)]
    barrier = pltpu.get_barrier_semaphore()
    for group in price_peers(x, y, z, core):
        for peer in group:
            pl.semaphore_signal(barrier, inc=1, device_id=(peer,), device_id_type=MESH)
    loads = []
    for k, (far, near) in enumerate(
        (
            (params_hbm, params_ref),
            (lag_hbm, lag_ref),
            (inc_hbm, inc_ref),
            (w_mid_hbm, w_mid_ref),
            (table_hbm, table_ref),
            (w_in_hbm, w_in_ref),
            (b_in_hbm, b_in_ref),
            (b_mid_hbm, b_mid_ref),
            (w_out_hbm, w_out_ref),
        )
    ):
        copy = pltpu.make_async_copy(far, near, load_sem.at[k])
        copy.start()
        loads.append(copy)
    for copy in loads[:3]:
        copy.wait()

    def forward(own):
        for copy in loads[3:]:
            copy.wait()
        forward_part(
            own, table_ref, w_in_ref, b_in_ref, w_mid_ref, b_mid_ref, w_out_ref, b_out_ref,
            feats, hid_in, slope_in, hid_mid, slope_mid, pred, hid_turn,
        )

    sums = prices_part(
        params_ref,
        lag_ref,
        inc_ref,
        forward,
        p_sets,
        p_rows_ref,
        p_ratio_ref,
        p_scale_ref,
        p_noise,
        p_table,
        p_walk,
        p_part,
        p_sent,
        p_got,
        p_got_y,
        p_got_z,
        p_send_sem,
        p_got_sem,
        p_send_y,
        p_got_y_sem,
        p_send_z,
        p_got_z_sem,
    )
    prices = sums[:, :PAIRS] / TOTAL_PATHS
    prices_out[...] = prices
    backward_part(
        prices, w_mid_ref, w_out_ref, small,
        feats, hid_in, slope_in, hid_mid, slope_mid, pred, delta_mid, delta_in,
    )

    count = [0]
    started = []

    def send(src, dst, peer):
        k = count[0]
        count[0] += 1
        copy = pltpu.make_async_remote_copy(
            src_ref=src,
            dst_ref=dst,
            send_sem=t_send_sem.at[k],
            recv_sem=t_recv_sem.at[k],
            device_id=(peer,),
            device_id_type=MESH,
        )
        copy.start()
        started.append(copy)
        return copy

    def part(index, size):
        return pl.ds(pl.multiple_of(index * size, size), size)

    def rows_of(aa, bb):
        return part((aa % NX) * NY + bb % NY, ROWS_B)

    def product(first, second, e, cols):
        left = jnp.concatenate(
            [hid_turn[rows_of(first + d, second + e), :] for d in range(NX)], axis=0
        )
        out = jnp.dot(left, delta_mid[:, cols], preferred_element_type=jnp.float32)
        return out.reshape(NX, ROWS_B, HALF)

    own_cols, other_cols = part(core, HALF), part(1 - core, HALF)
    little = send(small.at[:, other_cols], s_got_c, partner)
    pair = {}
    for e in LATER:
        other[e] = product(b, a, e, other_cols)
        pair[e] = send(other.at[e], got_c.at[e], partner)
    little.wait_recv()
    s_got_c[...] += small[:, own_cols]
    littles = []
    for d in range(1, NX):
        littles.append(
            send(s_got_c.at[:, part((a + d) % NX, SLICE)], s_got_a.at[d - 1], along_a[d - 1])
        )
    near_a, near_b = [along_a[0], along_a[2]], [along_b[0], along_b[2]]
    top, bottom = pl.ds(0, ROWS_B // 2), pl.ds(ROWS_B // 2, ROWS_B // 2)
    steps, ahead = {}, {}
    for e in LATER:
        mine = product(a, b, e, own_cols)
        pair[e].wait_recv()
        work[e] = mine + got_c[e]
        ahead[e] = [
            send(work.at[e, 2, top], far_a.at[e, 0], near_a[0]),
            send(work.at[e, 2, bottom], far_a.at[e, 1], near_a[1]),
        ]
    for e in LATER:
        ahead[e][0].wait_recv()
        work[e, 1, top] += far_a[e, 0]
        steps[e] = [send(work.at[e, 1], got_a.at[e, 0], near_a[0])]
        ahead[e][1].wait_recv()
        work[e, 3, bottom] += far_a[e, 1]
        steps[e].append(send(work.at[e, 3], got_a.at[e, 1], near_a[1]))
    for copy in littles:
        copy.wait_recv()
    s_b[b] = s_got_c[:, part(a, SLICE)] + s_got_a[0] + s_got_a[1] + s_got_a[2]
    littles = [send(s_b.at[b], s_b.at[b], peer) for peer in along_b]
    def collect(e):
        for copy in steps[e]:
            copy.wait_recv()
        mid[e] = work[e, 0] + got_a[e, 0] + got_a[e, 1]

    collect(2)
    beyond = [
        send(mid.at[2, top], far_b.at[0], near_b[0]),
        send(mid.at[2, bottom], far_b.at[1], near_b[1]),
    ]
    collect(1)
    beyond[0].wait_recv()
    mid[1, top] += far_b[0]
    across = [send(mid.at[1], got_b.at[0], near_b[0])]
    collect(3)
    beyond[1].wait_recv()
    mid[3, bottom] += far_b[1]
    across.append(send(mid.at[3], got_b.at[1], near_b[1]))
    collect(0)
    for copy in littles:
        copy.wait_recv()
    s_z[z] = (s_b[0] + s_b[1]) + (s_b[2] + s_b[3])
    littles = [send(s_z.at[z], s_z.at[z], peer) for peer in along_z]
    for copy in across:
        copy.wait_recv()
    low[...] = mid[0] + got_b[0] + got_b[1]
    deep = [
        send(low.at[part((z + d) % NZ, ROWS_Z), :], got_z.at[d - 1], along_z[d - 1])
        for d in range(1, NZ)
    ]
    for copy in littles:
        copy.wait_recv()
    s_all = ((s_z[0] + s_z[1]) + (s_z[2] + s_z[3])) + ((s_z[4] + s_z[5]) + (s_z[6] + s_z[7]))
    s_sum[:, part(a, SLICE)] = s_all
    littles = [
        send(s_sum.at[:, part(a, SLICE)], s_sum.at[:, part(a, SLICE)], peer) for peer in along_a
    ]
    final = low[part(z, ROWS_Z), :]
    for d in range(1, NZ):
        deep[d - 1].wait_recv()
        final = final + got_z[d - 1]

    half_out = big_out.at[core]
    mine = part((a * NY + b) * NZ + z, ROWS_Z)
    half_out[mine, :] = final
    deep = [send(half_out.at[mine, :], half_out.at[mine, :], peer) for peer in along_z]
    for copy in littles:
        copy.wait_recv()
    small_out[core] = s_sum[...]
    little = send(small_out.at[core], small_out.at[core], partner)
    for copy in deep:
        copy.wait_recv()

    def spread(rows, targets):
        return [send(half_out.at[rows, :], half_out.at[rows, :], peer) for peer in targets]

    def top_of(aa, bb):
        return part(((aa % NX) * NY + bb % NY) * 2, ROWS_B // 2)

    def bottom_of(aa, bb):
        return part(((aa % NX) * NY + bb % NY) * 2 + 1, ROWS_B // 2)

    near_a, near_b = [along_a[0], along_a[2]], [along_b[0], along_b[2]]
    across = spread(rows_of(a, b), near_b)
    steps = [spread(rows_of(a, b), near_a)]
    pairs = spread(rows_of(a, b), [partner])
    relays_b, relays_a = [], {}

    def pass_on(e, bb):
        steps[e][0].wait_recv()
        first = spread(top_of(a + 3, bb), near_a[:1])
        pairs.extend(spread(rows_of(a + 3, bb), [partner]))
        steps[e][1].wait_recv()
        second = spread(bottom_of(a + 1, bb), near_a[1:])
        pairs.extend(spread(rows_of(a + 1, bb), [partner]))
        relays_a[e] = first + second

    across[0].wait_recv()
    relays_b += spread(top_of(a, b + 3), near_b[:1])
    steps.append(spread(rows_of(a, b + 3), near_a))
    across[1].wait_recv()
    relays_b += spread(bottom_of(a, b + 1), near_b[1:])
    steps.append(spread(rows_of(a, b + 1), near_a))
    pairs += spread(rows_of(a, b + 3), [partner]) + spread(rows_of(a, b + 1), [partner])
    pass_on(0, b)
    for copy in relays_b:
        copy.wait_recv()
    steps.append(spread(rows_of(a, b + 2), near_a))
    pairs += spread(rows_of(a, b + 2), [partner])
    pass_on(1, b + 3)
    pass_on(2, b + 1)
    pass_on(3, b + 2)
    for e, bb in enumerate((b, b + 3, b + 1, b + 2)):
        for copy in relays_a[e]:
            copy.wait_recv()
        pairs += spread(rows_of(a + 2, bb), [partner])
    little.wait_recv()
    for copy in pairs:
        copy.wait_recv()
    for copy in started:
        copy.wait_send()


def train(params, increments, w_in, b_in, w_mid, b_mid, w_out, b_out):
    f32, bf16 = jnp.float32, jnp.bfloat16
    vmem = pl.BlockSpec(memory_space=pltpu.VMEM)
    smem = pl.BlockSpec(memory_space=pltpu.SMEM)
    hbm = pl.BlockSpec(memory_space=pltpu.HBM)
    loads = [
        params.T,
        jnp.asarray(lag_tables()),
        increments,
        w_mid,
        jnp.asarray(pair_table()),
        w_in,
        b_in.reshape(1, WIDE),
        b_mid.reshape(1, WIDE),
        w_out,
    ]
    return pl.pallas_call(
        step_kernel,
        in_specs=[hbm] * 9 + [smem],
        out_specs=[vmem, vmem, vmem],
        out_shape=[
            jax.ShapeDtypeStruct((OWN, PAIRS), f32),
            jax.ShapeDtypeStruct((NC, WIDE, HALF), f32),
            jax.ShapeDtypeStruct((NC, SMALL, HALF), f32),
        ],
        scratch_shapes=[
            pltpu.VMEM((4, SETS), f32),
            pltpu.VMEM((8, 128), f32),
            pltpu.VMEM((2, STEPS, 128), bf16),
            pltpu.VMEM((WIDE, WIDE), bf16),
            pltpu.VMEM((PAIRS, 128), f32),
            pltpu.VMEM((6, WIDE), bf16),
            pltpu.VMEM((1, WIDE), f32),
            pltpu.VMEM((1, WIDE), f32),
            pltpu.VMEM((WIDE,), bf16),
            pltpu.SemaphoreType.DMA((9,)),
            pltpu.VMEM((NX, NY * NZ, NC, OWN, 128), f32),
            pltpu.VMEM((BLOCK, 256), bf16),
            pltpu.VMEM((BLOCK, 128), f32),
            pltpu.VMEM((BLOCK, 128), f32),
            pltpu.VMEM((2, STEPS, 128), f32),
            pltpu.VMEM((STEPS // 2, 256, 256), bf16),
            pltpu.VMEM((BLOCK, 128), f32),
            pltpu.VMEM((128, BLOCK), f32),
            pltpu.VMEM((BLOCKS, BLOCK, 128), f32),
            pltpu.VMEM((BLOCKS - 1, BLOCK, 128), f32),
            pltpu.VMEM((NY, NZ * OWN, 128), f32),
            pltpu.VMEM((NZ, OWN, 128), f32),
            pltpu.SemaphoreType.DMA((BLOCKS,)),
            pltpu.SemaphoreType.DMA((BLOCKS,)),
            pltpu.SemaphoreType.DMA((NY,)),
            pltpu.SemaphoreType.DMA((NY,)),
            pltpu.SemaphoreType.DMA((NZ,)),
            pltpu.SemaphoreType.DMA((NZ,)),
            pltpu.VMEM((SMALL, WIDE), f32),
            pltpu.VMEM((ROWS, 128), bf16),
            pltpu.VMEM((DEPTH, WIDE), bf16),
            pltpu.VMEM((ROWS, WIDE), f32),
            pltpu.VMEM((ROWS, WIDE), bf16),
            pltpu.VMEM((ROWS, WIDE), f32),
            pltpu.VMEM((ROWS, 1), f32),
            pltpu.VMEM((DEPTH, WIDE), bf16),
            pltpu.VMEM((ROWS, WIDE), bf16),
            pltpu.VMEM((WIDE, DEPTH), bf16),
            pltpu.VMEM((NY, NX, ROWS_B, HALF), f32),
            pltpu.VMEM((NY, NX, ROWS_B, HALF), f32),
            pltpu.VMEM((NY, NX, ROWS_B, HALF), f32),
            pltpu.VMEM((NY, 2, ROWS_B, HALF), f32),
            pltpu.VMEM((NY, 2, ROWS_B // 2, HALF), f32),
            pltpu.VMEM((2, ROWS_B // 2, HALF), f32),
            pltpu.VMEM((NY, ROWS_B, HALF), f32),
            pltpu.VMEM((2, ROWS_B, HALF), f32),
            pltpu.VMEM((ROWS_B, HALF), f32),
            pltpu.VMEM((NZ - 1, ROWS_Z, HALF), f32),
            pltpu.VMEM((SMALL, HALF), f32),
            pltpu.VMEM((NX - 1, SMALL, SLICE), f32),
            pltpu.VMEM((NY, SMALL, SLICE), f32),
            pltpu.VMEM((NZ, SMALL, SLICE), f32),
            pltpu.VMEM((SMALL, HALF), f32),
            pltpu.SemaphoreType.DMA((SENDS,)),
            pltpu.SemaphoreType.DMA((SENDS,)),
        ],
        compiler_params=pltpu.CompilerParams(
            collective_id=0, has_side_effects=True, vmem_limit_bytes=46 * 1024 * 1024
        ),
        name="step",
    )(
        *[pltpu.with_memory_space_constraint(value, pltpu.HBM) for value in loads],
        b_out.reshape(1, 1),
    )


def finish_kernel(
    prices_ref,
    big_ref,
    small_ref,
    prices_out,
    w_in_out,
    b_in_out,
    w_mid_out,
    b_mid_out,
    w_out_out,
    b_out_out,
):
    prices_out[...] = prices_ref[...]

    def factor(total, entries):
        return lax.rsqrt(total * (1.0 / entries) + EPSILON)

    def sumsq(value):
        return jnp.sum(jnp.sum(value * value, axis=1, keepdims=True), axis=0, keepdims=True)

    small = jnp.concatenate([small_ref[0], small_ref[1]], axis=1)
    g_bout = small[9:10, 0:1]
    s_mid = sumsq(small[7:8])
    for k in range(8):
        for c in range(NC):
            s_mid = s_mid + sumsq(big_ref[c, pl.ds(k * 128, 128), :])
    f_in = factor(sumsq(small[0:7]), 7 * WIDE)
    f_mid = factor(s_mid, (WIDE + 1) * WIDE)
    f_out = factor(sumsq(small[8:9]) + g_bout * g_bout, WIDE + 1)
    w_in_out[...] = small[0:6] * f_in
    b_in_out[...] = small[6:7] * f_in
    b_mid_out[...] = small[7:8] * f_mid
    w_out_out[...] = small[8:9] * f_out
    b_out_out[...] = g_bout * f_out
    for c in range(NC):
        w_mid_out[:, pl.ds(c * HALF, HALF)] = big_ref[c] * f_mid


def finish(prices, big, small):
    f32 = jnp.float32
    vmem = pl.BlockSpec(memory_space=pltpu.VMEM)
    shapes = [(OWN, PAIRS), (6, WIDE), (1, WIDE), (WIDE, WIDE), (1, WIDE), (1, WIDE), (1, 1)]
    prices, w_in, b_in, w_mid, b_mid, w_out, b_out = pl.pallas_call(
        finish_kernel,
        in_specs=[vmem] * 3,
        out_specs=[vmem] * 7,
        out_shape=[jax.ShapeDtypeStruct(shape, f32) for shape in shapes],
        compiler_params=pltpu.CompilerParams(vmem_limit_bytes=16 * 1024 * 1024), name="finish",
    )(prices, big, small)
    b_in, b_mid, w_out = b_in.reshape(WIDE), b_mid.reshape(WIDE), w_out.reshape(WIDE)
    return prices, w_in, b_in, w_mid, b_mid, w_out, b_out.reshape(1)


def on_device(params, increments, w_in, b_in, w_mid, b_mid, w_out, b_out):
    prices, big, small = train(params, increments, w_in, b_in, w_mid, b_mid, w_out, b_out)
    return finish(prices, big, small)


def solution(mesh):
    in_specs = (P(), P(None, None, "paths"), P(), P(), P(), P(), P(), P())
    out_specs = (P("paths", None), P(), P(), P(), P(), P(), P())
    return jax.shard_map(
        on_device, mesh=mesh, in_specs=in_specs, out_specs=out_specs, check_vma=False
    )
```
